32 devices in a mesh: ctx: 8 (over z, x), wsh: 4 (over y, core).
Axes of the slice: x: 2, y: 2, z: 4, core: 2. Of those that a mesh axis runs over, the one named last changes fastest.
Arguments:
- tokens: bfloat16 [4096, 768], P(('ctx', 'wsh')), may hold values from -6 to 6
- block_order: int32 [32], replicated, may hold values from 0 to 31, each once
- seq_lengths: int32 [4], replicated, may hold values from 1 to 2048, 4096 in all
- cotangent: bfloat16 [4096, 768], P(('ctx', 'wsh')), may hold values from -6 to 6
- query_matrix: float32 [768, 768], P('wsh'), may hold values from -0.4375 to 0.4375
- key_matrix: float32 [768, 768], P('wsh'), may hold values from -0.21875 to 0.21875
- value_matrix: float32 [768, 768], P('wsh'), may hold values from -0.21875 to 0.21875
- output_matrix: float32 [768, 768], P('wsh'), may hold values from -1.25 to 1.25
- expand_matrix: float32 [768, 3072], P('wsh'), may hold values from -0.21875 to 0.21875
- reduce_matrix: float32 [3072, 768], P('wsh'), may hold values from -0.109375 to 0.109375
- query_bias: float32 [768], P('wsh'), may hold values from -3 to 3
- value_bias: float32 [768], P('wsh'), may hold values from -3 to 3
- output_bias: float32 [768], P('wsh'), may hold values from -3 to 3
- expand_bias: float32 [3072], P('wsh'), may hold values from -3 to 3
- reduce_bias: float32 [768], P('wsh'), may hold values from -3 to 3
- first_gain: float32 [768], P('wsh'), may hold values from 0.5 to 1.5
- first_shift: float32 [768], P('wsh'), may hold values from -3 to 3
- second_gain: float32 [768], P('wsh'), may hold values from 0.5 to 1.5
- second_shift: float32 [768], P('wsh'), may hold values from -3 to 3
Outputs:
- layer_out: bfloat16 [4096, 768], P(('ctx', 'wsh'))
- tokens_grad: bfloat16 [4096, 768], P(('ctx', 'wsh'))
- query_matrix_grad: float32 [768, 768], P('wsh')
- key_matrix_grad: float32 [768, 768], P('wsh')
- value_matrix_grad: float32 [768, 768], P('wsh')
- output_matrix_grad: float32 [768, 768], P('wsh')
- expand_matrix_grad: float32 [768, 3072], P('wsh')
- reduce_matrix_grad: float32 [3072, 768], P('wsh')
- query_bias_grad: float32 [768], P('wsh')
- value_bias_grad: float32 [768], P('wsh')
- output_bias_grad: float32 [768], P('wsh')
- expand_bias_grad: float32 [3072], P('wsh')
- reduce_bias_grad: float32 [768], P('wsh')
- first_gain_grad: float32 [768], P('wsh')
- first_shift_grad: float32 [768], P('wsh')
- second_gain_grad: float32 [768], P('wsh')
- second_shift_grad: float32 [768], P('wsh')
The draws below stay inside these ranges and needn't reach their ends.
Inputs may be any that keep to these rules, and one draw needn't show every extreme that they name: `block_order`: each of the 32 block numbers appears once. `seq_lengths`: the 4 lengths add up to 4096; the longest is 2048.
All inputs are finite; a program needn't handle non-finite values.
Results may differ from the reference program's by a relative error of at most 0.025.
The reference program's roundings to bfloat16 on the way count: a program that leaves them out, or rounds other values in their place, can miss the bound.
Values may be sent and summed in bfloat16 or wider, within the bound.
No kernel may reach another device: no remote copies, remote signals or barrier semaphores. Data moves between devices by JAX's collectives and lax.ppermute only.
A program may use at most 256 MiB of HBM per device.

```python
import math
import jax
import jax.numpy as jnp
import numpy as np
from jax import lax

D = 768
HEADS = 12
HDIM = 64
FF = 3072
BLOCK = 128
TOKENS = 4096
NBLK = 32
NSEQ = 4
MOST = 2048


def shard_levels(key, dims, cuts, least, top_value):
    loudness, own = 1.0, jax.random.fold_in(key, 6)
    for dim, blocks in cuts:
        draws = jnp.exp(jax.random.uniform(jax.random.fold_in(own, dim), (blocks,), jnp.float32, least / len(cuts), top_value / len(cuts)))
        loudness = loudness * jnp.repeat(draws, dims[dim] // blocks).reshape([-1 if axis == dim else 1 for axis in range(len(dims))])
    return loudness


def length_profile(amount, total, most, lean):
    weights = [(1 << 20) // math.isqrt(grade ** lean) + 1 for grade in range(2, amount + 1)]
    rest, holding = total - most - (amount - 1), [1] * (amount - 1)
    while rest > 0:
        free = [i for i in range(amount - 1) if holding[i] < most]
        mass, budget = sum([weights[i] for i in free]), rest
        for i in free:
            extra = min(most - holding[i], max(1, budget * weights[i] // mass), rest)
            holding[i] = holding[i] + extra
            rest = rest - extra
    return np.array([most] + holding)


def uneven_parts(key, amount, total, reach, lean):
    if amount == 2:
        one = jax.random.randint(key, (), max(1, total - reach), min(reach, total - 1) + 1)
        return jnp.stack([one, total - one])
    sizes = jnp.asarray(length_profile(amount, total, reach, lean), jnp.int32)
    pairs = (amount - 1) // 2
    source_of, sink = sizes[1:1 + 2 * pairs:2], sizes[2:2 + 2 * pairs:2]
    room = jnp.minimum(source_of - 1, reach - sink)
    moved = jax.random.randint(jax.random.fold_in(key, 1), (pairs,), 0, 1 << 20) % (room + 1)
    sizes = sizes.at[1:1 + 2 * pairs:2].set(source_of - moved).at[2:2 + 2 * pairs:2].set(sink + moved)
    return sizes[jax.random.permutation(jax.random.fold_in(key, 2), amount)]


def scatter_about(key, shape, deviation, limit, pieces=(), kind=jnp.bfloat16):
    drawn = jax.random.normal(key, shape, jnp.float32) * deviation
    if len(pieces) > 0:
        drawn = shard_levels(key, shape, pieces, -0.22, 0.18) * drawn
    return jnp.clip(drawn, min=-limit, max=limit).astype(kind)


def setup_inputs(seed: int = 0) -> dict:
    splits = jax.random.split(jax.random.key(seed), 20)
    return {
        "tokens": scatter_about(splits[0], (TOKENS, D), 1.0, 6.0, ((0, 32),)),
        "block_order": jax.random.permutation(splits[1], NBLK).astype(jnp.int32),
        "seq_lengths": uneven_parts(splits[2], NSEQ, TOKENS, MOST, 2).astype(jnp.int32),
        "cotangent": scatter_about(splits[3], (TOKENS, D), 1.0, 6.0, ((0, 32),)),
        "query_matrix": scatter_about(splits[4], (D, D), (D // 4) ** -0.5, 0.4375, ((0, 4),), jnp.float32),
        "key_matrix": scatter_about(splits[5], (D, D), D ** -0.5, 0.21875, ((0, 4),), jnp.float32),
        "value_matrix": scatter_about(splits[6], (D, D), D ** -0.5, 0.21875, ((0, 4),), jnp.float32),
        "output_matrix": scatter_about(splits[7], (D, D), (D // 32) ** -0.5, 1.25, ((0, 4),), jnp.float32),
        "expand_matrix": scatter_about(splits[8], (D, FF), D ** -0.5, 0.21875, ((0, 4),), jnp.float32),
        "reduce_matrix": scatter_about(splits[9], (FF, D), FF ** -0.5, 0.109375, ((0, 4),), jnp.float32),
        "query_bias": scatter_about(splits[10], (D,), 0.5, 3.0, ((0, 4),), jnp.float32),
        "value_bias": scatter_about(splits[11], (D,), 0.5, 3.0, ((0, 4),), jnp.float32),
        "output_bias": scatter_about(splits[12], (D,), 0.5, 3.0, ((0, 4),), jnp.float32),
        "expand_bias": scatter_about(splits[13], (FF,), 0.5, 3.0, ((0, 4),), jnp.float32),
        "reduce_bias": scatter_about(splits[14], (D,), 0.5, 3.0, ((0, 4),), jnp.float32),
        "first_gain": jnp.clip(1.0 + 0.1 * jax.random.normal(splits[15], (D,), jnp.float32), 0.5, 1.5),
        "first_shift": scatter_about(splits[16], (D,), 0.5, 3.0, ((0, 4),), jnp.float32),
        "second_gain": jnp.clip(1.0 + 0.1 * jax.random.normal(splits[17], (D,), jnp.float32), 0.5, 1.5),
        "second_shift": scatter_about(splits[18], (D,), 0.5, 3.0, ((0, 4),), jnp.float32),
    }


EPSILON = 1e-12
NEGATIVE = -1e+30

@jax.custom_vjp
def low(v):
    return lax.optimization_barrier(v.astype(jnp.bfloat16)).astype(jnp.float32)

@jax.custom_vjp
def low_back(v):
    return v

def low_keep(v):
    return (low(v), None)

def low_pass(kept, grad):
    return (grad,)

def back_keep(v):
    return (v, None)

def back_low(kept, grad):
    return (low(grad),)
low.defvjp(low_keep, low_pass)
low_back.defvjp(back_keep, back_low)

def both_ways(value):
    return low_back(low(value))

def layer_norm(values, gain, shift):
    centred = values - lax.optimization_barrier(jnp.mean(values, axis=-1, keepdims=True))
    spread = lax.optimization_barrier(jnp.mean(centred * centred, axis=-1, keepdims=True))
    return centred * lax.rsqrt(spread + EPSILON) * gain + shift

def exact_gelu(values):
    return jax.nn.gelu(values, approximate=False)

def reference(tokens, block_order, seq_lengths, cotangent, query_matrix, key_matrix, value_matrix, output_matrix, expand_matrix, reduce_matrix, query_bias, value_bias, output_bias, expand_bias, reduce_bias, first_gain, first_shift, second_gain, second_shift):
    all_rows = jnp.arange(TOKENS, dtype=jnp.int32)
    places = block_order[all_rows // BLOCK] * BLOCK + all_rows % BLOCK
    seq_ends = jnp.cumsum(seq_lengths).astype(jnp.int32)
    seq_ids = lax.optimization_barrier(jnp.sum((places[:, None] >= seq_ends[None, :]).astype(jnp.int32), axis=1))
    query_rows = math.gcd(TOKENS, 256)
    highest = lax.Precision.HIGHEST

    def matmul(left, right):
        return jnp.dot(left, right, precision=highest)

    def forward(inputs, params):
        rounded = [low(param) for param in params]
        query_w, key_w, value_w, output_w, expand_w, reduce_w, query_b, value_b, output_b, expand_b, reduce_b, first_g, first_s, second_g, second_s = rounded
        queries = both_ways(matmul(inputs, query_w) + query_b)
        keys = both_ways(matmul(inputs, key_w))
        values = both_ways(matmul(inputs, value_w) + value_b)
        key_heads = keys.reshape(TOKENS, HEADS, HDIM)
        value_heads = values.reshape(TOKENS, HEADS, HDIM)

        def attend_block(pair):
            query_block, id_block = pair
            scores = jnp.einsum('qhd,khd->hqk', query_block, key_heads, precision=highest) * HDIM ** (-0.5)
            scores = low_back(scores)
            allowed = (id_block[:, None] == seq_ids[None, :])[None]
            masked = jnp.where(allowed, scores, NEGATIVE)
            highest_score = lax.optimization_barrier(jnp.max(masked, axis=-1, keepdims=True))
            weights = jnp.where(allowed, jnp.exp(masked - highest_score), 0.0)
            probs = low(weights / lax.optimization_barrier(jnp.sum(weights, axis=-1, keepdims=True)))
            return jnp.einsum('hqk,khd->qhd', probs, value_heads, precision=highest)
        attended = lax.map(jax.checkpoint(attend_block), (queries.reshape(TOKENS // query_rows, query_rows, HEADS, HDIM), seq_ids.reshape(TOKENS // query_rows, query_rows)))
        attended = both_ways(attended.reshape(TOKENS, D))
        branch = low_back(matmul(attended, output_w) + output_b)
        normed = layer_norm(inputs + branch, first_g, first_s)
        expanded = low_back(matmul(low(normed), expand_w) + expand_b)
        activated = low(exact_gelu(expanded))
        reduced = low_back(matmul(activated, reduce_w) + reduce_b)
        return layer_norm(normed + reduced, second_g, second_s)
    params = (query_matrix, key_matrix, value_matrix, output_matrix, expand_matrix, reduce_matrix, query_bias, value_bias, output_bias, expand_bias, reduce_bias, first_gain, first_shift, second_gain, second_shift)
    params = tuple((param.astype(jnp.float32) for param in params))
    outcome, pullback = jax.vjp(forward, tokens.astype(jnp.float32), params)
    grad_inputs, grad_params = pullback(cotangent.astype(jnp.float32))
    return (outcome.astype(jnp.bfloat16), grad_inputs.astype(jnp.bfloat16), grad_params[0], grad_params[1], grad_params[2], grad_params[3], grad_params[4], grad_params[5], grad_params[6], grad_params[7], grad_params[8], grad_params[9], grad_params[10], grad_params[11], grad_params[12], grad_params[13], grad_params[14])
```

```python
import math

import jax
import jax.numpy as jnp
from jax import lax
from jax.experimental import pallas as pl
from jax.experimental.pallas import tpu as pltpu
from jax.sharding import PartitionSpec as P

HDIM = 64
BLOCK = 128
EPSILON = 1e-12
LOW = jnp.bfloat16
WIDE = jnp.float32

ORDER = (0, 2, 1, 3)

PAD = 256
DELTA_LANE = 192
LSE_LANE = 201
SEQ_LANE = 216
BIG = 1e30
CHUNK = 512


def ring_of(n):
    return list(range(0, n, 2)) + list(range(n - 1, 0, -2))


def exchange(value, axis, size, flip):
    return lax.ppermute(value, axis, [(i, i ^ flip) for i in range(size)])


def wsh_swap(value, flip):
    return exchange(value, "wsh", 4, flip)


def to_absolute(pieces, w):
    one = (w & 1) == 1
    two = (w & 2) == 2
    a = [jnp.where(one, pieces[j ^ 1], pieces[j]) for j in range(4)]
    return [jnp.where(two, a[j ^ 2], a[j]) for j in range(4)]


def gather_group(value):
    other = wsh_swap(value, 2)
    mate = wsh_swap(value, 1)
    last = wsh_swap(other, 1)
    return jnp.concatenate([value, other, mate, last], axis=0)


def scatter_group(parts):
    rows = parts.shape[0] // 4
    mine, other, mate, last = [parts[i * rows : (i + 1) * rows] for i in range(4)]
    got = wsh_swap(jnp.concatenate([mate, last], axis=0).astype(LOW), 1).astype(WIDE)
    mine = mine + got[:rows]
    other = other + got[rows:]
    return mine + wsh_swap(other.astype(LOW), 2).astype(WIDE)


def ring_shift(value, n, step):
    ring = ring_of(n)
    return lax.ppermute(value, "ctx", [(ring[i], ring[(i + step) % n]) for i in range(n)])


def ring_gather(value, n):
    half = n // 2
    rows = value.shape[0]
    ahead, back = [], []
    f = b = value
    for step in range(1, half + 1):
        if step < half:
            f = ring_shift(f, n, 1)
            b = ring_shift(b, n, -1)
            ahead.append(f)
            back.append(b)
        else:
            first = ring_shift(f[: rows // 2], n, 1)
            second = ring_shift(b[rows // 2 :], n, -1)
            ahead.append(jnp.concatenate([first, second], axis=0))
    return [value] + ahead + back


def slot_steps(n):
    half = n // 2
    return [0] + [-s for s in range(1, half + 1)] + list(range(1, half))


def layer_norm_parts(values):
    centred = values - jnp.mean(values, axis=-1, keepdims=True)
    spread = jnp.mean(centred * centred, axis=-1, keepdims=True)
    scale = lax.rsqrt(spread + EPSILON)
    return centred * scale, scale


def layer_norm_back(upstream, normal, scale):
    return scale * (
        upstream
        - jnp.mean(upstream, axis=-1, keepdims=True)
        - normal * jnp.mean(upstream * normal, axis=-1, keepdims=True)
    )


def lanes_of(head, lane):
    keep = (lane >= head * HDIM) & (lane < (head + 1) * HDIM)
    return keep


def stack_heads(value):
    lane = lax.broadcasted_iota(jnp.int32, value.shape, 1)
    out = []
    for head in range(3):
        keep = (
            lanes_of(head, lane)
            | ((lane >= DELTA_LANE + 3 * head) & (lane < DELTA_LANE + 3 * head + 3))
            | ((lane >= LSE_LANE + 3 * head) & (lane < LSE_LANE + 3 * head + 3))
            | (lane >= SEQ_LANE)
        )
        out.append(jnp.where(keep, value, jnp.zeros_like(value)))
    return jnp.concatenate(out, axis=0)


def pick_heads(value):
    lane = lax.broadcasted_iota(jnp.int32, (BLOCK, PAD), 1)
    total = jnp.zeros((BLOCK, PAD), WIDE)
    for head in range(3):
        total = jnp.where(lanes_of(head, lane), value[head * BLOCK : (head + 1) * BLOCK], total)
    return total


def dot_nt(a, b):
    return lax.dot_general(a, b, (((1,), (1,)), ((), ())), preferred_element_type=WIDE)


def dot_nn(a, b):
    return jnp.dot(a, b, preferred_element_type=WIDE)


def seq_marks(seq_ref, place):
    spot = place * BLOCK + lax.broadcasted_iota(jnp.int32, (BLOCK, PAD), 0)
    return (spot >= seq_ref[0:1, :]) & (spot < seq_ref[1:2, :])


def key_lanes(seq_ref, place, value):
    lane = lax.broadcasted_iota(jnp.int32, (BLOCK, PAD), 1)
    marks = seq_marks(seq_ref, place)
    minus = (lane >= LSE_LANE) & (lane < LSE_LANE + 9)
    out = jnp.where(minus, -1.0, value.astype(WIDE))
    return jnp.where((lane >= SEQ_LANE) & ~marks, -BIG, out).astype(LOW)


def query_lanes(seq_ref, place, value):
    return jnp.where(seq_marks(seq_ref, place), 1.0, value.astype(WIDE)).astype(LOW)


def value_lanes(value):
    lane = lax.broadcasted_iota(jnp.int32, (BLOCK, PAD), 1)
    minus = (lane >= DELTA_LANE) & (lane < DELTA_LANE + 9)
    return jnp.where(minus, -1.0, value.astype(WIDE)).astype(LOW)


def parts_of(column):
    high = column.astype(LOW).astype(WIDE)
    rest = column - high
    mid = rest.astype(LOW).astype(WIDE)
    return high, mid, (rest - mid).astype(LOW).astype(WIDE)


def fill_packed(arrays, column, target, sem, tab_ref):
    per = arrays[0].shape[0] // BLOCK
    for i, array in enumerate(arrays):
        for j in range(per):
            place = pl.multiple_of(tab_ref[i * per + j] * BLOCK, BLOCK)
            pltpu.make_async_copy(
                array.at[pl.ds(j * BLOCK, BLOCK), pl.ds(column * PAD, PAD)],
                target.at[pl.ds(place, BLOCK)],
                sem,
            ).start()


def wait_packed(target, sem, tokens_all):
    whole = target.at[pl.ds(0, tokens_all)]
    pltpu.make_async_copy(whole, whole, sem).wait()


def end_rows(seq_value):
    lane = lax.broadcasted_iota(jnp.int32, (CHUNK, PAD), 1)
    return jnp.where(lane >= SEQ_LANE, seq_value, 0.0).astype(LOW)


def attend_kernel(pieces, tokens_all, tab_ref, seq_ref, query_ref, *refs):
    qkv = refs[:pieces]
    out_ref, key_ref, value_ref, sems = refs[pieces:]
    fill_packed(qkv, 1, key_ref, sems.at[0], tab_ref)
    fill_packed(qkv, 2, value_ref, sems.at[1], tab_ref)
    rest = pl.ds(tokens_all, CHUNK)
    key_ref[rest, :] = end_rows(-BIG)
    value_ref[rest, :] = jnp.zeros((CHUNK, PAD), LOW)
    wait_packed(key_ref, sems.at[0], tokens_all)
    wait_packed(value_ref, sems.at[1], tokens_all)
    base = tokens_all // BLOCK

    def fix(place, unused):
        rows = pl.ds(pl.multiple_of(place * BLOCK, BLOCK), BLOCK)
        key_ref[rows, :] = key_lanes(seq_ref, place, key_ref[rows, :])
        return unused

    lax.fori_loop(0, base, fix, 0)
    lane = lax.broadcasted_iota(jnp.int32, (BLOCK, PAD), 1)

    def block(i, unused):
        rows = pl.ds(pl.multiple_of(i * BLOCK, BLOCK), BLOCK)
        low = tab_ref[base + i]
        count = tab_ref[base + 4 + i]
        queries = stack_heads(query_lanes(seq_ref, tab_ref[i], query_ref[rows, :]))

        def visit(c, state):
            top, total, accum = state
            spot = pl.ds(pl.multiple_of(low * BLOCK + c * CHUNK, BLOCK), CHUNK)
            scores = dot_nt(queries, key_ref[spot, :])
            top_new = jnp.maximum(top, jnp.max(scores, axis=1, keepdims=True))
            weights = jnp.exp(scores - top_new)
            factor = jnp.exp(top - top_new)
            total = total * factor + jnp.sum(weights, axis=1, keepdims=True)
            accum = accum * factor + dot_nn(weights.astype(LOW), value_ref[spot, :])
            return top_new, total, accum

        top, total, accum = lax.fori_loop(
            0,
            count,
            visit,
            (
                jnp.full((3 * BLOCK, 1), -2 * BIG, WIDE),
                jnp.zeros((3 * BLOCK, 1), WIDE),
                jnp.zeros((3 * BLOCK, PAD), WIDE),
            ),
        )
        result = pick_heads(accum / total)
        logsum = top + jnp.log(total)
        for head in range(3):
            result = jnp.where(
                lane == DELTA_LANE + head, logsum[head * BLOCK : (head + 1) * BLOCK], result
            )
        out_ref[rows, :] = result
        return unused

    lax.fori_loop(0, 4, block, 0)


def outgrad_kernel(branch_ref, matrix_ref, attn_ref, out_ref):
    grad = dot_nt(branch_ref[...], matrix_ref[...]).astype(LOW).astype(WIDE)
    attn = attn_ref[...]
    lane = lax.broadcasted_iota(jnp.int32, grad.shape, 1)
    product = grad * attn
    out = jnp.where(lane < DELTA_LANE, grad, 0.0)
    for head in range(3):
        delta = jnp.sum(jnp.where(lanes_of(head, lane), product, 0.0), axis=1, keepdims=True)
        logsum = jnp.sum(jnp.where(lane == DELTA_LANE + head, attn, 0.0), axis=1, keepdims=True)
        for first, column in ((DELTA_LANE, delta), (LSE_LANE, logsum)):
            for i, part in enumerate(parts_of(column)):
                out = jnp.where(lane == first + 3 * head + i, part, out)
    out_ref[...] = out.astype(LOW)


def backward_kernel(pieces, outs, tokens_all, tab_ref, seq_ref, *refs):
    qkv = refs[:pieces]
    grads = refs[pieces : pieces + outs]
    out_ref, query_ref, key_ref, value_ref, grad_ref, sems = refs[pieces + outs :]
    fill_packed(qkv, 0, query_ref, sems.at[0], tab_ref)
    fill_packed(qkv, 1, key_ref, sems.at[1], tab_ref)
    fill_packed(qkv, 2, value_ref, sems.at[2], tab_ref)
    fill_packed(grads, 0, grad_ref, sems.at[3], tab_ref)
    base = tokens_all // BLOCK
    rest = pl.ds(tokens_all, CHUNK)
    key_ref[rest, :] = end_rows(-BIG)
    query_ref[rest, :] = end_rows(1.0)
    value_ref[rest, :] = jnp.zeros((CHUNK, PAD), LOW)
    grad_ref[rest, :] = jnp.zeros((CHUNK, PAD), LOW)
    for i, target in enumerate((query_ref, key_ref, value_ref, grad_ref)):
        wait_packed(target, sems.at[i], tokens_all)

    def fix(place, unused):
        rows = pl.ds(pl.multiple_of(place * BLOCK, BLOCK), BLOCK)
        small = lax.broadcasted_iota(jnp.int32, (BLOCK, PAD), 1)
        key_ref[rows, :] = key_lanes(seq_ref, place, key_ref[rows, :])
        value_ref[rows, :] = value_lanes(value_ref[rows, :])
        query = query_lanes(seq_ref, place, query_ref[rows, :])
        is_lse = (small >= LSE_LANE) & (small < LSE_LANE + 9)
        query_ref[rows, :] = jnp.where(is_lse, grad_ref[rows, :], query)
        return unused

    lax.fori_loop(0, base, fix, 0)

    def block(i, unused):
        rows = pl.ds(pl.multiple_of(i * BLOCK, BLOCK), BLOCK)
        own = pl.ds(pl.multiple_of(tab_ref[i] * BLOCK, BLOCK), BLOCK)
        low = tab_ref[base + i]
        count = tab_ref[base + 4 + i]
        zeros = jnp.zeros((3 * BLOCK, PAD), WIDE)
        left = stack_heads(query_ref[own, :])
        right = stack_heads(grad_ref[own, :])

        def query_visit(c, accum):
            spot = pl.ds(pl.multiple_of(low * BLOCK + c * CHUNK, BLOCK), CHUNK)
            keys = key_ref[spot, :]
            probs = jnp.exp(dot_nt(left, keys))
            slopes = (probs * dot_nt(right, value_ref[spot, :])).astype(LOW)
            return accum + dot_nn(slopes, keys)

        accum = lax.fori_loop(0, count, query_visit, zeros)
        out_ref[rows, pl.ds(0, PAD)] = (pick_heads(accum) * 0.125).astype(LOW)
        key_left = stack_heads(key_ref[own, :])
        value_right = stack_heads(value_ref[own, :])

        def key_visit(c, state):
            key_accum, value_accum = state
            spot = pl.ds(pl.multiple_of(low * BLOCK + c * CHUNK, BLOCK), CHUNK)
            queries = query_ref[spot, :]
            outgrads = grad_ref[spot, :]
            probs = jnp.exp(dot_nt(key_left, queries))
            slopes = (probs * dot_nt(value_right, outgrads)).astype(LOW)
            value_accum = value_accum + dot_nn(probs.astype(LOW), outgrads)
            key_accum = key_accum + dot_nn(slopes, queries)
            return key_accum, value_accum

        key_accum, value_accum = lax.fori_loop(0, count, key_visit, (zeros, zeros))
        out_ref[rows, pl.ds(PAD, PAD)] = pick_heads(key_accum).astype(LOW)
        out_ref[rows, pl.ds(2 * PAD, PAD)] = pick_heads(value_accum).astype(LOW)
        return unused

    lax.fori_loop(0, 4, block, 0)


def whole_spec():
    return pl.BlockSpec(memory_space=pltpu.VMEM)


def any_spec():
    return pl.BlockSpec(memory_space=pl.ANY)


def attend(tab, seq_rows, queries, qkv_pieces, tokens_all):
    pieces = len(qkv_pieces)

    def kernel(*refs):
        attend_kernel(pieces, tokens_all, *refs)

    return pl.pallas_call(
        kernel,
        name="attend",
        out_shape=jax.ShapeDtypeStruct((4 * BLOCK, PAD), WIDE),
        in_specs=[pl.BlockSpec(memory_space=pltpu.SMEM), whole_spec(), whole_spec()]
        + [any_spec()] * pieces,
        out_specs=whole_spec(),
        scratch_shapes=[
            pltpu.VMEM((tokens_all + CHUNK, PAD), LOW),
            pltpu.VMEM((tokens_all + CHUNK, PAD), LOW),
            pltpu.SemaphoreType.DMA((2,)),
        ],
        compiler_params=pltpu.CompilerParams(vmem_limit_bytes=56 << 20),
    )(tab, seq_rows, queries, *qkv_pieces)


def attend_back(tab, seq_rows, qkv_pieces, grad_pieces, tokens_all):
    pieces, outs = len(qkv_pieces), len(grad_pieces)

    def kernel(*refs):
        backward_kernel(pieces, outs, tokens_all, *refs)

    return pl.pallas_call(
        kernel,
        name="attend_back",
        out_shape=jax.ShapeDtypeStruct((4 * BLOCK, 3 * PAD), LOW),
        in_specs=[pl.BlockSpec(memory_space=pltpu.SMEM), whole_spec()]
        + [any_spec()] * (pieces + outs),
        out_specs=whole_spec(),
        scratch_shapes=[pltpu.VMEM((tokens_all + CHUNK, PAD), LOW)] * 4
        + [pltpu.SemaphoreType.DMA((4,))],
        compiler_params=pltpu.CompilerParams(vmem_limit_bytes=56 << 20),
    )(tab, seq_rows, *qkv_pieces, *grad_pieces)


def attend_outgrad(branch, matrix, attn):
    return pl.pallas_call(
        outgrad_kernel,
        name="outgrad",
        out_shape=jax.ShapeDtypeStruct((4 * BLOCK, PAD), LOW),
        in_specs=[whole_spec()] * 3,
        out_specs=whole_spec(),
    )(branch, matrix, attn)


def pad_group(block):
    return jnp.pad(block, ((0, 0), (0, PAD - block.shape[1])))


def on_device(
    n,
    tokens,
    block_order,
    seq_lengths,
    cotangent,
    query_matrix,
    key_matrix,
    value_matrix,
    output_matrix,
    expand_matrix,
    reduce_matrix,
    query_bias,
    value_bias,
    output_bias,
    expand_bias,
    reduce_bias,
    first_gain,
    first_shift,
    second_gain,
    second_shift,
):
    w = lax.axis_index("wsh")
    c = lax.axis_index("ctx")
    ring = ring_of(n)
    rank = jnp.asarray([ring.index(i) for i in range(n)], jnp.int32)[c]
    width = tokens.shape[1]
    share = width // 4
    tokens_all = n * 4 * BLOCK

    pair = jnp.concatenate([tokens, wsh_swap(tokens, 2)], axis=0)
    own_pieces = ring_gather(pair, n)
    token_pieces = []
    for piece in own_pieces:
        token_pieces += [piece, wsh_swap(piece, 1)]

    def columns(matrix, group):
        low = matrix.astype(LOW)
        return [group(low[:, i * share : (i + 1) * share]) for i in range(4)]

    qkv_blocks = jnp.stack(
        [
            jnp.concatenate(parts, axis=1)
            for parts in zip(
                columns(query_matrix, pad_group),
                columns(key_matrix, pad_group),
                columns(value_matrix, pad_group),
            )
        ]
    )
    hidden_share = expand_matrix.shape[1] // 4
    expand_low = expand_matrix.astype(LOW)
    expand_blocks = jnp.stack(
        [expand_low[:, i * hidden_share : (i + 1) * hidden_share] for i in range(4)]
    )

    def deal(blocks):
        got = [lax.dynamic_index_in_dim(blocks, w ^ j, 0, keepdims=False) for j in range(4)]
        got = [got[0]] + [wsh_swap(got[j], j) for j in range(1, 4)]
        return jnp.concatenate(to_absolute(got, w), axis=0)

    qkv_matrix = deal(qkv_blocks)
    expand_full = deal(expand_blocks)
    vectors = jnp.stack(
        [output_bias, reduce_bias, first_gain, first_shift, second_gain, second_shift]
    ).astype(LOW)
    vectors = jnp.concatenate(
        to_absolute([vectors] + [wsh_swap(vectors, j) for j in range(1, 4)], w), axis=1
    ).astype(WIDE)
    output_add, reduce_add, first_scale, first_move, second_scale, second_move = [
        vectors[i : i + 1] for i in range(6)
    ]
    nothing = jnp.zeros((PAD,), LOW)
    fill = jnp.zeros((PAD - share,), LOW)
    qkv_add = jnp.concatenate(
        [query_bias.astype(LOW), fill, nothing, value_bias.astype(LOW), fill]
    ).astype(WIDE)
    qkv_scale = jnp.where(jnp.arange(3 * PAD) < PAD, HDIM ** (-0.5), 1.0).astype(LOW)
    output_low = output_matrix.astype(LOW)
    output_rows = jnp.pad(output_low, ((0, PAD - share), (0, 0)))
    reduce_low = reduce_matrix.astype(LOW)

    ends = jnp.cumsum(seq_lengths)
    steps = jnp.asarray(slot_steps(n), jnp.int32)
    from_ctx = jnp.asarray(ring, jnp.int32)[(rank + steps) % n]
    blocks = (from_ctx[:, None] * 4 + (w ^ jnp.asarray(ORDER, jnp.int32))[None, :]).reshape(-1)
    places = block_order[blocks]
    first = places[:4] * BLOCK
    low = jnp.max(jnp.where(ends[None, :] <= first[:, None], ends[None, :], 0), axis=1)
    last = first + BLOCK - 1
    high = jnp.min(jnp.where(ends[None, :] > last[:, None], ends[None, :], tokens_all), axis=1)
    low_block = low // BLOCK
    count = (high - low_block * BLOCK + CHUNK - 1) // CHUNK
    tab = jnp.concatenate([places, low_block, count]).astype(jnp.int32)
    seqs = seq_lengths.shape[0]
    seq_rows = jnp.pad(
        jnp.stack([ends - seq_lengths, ends]), ((0, 6), (SEQ_LANE, PAD - SEQ_LANE - seqs))
    ).astype(jnp.int32)

    qkv_pieces = [
        (jnp.dot(piece, qkv_matrix, preferred_element_type=WIDE) + qkv_add).astype(LOW) * qkv_scale
        for piece in token_pieces
    ]
    own_queries = jnp.concatenate([qkv_pieces[0][:, :PAD], qkv_pieces[1][:, :PAD]], axis=0)
    attn = attend(tab, seq_rows, own_queries, qkv_pieces, tokens_all)
    attended = attn.astype(LOW)
    branch = scatter_group(jnp.dot(attended, output_rows, preferred_element_type=WIDE))
    hidden = tokens.astype(WIDE) + (branch + output_add)
    first_normal, first_rate = layer_norm_parts(hidden)
    normed = first_normal * first_scale + first_move
    normed_all = gather_group(normed.astype(LOW))
    expanded = jnp.dot(normed_all, expand_full, preferred_element_type=WIDE) + expand_bias.astype(
        LOW
    ).astype(WIDE)
    phi_cdf = 0.5 * (1.0 + lax.erf(expanded * (2.0**-0.5)))
    activated = (expanded * phi_cdf).astype(LOW)
    slope = phi_cdf + expanded * (jnp.exp(-0.5 * expanded * expanded) * (2.0 * math.pi) ** -0.5)
    reduced = scatter_group(jnp.dot(activated, reduce_low, preferred_element_type=WIDE))
    summed = normed + (reduced + reduce_add)
    second_normal, second_rate = layer_norm_parts(summed)
    layer_out = (second_normal * second_scale + second_move).astype(LOW)

    upstream = cotangent.astype(WIDE)
    grad_second_gain = jnp.sum(upstream * second_normal, axis=0)
    grad_second_shift = jnp.sum(upstream, axis=0)
    grad_summed = layer_norm_back(upstream * second_scale, second_normal, second_rate)
    reduce_all = gather_group(grad_summed.astype(LOW))
    grad_reduce = lax.dot_general(
        activated, reduce_all, (((0,), (0,)), ((), ())), preferred_element_type=WIDE
    ).astype(LOW)
    grad_reduce_bias = jnp.sum(reduce_all, axis=0, dtype=WIDE)
    expand_in = (
        lax.dot_general(
            reduce_all, reduce_low, (((1,), (1,)), ((), ())), preferred_element_type=WIDE
        )
        * slope
    ).astype(LOW)
    grad_expand = lax.dot_general(
        normed_all, expand_in, (((0,), (0,)), ((), ())), preferred_element_type=WIDE
    ).astype(LOW)
    grad_expand_bias = jnp.sum(expand_in, axis=0, dtype=WIDE)
    grad_normed = grad_summed + scatter_group(
        lax.dot_general(
            expand_in, expand_full, (((1,), (1,)), ((), ())), preferred_element_type=WIDE
        )
    )
    grad_first_gain = jnp.sum(grad_normed * first_normal, axis=0)
    grad_first_shift = jnp.sum(grad_normed, axis=0)
    grad_hidden = layer_norm_back(grad_normed * first_scale, first_normal, first_rate)
    branch_all = gather_group(grad_hidden.astype(LOW))
    grad_output = lax.dot_general(
        attended[:, :share], branch_all, (((0,), (0,)), ((), ())), preferred_element_type=WIDE
    ).astype(LOW)
    grad_output_bias = jnp.sum(branch_all, axis=0, dtype=WIDE)
    outgrad = attend_outgrad(branch_all, output_rows, attn)
    grad_pieces = ring_gather(outgrad, n)
    grad_qkv = attend_back(tab, seq_rows, qkv_pieces, grad_pieces, tokens_all)
    tokens_grad = (
        scatter_group(
            lax.dot_general(
                grad_qkv, qkv_matrix, (((1,), (1,)), ((), ())), preferred_element_type=WIDE
            )
        )
        + grad_hidden
    ).astype(LOW)
    tokens_group = jnp.concatenate(token_pieces[:2], axis=0)
    grad_qkv_matrix = lax.dot_general(
        tokens_group, grad_qkv, (((0,), (0,)), ((), ())), preferred_element_type=WIDE
    ).astype(LOW)
    grad_qkv_bias = jnp.sum(grad_qkv, axis=0, dtype=WIDE)

    early = lax.psum(jnp.concatenate([grad_reduce, grad_expand, grad_output], axis=0), "ctx")
    late = lax.psum(grad_qkv_matrix, "ctx")
    rows = reduce_low.shape[0]
    out_reduce = early[:rows].astype(WIDE)
    summed_expand = early[rows : rows + width]
    out_output = early[rows + width :].astype(WIDE)

    def undeal(matrix):
        blocks = matrix.reshape(4, share, matrix.shape[1])
        got = [lax.dynamic_index_in_dim(blocks, w ^ j, 0, keepdims=False) for j in range(4)]
        got = [got[0]] + [wsh_swap(got[j], j) for j in range(1, 4)]
        return to_absolute(got, w)

    out_expand = jnp.concatenate(undeal(summed_expand), axis=1).astype(WIDE)
    qkv_blocks = undeal(late)
    out_query, out_key, out_value = [
        jnp.concatenate([b[:, i * PAD : i * PAD + share] for b in qkv_blocks], axis=1).astype(WIDE)
        for i in range(3)
    ]

    def quarter(vector):
        return lax.dynamic_slice_in_dim(vector, w * share, share)

    rows_of = jnp.stack([grad_first_gain, grad_first_shift, grad_second_gain, grad_second_shift])
    split = rows_of.reshape(4, 4, share).transpose(1, 0, 2)
    mine = lax.dynamic_index_in_dim(split, w, 0, keepdims=False)
    for j in range(1, 4):
        mine = mine + wsh_swap(lax.dynamic_index_in_dim(split, w ^ j, 0, keepdims=False), j)
    small = jnp.concatenate(
        [
            mine,
            jnp.stack([quarter(grad_output_bias), quarter(grad_reduce_bias)]),
            grad_expand_bias.reshape(4, share),
            jnp.stack([grad_qkv_bias[:share], grad_qkv_bias[2 * PAD : 2 * PAD + share]]),
        ],
        axis=0,
    )
    flip = 1
    while flip < n:
        small = small + exchange(small, "ctx", n, flip)
        flip *= 2
    out_expand_bias = small[6:10].reshape(-1)
    return (
        layer_out,
        tokens_grad,
        out_query,
        out_key,
        out_value,
        out_output,
        out_expand,
        out_reduce,
        small[10],
        small[11],
        small[4],
        out_expand_bias,
        small[5],
        small[0],
        small[1],
        small[2],
        small[3],
    )


def solution(mesh):
    n = mesh.shape["ctx"]
    rows = P(("ctx", "wsh"), None)
    in_specs = (rows, P(), P(), rows) + (P("wsh", None),) * 6 + (P("wsh"),) * 9
    out_specs = (rows, rows) + (P("wsh", None),) * 6 + (P("wsh"),) * 9

    def run(*args):
        return on_device(n, *args)

    return jax.shard_map(run, mesh=mesh, in_specs=in_specs, out_specs=out_specs, check_vma=False)
```

```python
import math

import jax
import jax.numpy as jnp
from jax import lax
from jax.experimental import pallas as pl
from jax.experimental.pallas import tpu as pltpu
from jax.sharding import PartitionSpec as P

HDIM = 64
BLOCK = 128
EPSILON = 1e-12
LOW = jnp.bfloat16
WIDE = jnp.float32

ORDER = (0, 2, 1, 3)

PAD = 256
DELTA_LANE = 192
LSE_LANE = 201
SEQ_LANE = 216
BIG = 1e30
CHUNK = 1024


def ring_of(n):
    return list(range(0, n, 2)) + list(range(n - 1, 0, -2))


def exchange(value, axis, size, flip):
    return lax.ppermute(value, axis, [(i, i ^ flip) for i in range(size)])


def wsh_swap(value, flip):
    return exchange(value, "wsh", 4, flip)


def to_absolute(pieces, w):
    one = (w & 1) == 1
    two = (w & 2) == 2
    a = [jnp.where(one, pieces[j ^ 1], pieces[j]) for j in range(4)]
    return [jnp.where(two, a[j ^ 2], a[j]) for j in range(4)]


def group_pieces(value):
    other = wsh_swap(value, 2)
    return [value, other, wsh_swap(value, 1), wsh_swap(other, 1)]


def scatter_group(parts):
    rows = parts.shape[0] // 4
    mine, other, mate, last = [parts[i * rows : (i + 1) * rows] for i in range(4)]
    got = wsh_swap(jnp.concatenate([mate, last], axis=0).astype(LOW), 1).astype(WIDE)
    mine = mine + got[:rows]
    other = other + got[rows:]
    return mine + wsh_swap(other.astype(LOW), 2).astype(WIDE)


def ring_shift(value, n, step):
    ring = ring_of(n)
    return lax.ppermute(value, "ctx", [(ring[i], ring[(i + step) % n]) for i in range(n)])


def ring_gather(value, n, split=True, tie=None):
    half = n // 2
    rows = value.shape[0]
    ahead, back = [], []
    f = b = value
    tied = None
    for step in range(1, half + 1):
        if tie is not None and step == tie[0]:
            f, b, tied = lax.optimization_barrier((f, b, tie[1]))
        if step < half:
            f = ring_shift(f, n, 1)
            b = ring_shift(b, n, -1)
            ahead.append(f)
            back.append(b)
        elif not split:
            ahead.append(ring_shift(f, n, 1))
        else:
            first = ring_shift(f[: rows // 2], n, 1)
            second = ring_shift(b[rows // 2 :], n, -1)
            ahead.append(jnp.concatenate([first, second], axis=0))
    pieces = [value] + ahead + back
    return pieces if tie is None else (pieces, tied)


def slot_steps(n):
    half = n // 2
    return [0] + [-s for s in range(1, half + 1)] + list(range(1, half))


def lanes_of(head, lane):
    keep = (lane >= head * HDIM) & (lane < (head + 1) * HDIM)
    return keep


def stack_heads(value):
    lane = lax.broadcasted_iota(jnp.int32, value.shape, 1)
    out = []
    for head in range(3):
        keep = (
            lanes_of(head, lane)
            | ((lane >= DELTA_LANE + 3 * head) & (lane < DELTA_LANE + 3 * head + 3))
            | ((lane >= LSE_LANE + 3 * head) & (lane < LSE_LANE + 3 * head + 3))
            | (lane >= SEQ_LANE)
        )
        out.append(jnp.where(keep, value, jnp.zeros_like(value)))
    return jnp.concatenate(out, axis=0)


def pick_heads(value):
    lane = lax.broadcasted_iota(jnp.int32, (BLOCK, PAD), 1)
    total = jnp.zeros((BLOCK, PAD), WIDE)
    for head in range(3):
        total = jnp.where(lanes_of(head, lane), value[head * BLOCK : (head + 1) * BLOCK], total)
    return total


def dot_nt(a, b):
    return lax.dot_general(a, b, (((1,), (1,)), ((), ())), preferred_element_type=WIDE)


def dot_nn(a, b):
    return jnp.dot(a, b, preferred_element_type=WIDE)


def seq_marks(seq_ref, place):
    spot = place * BLOCK + lax.broadcasted_iota(jnp.int32, (BLOCK, PAD), 0)
    return (spot >= seq_ref[0:1, :]) & (spot < seq_ref[1:2, :])


def key_lanes(seq_ref, place, value):
    lane = lax.broadcasted_iota(jnp.int32, (BLOCK, PAD), 1)
    marks = seq_marks(seq_ref, place)
    minus = (lane >= LSE_LANE) & (lane < LSE_LANE + 9)
    out = jnp.where(minus, -1.0, value.astype(WIDE))
    return jnp.where((lane >= SEQ_LANE) & ~marks, -BIG, out).astype(LOW)


def query_lanes(seq_ref, place, value):
    return jnp.where(seq_marks(seq_ref, place), 1.0, value.astype(WIDE)).astype(LOW)


def value_lanes(value):
    lane = lax.broadcasted_iota(jnp.int32, (BLOCK, PAD), 1)
    minus = (lane >= DELTA_LANE) & (lane < DELTA_LANE + 9)
    return jnp.where(minus, -1.0, value.astype(WIDE)).astype(LOW)


def parts_of(column):
    high = column.astype(LOW).astype(WIDE)
    rest = column - high
    mid = rest.astype(LOW).astype(WIDE)
    return high, mid, (rest - mid).astype(LOW).astype(WIDE)


def end_rows(seq_value):
    lane = lax.broadcasted_iota(jnp.int32, (CHUNK, PAD), 1)
    return jnp.where(lane >= SEQ_LANE, seq_value, 0.0).astype(LOW)


def attend_kernel(pieces, tokens_all, tab_ref, seq_ref, matrix_ref, add_ref, output_ref, *refs):
    tokens = refs[:pieces]
    (
        out_ref,
        low_ref,
        keep_ref,
        send_ref,
        query_out,
        key_out,
        value_out,
        token_ref,
        query_ref,
        key_ref,
        value_ref,
        token_sems,
        sems,
    ) = refs[pieces:]
    per = tokens[0].shape[0] // BLOCK
    many = tokens[0].shape[0]
    copies = [
        pltpu.make_async_copy(tokens[i], token_ref.at[pl.ds(i * many, many)], token_sems.at[i])
        for i in range(pieces)
    ]
    for copy in copies:
        copy.start()
    base = tokens_all // BLOCK
    rest = pl.ds(tokens_all, CHUNK)
    key_ref[rest, :] = end_rows(-BIG)
    query_ref[rest, :] = end_rows(1.0)
    value_ref[rest, :] = jnp.zeros((CHUNK, PAD), LOW)

    def project(i, unused):
        rows = pl.ds(pl.multiple_of(i * 2 * many, BLOCK), 2 * many)
        wide = dot_nn(token_ref[rows, :], matrix_ref[...]) + add_ref[...]
        low = wide.astype(LOW)
        for j in range(2 * per):
            place = tab_ref[i * 2 * per + j]
            spot = pl.ds(pl.multiple_of(place * BLOCK, BLOCK), BLOCK)
            block = low[j * BLOCK : (j + 1) * BLOCK]
            query = block[:, :PAD].astype(WIDE) * HDIM ** (-0.5)
            query_ref[spot, :] = query_lanes(seq_ref, place, query)
            key_ref[spot, :] = key_lanes(seq_ref, place, block[:, PAD : 2 * PAD])
            value_ref[spot, :] = value_lanes(block[:, 2 * PAD :])
        return unused

    for copy in copies:
        copy.wait()
    lax.fori_loop(0, pieces // 2, project, 0)
    stores = [
        pltpu.make_async_copy(source, target, sems.at[i])
        for i, (source, target) in enumerate(
            ((query_ref, query_out), (key_ref, key_out), (value_ref, value_out))
        )
    ]
    for store in stores:
        store.start()
    lane = lax.broadcasted_iota(jnp.int32, (BLOCK, PAD), 1)

    def block(i, unused):
        rows = pl.ds(pl.multiple_of(i * BLOCK, BLOCK), BLOCK)
        own = pl.ds(pl.multiple_of(tab_ref[i] * BLOCK, BLOCK), BLOCK)
        low = tab_ref[base + i]
        count = tab_ref[base + 4 + i]
        queries = stack_heads(query_ref[own, :])

        def visit(c, state):
            top, total, accum = state
            spot = pl.ds(pl.multiple_of(low * BLOCK + c * CHUNK, BLOCK), CHUNK)
            scores = dot_nt(queries, key_ref[spot, :])
            top_new = jnp.maximum(top, jnp.max(scores, axis=1, keepdims=True))
            weights = jnp.exp(scores - top_new)
            factor = jnp.exp(top - top_new)
            total = total * factor + jnp.sum(weights, axis=1, keepdims=True)
            accum = accum * factor + dot_nn(weights.astype(LOW), value_ref[spot, :])
            return top_new, total, accum

        top, total, accum = lax.fori_loop(
            0,
            count,
            visit,
            (
                jnp.full((3 * BLOCK, 1), -2 * BIG, WIDE),
                jnp.zeros((3 * BLOCK, 1), WIDE),
                jnp.zeros((3 * BLOCK, PAD), WIDE),
            ),
        )
        result = pick_heads(accum / total)
        logsum = top + jnp.log(total)
        for head in range(3):
            result = jnp.where(
                lane == DELTA_LANE + head, logsum[head * BLOCK : (head + 1) * BLOCK], result
            )
        out_ref[rows, :] = result
        return unused

    lax.fori_loop(0, 4, block, 0)
    low = out_ref[...].astype(LOW)
    low_ref[...] = low
    half = 2 * BLOCK
    keep_ref[...] = dot_nn(low[:half], output_ref[...])
    send_ref[...] = dot_nn(low[half:], output_ref[...]).astype(LOW)
    for store in stores:
        store.wait()


def row_mean(values):
    return jnp.sum(values, axis=1, keepdims=True) * (1.0 / values.shape[1])


def norm_parts(values):
    centred = values - row_mean(values)
    scale = lax.rsqrt(row_mean(centred * centred) + EPSILON)
    return centred * scale, scale


def norm_back(upstream, normal, scale):
    return scale * (upstream - row_mean(upstream) - normal * row_mean(upstream * normal))


def middle_kernel(
    expand_spots,
    reduce_spots,
    share,
    place_ref,
    tokens_ref,
    mine_ref,
    mate_ref,
    other_ref,
    cotangent_ref,
    vector_ref,
    expand_add_ref,
    *refs,
):
    parts = len(expand_spots)
    matrices = refs[: parts + len(reduce_spots)]
    (
        layer_ref,
        hidden_grad_ref,
        branch_ref,
        pair_ref,
        low_ref,
        sums_ref,
        expand_ref,
        reduce_ref,
        slope_ref,
        sems,
    ) = refs[len(matrices) :]
    copies = []
    for i, (part, (index, first)) in enumerate(zip(matrices, expand_spots + reduce_spots)):
        target, rows = (expand_ref, share) if i < parts else (reduce_ref, part.shape[0])
        spot = pl.ds(pl.multiple_of(place_ref[index] * rows + first, 8), part.shape[0])
        copies.append(pltpu.make_async_copy(part, target.at[spot], sems.at[i]))
    for copy in copies:
        copy.start()
    output_add, reduce_add, first_scale, first_move, second_scale, second_move = [
        vector_ref[i : i + 1, :] for i in range(6)
    ]
    own = pl.ds(0, BLOCK)
    branch = mine_ref[own, :] + mate_ref[own, :].astype(WIDE) + other_ref[...].astype(WIDE)
    hidden = tokens_ref[...].astype(WIDE) + (branch + output_add)
    first_normal, first_rate = norm_parts(hidden)
    normed = first_normal * first_scale + first_move
    normed_low = normed.astype(LOW)
    low_ref[pl.ds(BLOCK, BLOCK), :] = normed_low
    for copy in copies[:parts]:
        copy.wait()
    width = normed.shape[1]
    reduced = jnp.zeros(normed.shape, WIDE)
    for j in range(4):
        cols = pl.ds(j * width, width)
        expanded = dot_nn(normed_low, expand_ref[:, cols]) + expand_add_ref[:, cols]
        phi_cdf = 0.5 * (1.0 + lax.erf(expanded * (2.0**-0.5)))
        slope_ref[:, cols] = phi_cdf + expanded * (
            jnp.exp(-0.5 * expanded * expanded) * (2.0 * math.pi) ** -0.5
        )
        activated = (expanded * phi_cdf).astype(LOW)
        pair_ref[j, pl.ds(0, BLOCK), :] = activated
        if j == 0:
            for copy in copies[parts:]:
                copy.wait()
        reduced = reduced + dot_nn(activated, reduce_ref[cols, :])
    summed = normed + (reduced + reduce_add)
    second_normal, second_rate = norm_parts(summed)
    layer_ref[...] = (second_normal * second_scale + second_move).astype(LOW)
    upstream = cotangent_ref[...].astype(WIDE)

    def column_sum(row, values):
        sums_ref[row : row + 1, :] = jnp.sum(values, axis=0, keepdims=True)

    column_sum(2, upstream * second_normal)
    column_sum(3, upstream)
    grad_summed = norm_back(upstream * second_scale, second_normal, second_rate)
    reduce_in = grad_summed.astype(LOW)
    low_ref[pl.ds(0, BLOCK), :] = reduce_in
    column_sum(5, reduce_in.astype(WIDE))
    grad_normed = grad_summed
    for j in range(4):
        cols = pl.ds(j * width, width)
        expand_in = (dot_nt(reduce_in, reduce_ref[cols, :]) * slope_ref[:, cols]).astype(LOW)
        pair_ref[j, pl.ds(BLOCK, BLOCK), :] = expand_in
        column_sum(6 + j, expand_in.astype(WIDE))
        grad_normed = grad_normed + dot_nt(expand_in, expand_ref[:, cols])
    column_sum(0, grad_normed * first_normal)
    column_sum(1, grad_normed)
    grad_hidden = norm_back(grad_normed * first_scale, first_normal, first_rate)
    hidden_grad_ref[...] = grad_hidden
    branch_in = grad_hidden.astype(LOW)
    branch_ref[...] = branch_in
    column_sum(4, branch_in.astype(WIDE))


def outgrad_kernel(branch_ref, matrix_ref, attn_ref, out_ref):
    grad = dot_nt(branch_ref[...], matrix_ref[...]).astype(LOW).astype(WIDE)
    attn = attn_ref[...]
    lane = lax.broadcasted_iota(jnp.int32, grad.shape, 1)
    product = grad * attn
    out = jnp.where(lane < DELTA_LANE, grad, 0.0)
    for head in range(3):
        delta = jnp.sum(jnp.where(lanes_of(head, lane), product, 0.0), axis=1, keepdims=True)
        logsum = jnp.sum(jnp.where(lane == DELTA_LANE + head, attn, 0.0), axis=1, keepdims=True)
        for first, column in ((DELTA_LANE, delta), (LSE_LANE, logsum)):
            for i, part in enumerate(parts_of(column)):
                out = jnp.where(lane == first + 3 * head + i, part, out)
    out_ref[...] = out.astype(LOW)


def lse_lanes(query, outgrad):
    lane = lax.broadcasted_iota(jnp.int32, query.shape, 1)
    return jnp.where((lane >= LSE_LANE) & (lane < LSE_LANE + 9), outgrad, query)


def own_blocks(tab_ref, packed, target, sem):
    for i in range(4):
        own = pl.ds(pl.multiple_of(tab_ref[i] * BLOCK, BLOCK), BLOCK)
        pltpu.make_async_copy(packed.at[own], target.at[pl.ds(i * BLOCK, BLOCK)], sem).start()


def own_wait(target, sem):
    pltpu.make_async_copy(target, target, sem).wait()


def query_back_kernel(
    tokens_all, tab_ref, grad_ref, query_all, key_ref, value_ref, out_ref, own_ref, sems
):
    own_blocks(tab_ref, query_all, own_ref, sems.at[0])
    base = tokens_all // BLOCK
    own_wait(own_ref, sems.at[0])

    def block(i, unused):
        rows = pl.ds(pl.multiple_of(i * BLOCK, BLOCK), BLOCK)
        low = tab_ref[base + i]
        outgrad = grad_ref[rows, :]
        left = stack_heads(lse_lanes(own_ref[rows, :], outgrad))
        right = stack_heads(outgrad)

        def visit(c, accum):
            spot = pl.ds(pl.multiple_of(low * BLOCK + c * CHUNK, BLOCK), CHUNK)
            keys = key_ref[spot, :]
            probs = jnp.exp(dot_nt(left, keys))
            slopes = (probs * dot_nt(right, value_ref[spot, :])).astype(LOW)
            return accum + dot_nn(slopes, keys)

        accum = lax.fori_loop(
            0, tab_ref[base + 4 + i], visit, jnp.zeros((3 * BLOCK, PAD), WIDE)
        )
        out_ref[rows, :] = (pick_heads(accum) * HDIM ** (-0.5)).astype(LOW)
        return unused

    lax.fori_loop(0, 4, block, 0)


def vector_rows(n):
    return max(1, 16 // n)


def key_back_kernel(pieces, n, tokens_all, tab_ref, first_ref, last_ref, dq_ref, side_ref, sums_ref, *refs):
    grads = refs[:pieces]
    (
        query_all,
        key_all,
        value_all,
        out_ref,
        late_ref,
        query_ref,
        grad_ref,
        key_ref,
        value_ref,
        sems,
    ) = refs[pieces:]
    query_copy = pltpu.make_async_copy(query_all, query_ref, sems.at[0])
    query_copy.start()
    for i, array in enumerate(grads):
        for j in range(4):
            place = pl.multiple_of(tab_ref[i * 4 + j] * BLOCK, BLOCK)
            pltpu.make_async_copy(
                array.at[pl.ds(j * BLOCK, BLOCK)], grad_ref.at[pl.ds(place, BLOCK)], sems.at[1]
            ).start()
    own_blocks(tab_ref, key_all, key_ref, sems.at[2])
    own_blocks(tab_ref, value_all, value_ref, sems.at[3])
    base = tokens_all // BLOCK
    grad_ref[pl.ds(tokens_all, CHUNK), :] = jnp.zeros((CHUNK, PAD), LOW)
    query_copy.wait()
    whole = grad_ref.at[pl.ds(0, tokens_all)]
    pltpu.make_async_copy(whole, whole, sems.at[1]).wait()
    own_wait(key_ref, sems.at[2])
    own_wait(value_ref, sems.at[3])

    def fix(place, unused):
        rows = pl.ds(pl.multiple_of(place * BLOCK, BLOCK), BLOCK)
        query_ref[rows, :] = lse_lanes(query_ref[rows, :], grad_ref[rows, :])
        return unused

    lax.fori_loop(0, base, fix, 0)

    def block(i, unused):
        rows = pl.ds(pl.multiple_of(i * BLOCK, BLOCK), BLOCK)
        low = tab_ref[base + i]
        zeros = jnp.zeros((3 * BLOCK, PAD), WIDE)
        key_left = stack_heads(key_ref[rows, :])
        value_right = stack_heads(value_ref[rows, :])

        def visit(c, state):
            key_accum, value_accum = state
            spot = pl.ds(pl.multiple_of(low * BLOCK + c * CHUNK, BLOCK), CHUNK)
            queries = query_ref[spot, :]
            outgrads = grad_ref[spot, :]
            probs = jnp.exp(dot_nt(key_left, queries))
            slopes = (probs * dot_nt(value_right, outgrads)).astype(LOW)
            value_accum = value_accum + dot_nn(probs.astype(LOW), outgrads)
            key_accum = key_accum + dot_nn(slopes, queries)
            return key_accum, value_accum

        key_accum, value_accum = lax.fori_loop(0, tab_ref[base + 4 + i], visit, (zeros, zeros))
        out_ref[rows, pl.ds(0, PAD)] = pick_heads(key_accum).astype(LOW)
        out_ref[rows, pl.ds(PAD, PAD)] = pick_heads(value_accum).astype(LOW)
        return unused

    lax.fori_loop(0, 4, block, 0)
    share = DELTA_LANE
    lines = share // n
    many = first_ref.shape[0]
    dkv = out_ref[...]
    columns = [dq_ref[:, :share], dkv[:, :share], dkv[:, PAD : PAD + share]]
    for i, column in enumerate(columns):
        grad = lax.dot_general(
            first_ref[...], column[:many], (((0,), (0,)), ((), ())), preferred_element_type=WIDE
        ) + lax.dot_general(
            last_ref[...], column[many:], (((0,), (0,)), ((), ())), preferred_element_type=WIDE
        )
        for place in range(n):
            for group in range(4):
                row = group * share + place * lines
                late_ref[
                    place, pl.ds(group * lines, lines), pl.ds(i * share, share)
                ] = grad[row : row + lines].astype(LOW)
    side = side_ref[...]
    for place in range(n):
        for group in range(4):
            late_ref[place, pl.ds(group * lines, lines), pl.ds(3 * share, share)] = side[
                place * lines : (place + 1) * lines, group * share : (group + 1) * share
            ]
    few = vector_rows(n)
    rows = jnp.concatenate(
        [
            sums_ref[0:10, :],
            jnp.sum(columns[0].astype(WIDE), axis=0, keepdims=True),
            jnp.sum(columns[2].astype(WIDE), axis=0, keepdims=True),
            jnp.zeros((few * n - 12, share), WIDE),
        ],
        axis=0,
    ).astype(LOW)
    for place in range(n):
        late_ref[place, pl.ds(4 * lines, 16), :] = jnp.zeros((16, late_ref.shape[2]), LOW)
        late_ref[place, pl.ds(4 * lines, few), pl.ds(0, share)] = rows[
            place * few : (place + 1) * few
        ]


def assemble_kernel(n, layout, tab_ref, *refs):
    pieces = refs[:n]
    outs = refs[n:]
    for i, piece in enumerate(pieces):
        chunk = tab_ref[i]
        for out_ref, (first, rows, blocks) in zip(outs, layout):
            wide = out_ref.shape[2] // blocks
            for j in range(blocks):
                out_ref[chunk, :, pl.ds(j * wide, wide)] = piece[
                    pl.ds(first + j * rows, rows), :
                ].astype(WIDE)


def lasting(micros):
    return pl.CostEstimate(flops=0, transcendentals=0, bytes_accessed=int(micros * 3_000_000))


def whole_spec():
    return pl.BlockSpec(memory_space=pltpu.VMEM)


def any_spec():
    return pl.BlockSpec(memory_space=pl.ANY)


def smem_spec():
    return pl.BlockSpec(memory_space=pltpu.SMEM)


PARAMS = pltpu.CompilerParams(vmem_limit_bytes=60 << 20)


def attend(tab, seq_rows, matrix, add, output_rows, token_pieces, tokens_all):
    pieces = len(token_pieces)

    def kernel(*refs):
        attend_kernel(pieces, tokens_all, *refs)

    packed = jax.ShapeDtypeStruct((tokens_all + CHUNK, PAD), LOW)
    width = output_rows.shape[1]
    return pl.pallas_call(
        kernel,
        name="attend",
        out_shape=(
            jax.ShapeDtypeStruct((4 * BLOCK, PAD), WIDE),
            jax.ShapeDtypeStruct((4 * BLOCK, PAD), LOW),
            jax.ShapeDtypeStruct((2 * BLOCK, width), WIDE),
            jax.ShapeDtypeStruct((2 * BLOCK, width), LOW),
            packed,
            packed,
            packed,
        ),
        in_specs=[smem_spec()] + [whole_spec()] * 4 + [any_spec()] * pieces,
        out_specs=(whole_spec(),) * 4 + (any_spec(),) * 3,
        scratch_shapes=[pltpu.VMEM((tokens_all, matrix.shape[0]), LOW)]
        + [pltpu.VMEM((tokens_all + CHUNK, PAD), LOW)] * 3
        + [pltpu.SemaphoreType.DMA((pieces,)), pltpu.SemaphoreType.DMA((3,))],
        compiler_params=PARAMS,
    )(tab, seq_rows, matrix, add, output_rows, *token_pieces)


def query_back(tab, outgrad, queries, keys, values, tokens_all):
    def kernel(*refs):
        query_back_kernel(tokens_all, *refs)

    return pl.pallas_call(
        kernel,
        name="query_back",
        cost_estimate=lasting(11),
        out_shape=jax.ShapeDtypeStruct((4 * BLOCK, PAD), LOW),
        in_specs=[smem_spec(), whole_spec(), any_spec(), whole_spec(), whole_spec()],
        out_specs=whole_spec(),
        scratch_shapes=[pltpu.VMEM((4 * BLOCK, PAD), LOW), pltpu.SemaphoreType.DMA((1,))],
        compiler_params=PARAMS,
    )(tab, outgrad, queries, keys, values)


def key_back(tab, token_pieces, grad_query, side, sums, grad_pieces, packed, tokens_all):
    pieces = len(grad_pieces)
    n = tokens_all // (4 * BLOCK)
    width = token_pieces[0].shape[1]

    def kernel(*refs):
        key_back_kernel(pieces, n, tokens_all, *refs)

    return pl.pallas_call(
        kernel,
        name="key_back",
        cost_estimate=lasting(16),
        out_shape=(
            jax.ShapeDtypeStruct((4 * BLOCK, 2 * PAD), LOW),
            jax.ShapeDtypeStruct((n, width // n + 16, width), LOW),
        ),
        in_specs=[smem_spec()] + [whole_spec()] * 5 + [any_spec()] * (pieces + 3),
        out_specs=(whole_spec(), whole_spec()),
        scratch_shapes=[pltpu.VMEM((tokens_all + CHUNK, PAD), LOW)] * 2
        + [pltpu.VMEM((4 * BLOCK, PAD), LOW)] * 2
        + [pltpu.SemaphoreType.DMA((4,))],
        compiler_params=PARAMS,
    )(tab, *token_pieces, grad_query, side, sums, *grad_pieces, *packed)


def middle(places, tokens, mine, mate, other, cotangent, vectors, expand_add, expands, reduces):
    rows, width = tokens.shape
    hidden = expand_add.shape[1]
    matrices = [part[0] for part in expands + reduces]
    expand_spots = [part[1:] for part in expands]
    reduce_spots = [part[1:] for part in reduces]

    def kernel(*refs):
        middle_kernel(expand_spots, reduce_spots, width // 4, *refs)

    return pl.pallas_call(
        kernel,
        name="middle",
        cost_estimate=lasting(11),
        out_shape=(
            jax.ShapeDtypeStruct((rows, width), LOW),
            jax.ShapeDtypeStruct((rows, width), WIDE),
            jax.ShapeDtypeStruct((rows, width), LOW),
            jax.ShapeDtypeStruct((4, 2 * rows, hidden // 4), LOW),
            jax.ShapeDtypeStruct((2 * rows, width), LOW),
            jax.ShapeDtypeStruct((16, width), WIDE),
        ),
        in_specs=[smem_spec()] + [whole_spec()] * 7 + [any_spec()] * len(matrices),
        out_specs=(whole_spec(),) * 6,
        scratch_shapes=[
            pltpu.VMEM((width, hidden), LOW),
            pltpu.VMEM((hidden, width), LOW),
            pltpu.VMEM((rows, hidden), WIDE),
            pltpu.SemaphoreType.DMA((len(matrices),)),
        ],
        compiler_params=PARAMS,
    )(places, tokens, mine, mate, other, cotangent, vectors, expand_add, *matrices)


def attend_outgrad(branch, matrix, attn):
    return pl.pallas_call(
        outgrad_kernel,
        name="outgrad",
        cost_estimate=lasting(3),
        out_shape=jax.ShapeDtypeStruct((4 * BLOCK, PAD), LOW),
        in_specs=[whole_spec()] * 3,
        out_specs=whole_spec(),
    )(branch, matrix, attn)


def assemble(chunks, pieces, layout, shapes):
    n = len(pieces)

    def kernel(*refs):
        assemble_kernel(n, layout, *refs)

    outs = pl.pallas_call(
        kernel,
        name="assemble",
        cost_estimate=lasting(4),
        out_shape=tuple(
            jax.ShapeDtypeStruct((n, shape[0] // n, shape[1]), WIDE) for shape in shapes
        ),
        in_specs=[smem_spec()] + [whole_spec()] * n,
        out_specs=tuple(whole_spec() for _ in shapes),
        compiler_params=PARAMS,
    )(chunks, *pieces)
    return [out.reshape(shape) for out, shape in zip(outs, shapes)]


class RingGather:
    def __init__(self, value, n, split=True):
        self.n, self.split, self.done = n, split, 0
        self.value = value
        self.last = (value, value)
        self.ahead, self.back = [], []

    def keep(self):
        if self.done:
            self.ahead.append(self.last[0])
            if self.done < self.n // 2:
                self.back.append(self.last[1])

    def step(self):
        self.keep()
        self.done += 1
        f, b = self.last
        rows = self.value.shape[0] // 2
        if self.done < self.n // 2:
            self.last = (ring_shift(f, self.n, 1), ring_shift(b, self.n, -1))
        elif self.split:
            parts = ring_shift(f[:rows], self.n, 1), ring_shift(b[rows:], self.n, -1)
            self.last = (jnp.concatenate(parts, axis=0),)
        else:
            self.last = (ring_shift(f, self.n, 1),)

    def pieces(self):
        self.keep()
        return [self.value] + self.ahead + self.back


class RingReduce:
    def __init__(self, local, rank, n):
        self.local, self.rank, self.n, self.done = local, rank, n, 0
        self.last = None

    def part(self, step):
        return lax.dynamic_index_in_dim(
            self.local, (self.rank + step) % self.n, 0, keepdims=False
        )

    def step(self):
        half = self.n // 2
        if self.done == 0:
            f, b = self.part(half), self.part(1 - half)
        else:
            f, b = self.last
            f = (f.astype(WIDE) + self.part(half - self.done).astype(WIDE)).astype(LOW)
            if self.done < half - 1:
                b = (b.astype(WIDE) + self.part(1 - half + self.done).astype(WIDE)).astype(LOW)
        f = ring_shift(f, self.n, 1)
        if self.done < half - 1:
            b = ring_shift(b, self.n, -1)
        self.last = (f, b)
        self.done += 1

    def total(self):
        f, b = self.last
        return f.astype(WIDE) + b.astype(WIDE) + self.part(0).astype(WIDE)


def pad_group(block):
    return jnp.pad(block, ((0, 0), (0, PAD - block.shape[1])))


def on_device(
    n,
    tokens,
    block_order,
    seq_lengths,
    cotangent,
    query_matrix,
    key_matrix,
    value_matrix,
    output_matrix,
    expand_matrix,
    reduce_matrix,
    query_bias,
    value_bias,
    output_bias,
    expand_bias,
    reduce_bias,
    first_gain,
    first_shift,
    second_gain,
    second_shift,
):
    w = lax.axis_index("wsh")
    c = lax.axis_index("ctx")
    barrier = lax.optimization_barrier
    order = ring_of(n)
    rank = jnp.asarray([order.index(i) for i in range(n)], jnp.int32)[c]
    width = tokens.shape[1]
    share = width // 4
    tokens_all = n * 4 * BLOCK

    other = wsh_swap(tokens, 2)
    both = jnp.concatenate([tokens, other], axis=0)
    (
        query_matrix,
        key_matrix,
        value_matrix,
        output_matrix,
        expand_matrix,
        reduce_matrix,
        output_bias,
        reduce_bias,
        expand_bias,
        first_gain,
        first_shift,
        second_gain,
        second_shift,
        other,
    ) = lax.optimization_barrier(
        (
            query_matrix,
            key_matrix,
            value_matrix,
            output_matrix,
            expand_matrix,
            reduce_matrix,
            output_bias,
            reduce_bias,
            expand_bias,
            first_gain,
            first_shift,
            second_gain,
            second_shift,
            other,
        )
    )

    def columns(matrix, group):
        low = matrix.astype(LOW)
        return [group(low[:, i * share : (i + 1) * share]) for i in range(4)]

    qkv_blocks = jnp.stack(
        [
            jnp.concatenate(parts, axis=1)
            for parts in zip(
                columns(query_matrix, pad_group),
                columns(key_matrix, pad_group),
                columns(value_matrix, pad_group),
            )
        ]
    )
    def deal(blocks):
        return lax.all_to_all(blocks, "wsh", 0, 0).reshape(-1, blocks.shape[2])

    qkv_matrix = deal(qkv_blocks)
    vectors = jnp.stack(
        [output_bias, reduce_bias, first_gain, first_shift, second_gain, second_shift]
    )
    vectors = jnp.concatenate([vectors, expand_bias.reshape(4, share)], axis=0).astype(LOW)
    vectors = jnp.concatenate(
        to_absolute([vectors] + [wsh_swap(vectors, j) for j in range(1, 4)], w), axis=1
    ).astype(WIDE)
    expand_add = vectors[6:].reshape(4, 4, share).transpose(1, 0, 2).reshape(1, -1)
    nothing = jnp.zeros((PAD,), LOW)
    fill = jnp.zeros((PAD - share,), LOW)
    qkv_add = jnp.concatenate(
        [query_bias.astype(LOW), fill, nothing, value_bias.astype(LOW), fill]
    ).astype(WIDE)[None, :]
    output_low = output_matrix.astype(LOW)
    output_rows = jnp.pad(output_low, ((0, PAD - share), (0, 0)))

    ends = jnp.cumsum(seq_lengths)
    steps = jnp.asarray(slot_steps(n), jnp.int32)
    from_ctx = jnp.asarray(order, jnp.int32)[(rank + steps) % n]
    blocks = (from_ctx[:, None] * 4 + (w ^ jnp.asarray(ORDER, jnp.int32))[None, :]).reshape(-1)
    places = block_order[blocks]
    first = places[:4] * BLOCK
    low = jnp.max(jnp.where(ends[None, :] <= first[:, None], ends[None, :], 0), axis=1)
    last = first + BLOCK - 1
    high = jnp.min(jnp.where(ends[None, :] > last[:, None], ends[None, :], tokens_all), axis=1)
    low_block = low // BLOCK
    count = (high - low_block * BLOCK + CHUNK - 1) // CHUNK
    tab = jnp.concatenate([places, low_block, count]).astype(jnp.int32)
    seqs = seq_lengths.shape[0]
    seq_rows = jnp.pad(
        jnp.stack([ends - seq_lengths, ends]), ((0, 6), (SEQ_LANE, PAD - SEQ_LANE - seqs))
    ).astype(jnp.int32)

    expand_low, reduce_low = expand_matrix.astype(LOW), reduce_matrix.astype(LOW)
    third = share // 3
    expand_other = []
    ring = RingGather(both, n)
    half = n // 2
    for step in range(1, half + 1):
        ring.step()
        if step > 2 and len(expand_other) < 3:
            first = len(expand_other) * third
            expand_other.append(wsh_swap(expand_low[first : first + third], 2))
        if step == 2:
            ready = (tab, seq_rows, qkv_add, output_rows, expand_low, reduce_low)
            ring.last, qkv_matrix, ready = barrier((ring.last, qkv_matrix, ready))
            tab, seq_rows, qkv_add, output_rows, expand_low, reduce_low = ready
        elif step == 3:
            ring.last, expand_other[0], vectors, expand_add = barrier(
                (ring.last, expand_other[0], vectors[:8], expand_add)
            )
        elif step == half:
            ring.last, expand_other[1] = barrier((ring.last, expand_other[1]))
    while len(expand_other) < 3:
        first = len(expand_other) * third
        expand_other.append(wsh_swap(expand_low[first : first + third], 2))
    token_pieces = []
    for piece in ring.pieces():
        token_pieces += [piece, wsh_swap(piece, 1)]
    reduce_other, unused = barrier((reduce_low, qkv_matrix))
    reduce_other = wsh_swap(reduce_other, 2)
    expand_mate, reduce_mate = wsh_swap(expand_low, 1), wsh_swap(reduce_low, 1)
    expand_last = [wsh_swap(expand_other[0], 1)]
    attn, attended, keep, send, packed_queries, packed_keys, packed_values = attend(
        tab, seq_rows, qkv_matrix, qkv_add, output_rows, token_pieces, tokens_all
    )
    from_mate = wsh_swap(send, 1)
    expand_other[1:], reduce_other, unused = barrier((expand_other[1:], reduce_other, from_mate))
    expand_last += [wsh_swap(part, 1) for part in expand_other[1:]]
    expand_parts = [(expand_low, 0, 0), (expand_mate, 2, 0)]
    for i in range(3):
        expand_parts += [(expand_other[i], 1, i * third), (expand_last[i], 3, i * third)]
    reduce_parts = [
        (reduce_low, 0, 0),
        (reduce_mate, 2, 0),
        (reduce_other, 1, 0),
        (wsh_swap(reduce_other, 1), 3, 0),
    ]
    from_other = wsh_swap((keep[BLOCK:] + from_mate[BLOCK:].astype(WIDE)).astype(LOW), 2)
    group = (w ^ jnp.asarray(ORDER, jnp.int32)).astype(jnp.int32)
    layer_out, grad_hidden, branch_in, pair, lows, sums = middle(
        group,
        tokens,
        keep,
        from_mate,
        from_other,
        cotangent,
        vectors,
        expand_add,
        expand_parts,
        reduce_parts,
    )
    branch_pieces = group_pieces(branch_in)
    branch_all = jnp.concatenate(branch_pieces, axis=0)
    outgrad = attend_outgrad(branch_all, output_rows, attn)
    grad_output = lax.dot_general(
        attended[:, :share], branch_all, (((0,), (0,)), ((), ())), preferred_element_type=WIDE
    ).astype(LOW)

    def rows_dot(left, right):
        return lax.dot_general(
            left, right, (((0,), (0,)), ((), ())), preferred_element_type=WIDE
        ).astype(LOW)

    def redeal(chunk):
        lines = chunk.shape[0] // 4
        return lax.all_to_all(chunk.astype(LOW).reshape(4, lines, -1), "wsh", 0, 0)

    def by_place(matrix):
        cols = matrix.shape[1]
        return matrix.reshape(4, n, share // n, cols).transpose(1, 0, 2, 3).reshape(n, -1, cols)

    def joined(dealt, first):
        return jnp.concatenate([dealt[i, :, first : first + share] for i in range(4)], axis=1)

    shard = reduce_matrix.shape[0]
    lines = share // n
    pair, lows, branch_pieces[1] = barrier((pair, lows, branch_pieces[1]))
    pair = lax.all_to_all(pair, "wsh", 0, 0)
    lows = [lows, wsh_swap(lows, 2)]
    grad_ring = RingGather(outgrad, n, split=False)
    for step in range(2):
        grad_ring.step()
        grad_ring.last, outgrad = barrier((grad_ring.last, outgrad))
    pair, lows, sums, outgrad = barrier((pair, lows, sums, outgrad))
    lows = to_absolute([lows[0], wsh_swap(lows[0], 1), lows[1], wsh_swap(lows[1], 1)], w)
    reduce_all = jnp.concatenate([low[:BLOCK] for low in lows], axis=0)
    normed_all = jnp.concatenate([low[BLOCK:] for low in lows], axis=0)
    grad_reduce = rows_dot(pair[:, :BLOCK].reshape(4 * BLOCK, -1), reduce_all)
    grad_expand = rows_dot(normed_all, pair[:, BLOCK:].reshape(4 * BLOCK, -1))
    early_ring = RingReduce(
        jnp.concatenate(
            [grad_reduce.reshape(n, shard // n, width), by_place(grad_expand)], axis=1
        ),
        rank,
        n,
    )
    grad_ring.step()
    early_ring.step()
    grad_query = query_back(tab, outgrad, packed_queries, packed_keys, packed_values, tokens_all)
    grad_ring.last, early_ring.last, grad_query, sums = barrier(
        (grad_ring.last, early_ring.last, grad_query, sums)
    )
    split = jnp.concatenate(
        [sums[:6].reshape(6, 4, share).transpose(1, 0, 2), sums[6:10].reshape(4, 4, share)], axis=1
    )
    sums = jnp.sum(lax.all_to_all(split, "wsh", 0, 0), axis=0)

    grad_ring.step()
    early_ring.step()
    grad_ring.last, early_ring.last, sums = barrier((grad_ring.last, early_ring.last, sums))
    for step in range(4, half):
        grad_ring.step()
        early_ring.step()
        grad_ring.last, early_ring.last, sums = barrier((grad_ring.last, early_ring.last, sums))
    early_ring.step()
    grad_kv, late = key_back(
        tab,
        token_pieces[:2],
        grad_query,
        grad_output,
        sums,
        grad_ring.pieces(),
        (packed_queries, packed_keys, packed_values),
        tokens_all,
    )
    early_ring.last, grad_kv, late = barrier((early_ring.last, grad_kv, late))
    late_ring = RingReduce(late, rank, n)
    early_gather = None
    for step in range(half):
        late_ring.step()
        if early_ring.done < half:
            early_ring.step()
            late_ring.last, early_ring.last = barrier((late_ring.last, early_ring.last))
        elif early_gather is None:
            early = early_ring.total()
            early = jnp.concatenate(
                [
                    early[: shard // n].astype(LOW),
                    redeal(early[shard // n :]).reshape(4 * lines, width),
                ],
                axis=0,
            )
            late_ring.last, early = barrier((late_ring.last, early))
            early_gather = RingGather(early, n, split=False)
        else:
            early_gather.step()
            late_ring.last, early_gather.last = barrier((late_ring.last, early_gather.last))
    late = late_ring.total()
    early_gather.step()
    extra = late[4 * lines :].astype(LOW)
    side = late[: 4 * lines, 3 * share :].astype(LOW).reshape(4, lines, share)
    dealt = redeal(late[: 4 * lines, : 3 * share])
    late = jnp.concatenate(
        [joined(dealt, i * share) for i in range(3)] + [joined(side, 0), extra], axis=0
    )
    late, early_gather.last = barrier((late, early_gather.last))
    chunks = (rank + steps) % n
    late_gather = RingGather(late, n, split=False)
    out_reduce = None
    for step in range(half):
        late_gather.step()
        if early_gather.done < half:
            early_gather.step()
            late_gather.last, early_gather.last = barrier((late_gather.last, early_gather.last))
        elif out_reduce is None:
            out_reduce, out_expand = assemble(
                chunks,
                early_gather.pieces(),
                ((0, shard // n, 1), (shard // n, lines, 4)),
                ((shard, width), (share, 4 * width)),
            )
            late_gather.last, out_reduce, out_expand = barrier(
                (late_gather.last, out_reduce, out_expand)
            )
    tokens_grad = (
        scatter_group(
            dot_nt(grad_query, qkv_matrix[:, :PAD]) + dot_nt(grad_kv, qkv_matrix[:, PAD:])
        )
        + grad_hidden
    ).astype(LOW)
    out_query, out_key, out_value, out_output, small = assemble(
        chunks,
        late_gather.pieces(),
        tuple((i * lines, lines, 1) for i in range(4)) + ((4 * lines, 8, 1),),
        ((share, width),) * 4 + ((8 * n, width),),
    )
    small = small.reshape(n, 8, width)[:, : vector_rows(n), :share].reshape(-1, share)
    out_expand_bias = small[6:10].reshape(-1)
    return (
        layer_out,
        tokens_grad,
        out_query,
        out_key,
        out_value,
        out_output,
        out_expand,
        out_reduce,
        small[10],
        small[11],
        small[4],
        out_expand_bias,
        small[5],
        small[0],
        small[1],
        small[2],
        small[3],
    )


def solution(mesh):
    n = mesh.shape["ctx"]
    rows = P(("ctx", "wsh"), None)
    in_specs = (rows, P(), P(), rows) + (P("wsh", None),) * 6 + (P("wsh"),) * 9
    out_specs = (rows, rows) + (P("wsh", None),) * 6 + (P("wsh"),) * 9

    def run(*args):
        return on_device(n, *args)

    return jax.shard_map(run, mesh=mesh, in_specs=in_specs, out_specs=out_specs, check_vma=False)
```

```python
import math

import jax
import jax.numpy as jnp
from jax import lax
from jax.experimental import pallas as pl
from jax.experimental.pallas import tpu as pltpu
from jax.sharding import PartitionSpec as P

HDIM = 64
BLOCK = 128
EPSILON = 1e-12
LOW = jnp.bfloat16
WIDE = jnp.float32

ORDER = (0, 2, 1, 3)

PAD = 256
DELTA_LANE = 192
LSE_LANE = 201
SEQ_LANE = 216
BIG = 1e30
CHUNK = 1024


def ring_of(n):
    return list(range(0, n, 2)) + list(range(n - 1, 0, -2))


def exchange(value, axis, size, flip):
    return lax.ppermute(value, axis, [(i, i ^ flip) for i in range(size)])


def wsh_swap(value, flip):
    return exchange(value, "wsh", 4, flip)


def to_absolute(pieces, w):
    one = (w & 1) == 1
    two = (w & 2) == 2
    a = [jnp.where(one, pieces[j ^ 1], pieces[j]) for j in range(4)]
    return [jnp.where(two, a[j ^ 2], a[j]) for j in range(4)]


def group_pieces(value):
    other = wsh_swap(value, 2)
    return [value, other, wsh_swap(value, 1), wsh_swap(other, 1)]


def scatter_group(parts):
    rows = parts.shape[0] // 4
    mine, other, mate, last = [parts[i * rows : (i + 1) * rows] for i in range(4)]
    got = wsh_swap(jnp.concatenate([mate, last], axis=0).astype(LOW), 1).astype(WIDE)
    mine = mine + got[:rows]
    other = other + got[rows:]
    return mine + wsh_swap(other.astype(LOW), 2).astype(WIDE)


def ring_shift(value, n, step):
    ring = ring_of(n)
    return lax.ppermute(value, "ctx", [(ring[i], ring[(i + step) % n]) for i in range(n)])


def ring_gather(value, n, split=True, tie=None):
    half = n // 2
    rows = value.shape[0]
    ahead, back = [], []
    f = b = value
    tied = None
    for step in range(1, half + 1):
        if tie is not None and step == tie[0]:
            f, b, tied = lax.optimization_barrier((f, b, tie[1]))
        if step < half:
            f = ring_shift(f, n, 1)
            b = ring_shift(b, n, -1)
            ahead.append(f)
            back.append(b)
        elif not split:
            ahead.append(ring_shift(f, n, 1))
        else:
            first = ring_shift(f[: rows // 2], n, 1)
            second = ring_shift(b[rows // 2 :], n, -1)
            ahead.append(jnp.concatenate([first, second], axis=0))
    pieces = [value] + ahead + back
    return pieces if tie is None else (pieces, tied)


def slot_steps(n):
    half = n // 2
    return [0] + [-s for s in range(1, half + 1)] + list(range(1, half))


def lanes_of(head, lane):
    keep = (lane >= head * HDIM) & (lane < (head + 1) * HDIM)
    return keep


def stack_heads(value):
    lane = lax.broadcasted_iota(jnp.int32, value.shape, 1)
    out = []
    for head in range(3):
        keep = (
            lanes_of(head, lane)
            | ((lane >= DELTA_LANE + 3 * head) & (lane < DELTA_LANE + 3 * head + 3))
            | ((lane >= LSE_LANE + 3 * head) & (lane < LSE_LANE + 3 * head + 3))
            | (lane >= SEQ_LANE)
        )
        out.append(jnp.where(keep, value, jnp.zeros_like(value)))
    return jnp.concatenate(out, axis=0)


def pick_heads(value):
    lane = lax.broadcasted_iota(jnp.int32, (BLOCK, PAD), 1)
    total = jnp.zeros((BLOCK, PAD), WIDE)
    for head in range(3):
        total = jnp.where(lanes_of(head, lane), value[head * BLOCK : (head + 1) * BLOCK], total)
    return total


def dot_nt(a, b):
    return lax.dot_general(a, b, (((1,), (1,)), ((), ())), preferred_element_type=WIDE)


def dot_nn(a, b):
    return jnp.dot(a, b, preferred_element_type=WIDE)


def seq_marks(seq_ref, place):
    spot = place * BLOCK + lax.broadcasted_iota(jnp.int32, (BLOCK, PAD), 0)
    return (spot >= seq_ref[0:1, :]) & (spot < seq_ref[1:2, :])


def key_lanes(seq_ref, place, value):
    lane = lax.broadcasted_iota(jnp.int32, (BLOCK, PAD), 1)
    marks = seq_marks(seq_ref, place)
    minus = (lane >= LSE_LANE) & (lane < LSE_LANE + 9)
    out = jnp.where(minus, -1.0, value.astype(WIDE))
    return jnp.where((lane >= SEQ_LANE) & ~marks, -BIG, out).astype(LOW)


def query_lanes(seq_ref, place, value):
    return jnp.where(seq_marks(seq_ref, place), 1.0, value.astype(WIDE)).astype(LOW)


def value_lanes(value):
    lane = lax.broadcasted_iota(jnp.int32, (BLOCK, PAD), 1)
    minus = (lane >= DELTA_LANE) & (lane < DELTA_LANE + 9)
    return jnp.where(minus, -1.0, value.astype(WIDE)).astype(LOW)


def parts_of(column):
    high = column.astype(LOW).astype(WIDE)
    rest = column - high
    mid = rest.astype(LOW).astype(WIDE)
    return high, mid, (rest - mid).astype(LOW).astype(WIDE)


def end_rows(seq_value):
    lane = lax.broadcasted_iota(jnp.int32, (CHUNK, PAD), 1)
    return jnp.where(lane >= SEQ_LANE, seq_value, 0.0).astype(LOW)


def attend_kernel(pieces, tokens_all, tab_ref, seq_ref, matrix_ref, add_ref, output_ref, *refs):
    tokens = refs[:pieces]
    (
        out_ref,
        low_ref,
        keep_ref,
        send_ref,
        query_out,
        key_out,
        value_out,
        token_ref,
        query_ref,
        key_ref,
        value_ref,
        token_sems,
        sems,
    ) = refs[pieces:]
    per = tokens[0].shape[0] // BLOCK
    many = tokens[0].shape[0]
    copies = [
        pltpu.make_async_copy(tokens[i], token_ref.at[pl.ds(i * many, many)], token_sems.at[i])
        for i in range(pieces)
    ]
    for copy in copies:
        copy.start()
    base = tokens_all // BLOCK
    rest = pl.ds(tokens_all, CHUNK)
    key_ref[rest, :] = end_rows(-BIG)
    query_ref[rest, :] = end_rows(1.0)
    value_ref[rest, :] = jnp.zeros((CHUNK, PAD), LOW)

    def project(i, unused):
        rows = pl.ds(pl.multiple_of(i * 2 * many, BLOCK), 2 * many)
        for j in range(2):
            spot = token_ref.at[pl.ds(pl.multiple_of((i * 2 + j) * many, BLOCK), many)]
            pltpu.make_async_copy(spot, spot, token_sems.at[i * 2 + j]).wait()
        wide = dot_nn(token_ref[rows, :], matrix_ref[...]) + add_ref[...]
        low = wide.astype(LOW)
        for j in range(2 * per):
            place = tab_ref[i * 2 * per + j]
            spot = pl.ds(pl.multiple_of(place * BLOCK, BLOCK), BLOCK)
            block = low[j * BLOCK : (j + 1) * BLOCK]
            query = block[:, :PAD].astype(WIDE) * HDIM ** (-0.5)
            query_ref[spot, :] = query_lanes(seq_ref, place, query)
            key_ref[spot, :] = key_lanes(seq_ref, place, block[:, PAD : 2 * PAD])
            value_ref[spot, :] = value_lanes(block[:, 2 * PAD :])
        return unused

    lax.fori_loop(0, pieces // 2, project, 0)
    stores = [
        pltpu.make_async_copy(source, target, sems.at[i])
        for i, (source, target) in enumerate(
            ((query_ref, query_out), (key_ref, key_out), (value_ref, value_out))
        )
    ]
    for store in stores:
        store.start()
    lane = lax.broadcasted_iota(jnp.int32, (BLOCK, PAD), 1)

    def block(i, unused):
        rows = pl.ds(pl.multiple_of(i * BLOCK, BLOCK), BLOCK)
        own = pl.ds(pl.multiple_of(tab_ref[i] * BLOCK, BLOCK), BLOCK)
        low = tab_ref[base + i]
        count = tab_ref[base + 4 + i]
        queries = stack_heads(query_ref[own, :])

        def visit(c, state):
            top, total, accum = state
            spot = pl.ds(pl.multiple_of(low * BLOCK + c * CHUNK, BLOCK), CHUNK)
            scores = dot_nt(queries, key_ref[spot, :])
            top_new = jnp.maximum(top, jnp.max(scores, axis=1, keepdims=True))
            weights = jnp.exp(scores - top_new)
            factor = jnp.exp(top - top_new)
            total = total * factor + jnp.sum(weights, axis=1, keepdims=True)
            accum = accum * factor + dot_nn(weights.astype(LOW), value_ref[spot, :])
            return top_new, total, accum

        top, total, accum = lax.fori_loop(
            0,
            count,
            visit,
            (
                jnp.full((3 * BLOCK, 1), -2 * BIG, WIDE),
                jnp.zeros((3 * BLOCK, 1), WIDE),
                jnp.zeros((3 * BLOCK, PAD), WIDE),
            ),
        )
        result = pick_heads(accum / total)
        logsum = top + jnp.log(total)
        for head in range(3):
            result = jnp.where(
                lane == DELTA_LANE + head, logsum[head * BLOCK : (head + 1) * BLOCK], result
            )
        out_ref[rows, :] = result
        return unused

    lax.fori_loop(0, 4, block, 0)
    low = out_ref[...].astype(LOW)
    low_ref[...] = low
    half = 2 * BLOCK
    keep_ref[...] = dot_nn(low[:half], output_ref[...])
    send_ref[...] = dot_nn(low[half:], output_ref[...]).astype(LOW)
    for store in stores:
        store.wait()


def row_mean(values):
    return jnp.sum(values, axis=1, keepdims=True) * (1.0 / values.shape[1])


def norm_parts(values):
    centred = values - row_mean(values)
    scale = lax.rsqrt(row_mean(centred * centred) + EPSILON)
    return centred * scale, scale


def norm_back(upstream, normal, scale):
    return scale * (upstream - row_mean(upstream) - normal * row_mean(upstream * normal))


def middle_kernel(
    expand_spots,
    reduce_spots,
    share,
    place_ref,
    tokens_ref,
    mine_ref,
    mate_ref,
    other_ref,
    cotangent_ref,
    *refs,
):
    parts = len(expand_spots)
    vectors, refs = refs[:4], refs[4:]
    matrices = refs[: parts + len(reduce_spots)]
    (
        layer_ref,
        hidden_grad_ref,
        branch_ref,
        pair_ref,
        low_ref,
        expand_ref,
        reduce_ref,
        slope_ref,
        sums_ref,
        vector_ref,
        sems,
    ) = refs[len(matrices) :]
    copies = []
    for i, (part, (index, first)) in enumerate(zip(matrices, expand_spots + reduce_spots)):
        target, rows = (expand_ref, share) if i < parts else (reduce_ref, reduce_ref.shape[0] // 4)
        if isinstance(first, tuple):
            first = place_ref[first[0]]
        spot = pl.ds(pl.multiple_of(place_ref[index] * rows + first, 8), part.shape[0])
        copies.append(pltpu.make_async_copy(part, target.at[spot], sems.at[i]))
    for copy in copies:
        copy.start()
    for i, piece in enumerate(vectors):
        vector_ref[place_ref[i]] = piece[...].astype(WIDE)
    by_device = [vector_ref[j] for j in range(4)]
    output_add, reduce_add, first_scale, first_move, second_scale, second_move = [
        jnp.concatenate([rows[i : i + 1] for rows in by_device], axis=1) for i in range(6)
    ]
    expand_add = [
        jnp.concatenate([rows[i : i + 1] for i in range(6, 10)], axis=1) for rows in by_device
    ]
    own = pl.ds(0, BLOCK)
    branch = mine_ref[own, :] + mate_ref[own, :].astype(WIDE) + other_ref[...].astype(WIDE)
    hidden = tokens_ref[...].astype(WIDE) + (branch + output_add)
    first_normal, first_rate = norm_parts(hidden)
    normed = first_normal * first_scale + first_move
    normed_low = normed.astype(LOW)
    low_ref[pl.ds(BLOCK, BLOCK), :] = normed_low
    for copy in copies[:parts]:
        copy.wait()
    width = normed.shape[1]
    reduced = jnp.zeros(normed.shape, WIDE)
    for j in range(4):
        cols = pl.ds(j * width, width)
        expanded = dot_nn(normed_low, expand_ref[:, cols]) + expand_add[j]
        phi_cdf = 0.5 * (1.0 + lax.erf(expanded * (2.0**-0.5)))
        slope_ref[:, cols] = phi_cdf + expanded * (
            jnp.exp(-0.5 * expanded * expanded) * (2.0 * math.pi) ** -0.5
        )
        activated = (expanded * phi_cdf).astype(LOW)
        pair_ref[j, pl.ds(0, BLOCK), :] = activated
        if j == 0:
            for copy in copies[parts:]:
                copy.wait()
        reduced = reduced + dot_nn(activated, reduce_ref[cols, :])
    summed = normed + (reduced + reduce_add)
    second_normal, second_rate = norm_parts(summed)
    layer_ref[...] = (second_normal * second_scale + second_move).astype(LOW)
    upstream = cotangent_ref[...].astype(WIDE)

    def column_sum(row, values):
        sums_ref[row : row + 1, :] = jnp.sum(values, axis=0, keepdims=True)

    column_sum(2, upstream * second_normal)
    column_sum(3, upstream)
    grad_summed = norm_back(upstream * second_scale, second_normal, second_rate)
    reduce_in = grad_summed.astype(LOW)
    low_ref[pl.ds(0, BLOCK), :] = reduce_in
    column_sum(5, reduce_in.astype(WIDE))
    grad_normed = grad_summed
    for j in range(4):
        cols = pl.ds(j * width, width)
        expand_in = (dot_nt(reduce_in, reduce_ref[cols, :]) * slope_ref[:, cols]).astype(LOW)
        pair_ref[j, pl.ds(BLOCK, BLOCK), :] = expand_in
        column_sum(6 + j, expand_in.astype(WIDE))
        grad_normed = grad_normed + dot_nt(expand_in, expand_ref[:, cols])
    column_sum(0, grad_normed * first_normal)
    column_sum(1, grad_normed)
    grad_hidden = norm_back(grad_normed * first_scale, first_normal, first_rate)
    hidden_grad_ref[...] = grad_hidden
    branch_in = grad_hidden.astype(LOW)
    branch_ref[...] = branch_in
    column_sum(4, branch_in.astype(WIDE))
    for j in range(4):
        rows = [sums_ref[0:6, j * share : (j + 1) * share]]
        rows += [sums_ref[6 + j : 7 + j, k * share : (k + 1) * share] for k in range(4)]
        rows = jnp.concatenate(rows + [jnp.zeros((6, share), WIDE)], axis=0)
        pair_ref[j, pl.ds(2 * BLOCK, 16), :] = jnp.zeros((16, width), LOW)
        pair_ref[j, pl.ds(2 * BLOCK, 16), pl.ds(0, share)] = rows.astype(LOW)


def outgrad_kernel(branch_ref, matrix_ref, attn_ref, out_ref):
    grad = dot_nt(branch_ref[...], matrix_ref[...]).astype(LOW).astype(WIDE)
    attn = attn_ref[...]
    lane = lax.broadcasted_iota(jnp.int32, grad.shape, 1)
    product = grad * attn
    out = jnp.where(lane < DELTA_LANE, grad, 0.0)
    for head in range(3):
        delta = jnp.sum(jnp.where(lanes_of(head, lane), product, 0.0), axis=1, keepdims=True)
        logsum = jnp.sum(jnp.where(lane == DELTA_LANE + head, attn, 0.0), axis=1, keepdims=True)
        for first, column in ((DELTA_LANE, delta), (LSE_LANE, logsum)):
            for i, part in enumerate(parts_of(column)):
                out = jnp.where(lane == first + 3 * head + i, part, out)
    out_ref[...] = out.astype(LOW)


def lse_lanes(query, outgrad):
    lane = lax.broadcasted_iota(jnp.int32, query.shape, 1)
    return jnp.where((lane >= LSE_LANE) & (lane < LSE_LANE + 9), outgrad, query)


def own_blocks(tab_ref, packed, target, sem):
    for i in range(4):
        own = pl.ds(pl.multiple_of(tab_ref[i] * BLOCK, BLOCK), BLOCK)
        pltpu.make_async_copy(packed.at[own], target.at[pl.ds(i * BLOCK, BLOCK)], sem).start()


def own_wait(target, sem):
    pltpu.make_async_copy(target, target, sem).wait()


def query_back_kernel(
    tokens_all, tab_ref, grad_ref, query_all, key_ref, value_ref, out_ref, own_ref, sems
):
    own_blocks(tab_ref, query_all, own_ref, sems.at[0])
    base = tokens_all // BLOCK
    own_wait(own_ref, sems.at[0])

    def block(i, unused):
        rows = pl.ds(pl.multiple_of(i * BLOCK, BLOCK), BLOCK)
        low = tab_ref[base + i]
        outgrad = grad_ref[rows, :]
        left = stack_heads(lse_lanes(own_ref[rows, :], outgrad))
        right = stack_heads(outgrad)

        def visit(c, accum):
            spot = pl.ds(pl.multiple_of(low * BLOCK + c * CHUNK, BLOCK), CHUNK)
            keys = key_ref[spot, :]
            probs = jnp.exp(dot_nt(left, keys))
            slopes = (probs * dot_nt(right, value_ref[spot, :])).astype(LOW)
            return accum + dot_nn(slopes, keys)

        accum = lax.fori_loop(
            0, tab_ref[base + 4 + i], visit, jnp.zeros((3 * BLOCK, PAD), WIDE)
        )
        out_ref[rows, :] = (pick_heads(accum) * HDIM ** (-0.5)).astype(LOW)
        return unused

    lax.fori_loop(0, 4, block, 0)


def vector_rows(n):
    return max(1, 16 // n)


def key_back_kernel(pieces, n, tokens_all, tab_ref, first_ref, last_ref, dq_ref, side_ref, sums_ref, *refs):
    grads = refs[:pieces]
    (
        query_all,
        key_all,
        value_all,
        out_ref,
        late_ref,
        query_ref,
        grad_ref,
        key_ref,
        value_ref,
        sems,
    ) = refs[pieces:]
    query_copy = pltpu.make_async_copy(query_all, query_ref, sems.at[0])
    query_copy.start()
    for i, array in enumerate(grads):
        for j in range(4):
            place = pl.multiple_of(tab_ref[i * 4 + j] * BLOCK, BLOCK)
            pltpu.make_async_copy(
                array.at[pl.ds(j * BLOCK, BLOCK)], grad_ref.at[pl.ds(place, BLOCK)], sems.at[1]
            ).start()
    own_blocks(tab_ref, key_all, key_ref, sems.at[2])
    own_blocks(tab_ref, value_all, value_ref, sems.at[3])
    base = tokens_all // BLOCK
    grad_ref[pl.ds(tokens_all, CHUNK), :] = jnp.zeros((CHUNK, PAD), LOW)
    query_copy.wait()
    whole = grad_ref.at[pl.ds(0, tokens_all)]
    pltpu.make_async_copy(whole, whole, sems.at[1]).wait()
    own_wait(key_ref, sems.at[2])
    own_wait(value_ref, sems.at[3])

    def fix(place, unused):
        rows = pl.ds(pl.multiple_of(place * BLOCK, BLOCK), BLOCK)
        query_ref[rows, :] = lse_lanes(query_ref[rows, :], grad_ref[rows, :])
        return unused

    lax.fori_loop(0, base, fix, 0)

    def block(i, unused):
        rows = pl.ds(pl.multiple_of(i * BLOCK, BLOCK), BLOCK)
        low = tab_ref[base + i]
        zeros = jnp.zeros((3 * BLOCK, PAD), WIDE)
        key_left = stack_heads(key_ref[rows, :])
        value_right = stack_heads(value_ref[rows, :])

        def visit(c, state):
            key_accum, value_accum = state
            spot = pl.ds(pl.multiple_of(low * BLOCK + c * CHUNK, BLOCK), CHUNK)
            queries = query_ref[spot, :]
            outgrads = grad_ref[spot, :]
            probs = jnp.exp(dot_nt(key_left, queries))
            slopes = (probs * dot_nt(value_right, outgrads)).astype(LOW)
            value_accum = value_accum + dot_nn(probs.astype(LOW), outgrads)
            key_accum = key_accum + dot_nn(slopes, queries)
            return key_accum, value_accum

        key_accum, value_accum = lax.fori_loop(0, tab_ref[base + 4 + i], visit, (zeros, zeros))
        out_ref[rows, pl.ds(0, PAD)] = pick_heads(key_accum).astype(LOW)
        out_ref[rows, pl.ds(PAD, PAD)] = pick_heads(value_accum).astype(LOW)
        return unused

    lax.fori_loop(0, 4, block, 0)
    share = DELTA_LANE
    lines = share // n
    many = first_ref.shape[0]
    dkv = out_ref[...]
    columns = [dq_ref[:, :share], dkv[:, :share], dkv[:, PAD : PAD + share]]
    grad_all = jnp.concatenate([dq_ref[...], dkv], axis=1)

    def turned(left, right):
        return lax.dot_general(
            left, right, (((0,), (0,)), ((), ())), preferred_element_type=WIDE
        )

    grad = turned(first_ref[...], grad_all[:many]) + turned(last_ref[...], grad_all[many:])
    for i in range(3):
        column = grad[:, i * PAD : i * PAD + share].astype(LOW)
        for place in range(n):
            for group in range(4):
                row = group * share + place * lines
                late_ref[
                    place, pl.ds(group * lines, lines), pl.ds(i * share, share)
                ] = column[row : row + lines]
    side = side_ref[...]
    for place in range(n):
        for group in range(4):
            late_ref[place, pl.ds(group * lines, lines), pl.ds(3 * share, share)] = side[
                place * lines : (place + 1) * lines, group * share : (group + 1) * share
            ]
    few = vector_rows(n)
    rows = jnp.concatenate(
        [
            jnp.sum(sums_ref[...].astype(WIDE), axis=0)[0:10],
            jnp.sum(columns[0].astype(WIDE), axis=0, keepdims=True),
            jnp.sum(columns[2].astype(WIDE), axis=0, keepdims=True),
            jnp.zeros((few * n - 12, share), WIDE),
        ],
        axis=0,
    ).astype(LOW)
    for place in range(n):
        late_ref[place, pl.ds(4 * lines, 16), :] = jnp.zeros((16, late_ref.shape[2]), LOW)
        late_ref[place, pl.ds(4 * lines, few), pl.ds(0, share)] = rows[
            place * few : (place + 1) * few
        ]


def assemble_kernel(n, layout, tab_ref, *refs):
    pieces = refs[:n]
    outs = refs[n:]
    for i, piece in enumerate(pieces):
        chunk = tab_ref[i]
        for out_ref, (first, rows, blocks) in zip(outs, layout):
            wide = out_ref.shape[2] // blocks
            for j in range(blocks):
                out_ref[chunk, :, pl.ds(j * wide, wide)] = piece[
                    pl.ds(first + j * rows, rows), :
                ].astype(WIDE)


def lasting(micros):
    return pl.CostEstimate(flops=0, transcendentals=0, bytes_accessed=int(micros * 3_000_000))


def whole_spec():
    return pl.BlockSpec(memory_space=pltpu.VMEM)


def any_spec():
    return pl.BlockSpec(memory_space=pl.ANY)


def smem_spec():
    return pl.BlockSpec(memory_space=pltpu.SMEM)


PARAMS = pltpu.CompilerParams(vmem_limit_bytes=60 << 20)


def attend(tab, seq_rows, matrix, add, output_rows, token_pieces, tokens_all):
    pieces = len(token_pieces)

    def kernel(*refs):
        attend_kernel(pieces, tokens_all, *refs)

    packed = jax.ShapeDtypeStruct((tokens_all + CHUNK, PAD), LOW)
    width = output_rows.shape[1]
    return pl.pallas_call(
        kernel,
        name="attend",
        cost_estimate=lasting(18),
        out_shape=(
            jax.ShapeDtypeStruct((4 * BLOCK, PAD), WIDE),
            jax.ShapeDtypeStruct((4 * BLOCK, PAD), LOW),
            jax.ShapeDtypeStruct((2 * BLOCK, width), WIDE),
            jax.ShapeDtypeStruct((2 * BLOCK, width), LOW),
            packed,
            packed,
            packed,
        ),
        in_specs=[smem_spec()] + [whole_spec()] * 4 + [any_spec()] * pieces,
        out_specs=(whole_spec(),) * 4 + (any_spec(),) * 3,
        scratch_shapes=[pltpu.VMEM((tokens_all, matrix.shape[0]), LOW)]
        + [pltpu.VMEM((tokens_all + CHUNK, PAD), LOW)] * 3
        + [pltpu.SemaphoreType.DMA((pieces,)), pltpu.SemaphoreType.DMA((3,))],
        compiler_params=PARAMS,
    )(tab, seq_rows, matrix, add, output_rows, *token_pieces)


def query_back(tab, outgrad, queries, keys, values, tokens_all):
    def kernel(*refs):
        query_back_kernel(tokens_all, *refs)

    return pl.pallas_call(
        kernel,
        name="query_back",
        cost_estimate=lasting(11),
        out_shape=jax.ShapeDtypeStruct((4 * BLOCK, PAD), LOW),
        in_specs=[smem_spec(), whole_spec(), any_spec(), whole_spec(), whole_spec()],
        out_specs=whole_spec(),
        scratch_shapes=[pltpu.VMEM((4 * BLOCK, PAD), LOW), pltpu.SemaphoreType.DMA((1,))],
        compiler_params=PARAMS,
    )(tab, outgrad, queries, keys, values)


def key_back(tab, token_pieces, grad_query, side, sums, grad_pieces, packed, tokens_all):
    pieces = len(grad_pieces)
    n = tokens_all // (4 * BLOCK)
    width = token_pieces[0].shape[1]

    def kernel(*refs):
        key_back_kernel(pieces, n, tokens_all, *refs)

    return pl.pallas_call(
        kernel,
        name="key_back",
        cost_estimate=lasting(16),
        out_shape=(
            jax.ShapeDtypeStruct((4 * BLOCK, 2 * PAD), LOW),
            jax.ShapeDtypeStruct((n, width // n + 16, width), LOW),
        ),
        in_specs=[smem_spec()] + [whole_spec()] * 5 + [any_spec()] * (pieces + 3),
        out_specs=(whole_spec(), whole_spec()),
        scratch_shapes=[pltpu.VMEM((tokens_all + CHUNK, PAD), LOW)] * 2
        + [pltpu.VMEM((4 * BLOCK, PAD), LOW)] * 2
        + [pltpu.SemaphoreType.DMA((4,))],
        compiler_params=PARAMS,
    )(tab, *token_pieces, grad_query, side, sums, *grad_pieces, *packed)


def middle(places, tokens, mine, mate, other, cotangent, vectors, expands, reduces):
    rows, width = tokens.shape
    hidden = expands[0][0].shape[1]
    matrices = [part[0] for part in expands + reduces]
    expand_spots = [part[1:] for part in expands]
    reduce_spots = [part[1:] for part in reduces]

    def kernel(*refs):
        middle_kernel(expand_spots, reduce_spots, width // 4, *refs)

    return pl.pallas_call(
        kernel,
        name="middle",
        cost_estimate=lasting(11),
        out_shape=(
            jax.ShapeDtypeStruct((rows, width), LOW),
            jax.ShapeDtypeStruct((rows, width), WIDE),
            jax.ShapeDtypeStruct((rows, width), LOW),
            jax.ShapeDtypeStruct((4, 2 * rows + 16, hidden // 4), LOW),
            jax.ShapeDtypeStruct((2 * rows, width), LOW),
        ),
        in_specs=[smem_spec()] + [whole_spec()] * 9 + [any_spec()] * len(matrices),
        out_specs=(whole_spec(),) * 5,
        scratch_shapes=[
            pltpu.VMEM((width, hidden), LOW),
            pltpu.VMEM((hidden, width), LOW),
            pltpu.VMEM((rows, hidden), WIDE),
            pltpu.VMEM((16, width), WIDE),
            pltpu.VMEM((4,) + vectors[0].shape, WIDE),
            pltpu.SemaphoreType.DMA((len(matrices),)),
        ],
        compiler_params=PARAMS,
    )(places, tokens, mine, mate, other, cotangent, *vectors, *matrices)


def attend_outgrad(branch, matrix, attn):
    return pl.pallas_call(
        outgrad_kernel,
        name="outgrad",
        cost_estimate=lasting(3),
        out_shape=jax.ShapeDtypeStruct((4 * BLOCK, PAD), LOW),
        in_specs=[whole_spec()] * 3,
        out_specs=whole_spec(),
    )(branch, matrix, attn)


def assemble(chunks, pieces, layout, shapes):
    n = len(pieces)

    def kernel(*refs):
        assemble_kernel(n, layout, *refs)

    outs = pl.pallas_call(
        kernel,
        name="assemble",
        cost_estimate=lasting(4),
        out_shape=tuple(
            jax.ShapeDtypeStruct((n, shape[0] // n, shape[1]), WIDE) for shape in shapes
        ),
        in_specs=[smem_spec()] + [whole_spec()] * n,
        out_specs=tuple(whole_spec() for _ in shapes),
        compiler_params=PARAMS,
    )(chunks, *pieces)
    return [out.reshape(shape) for out, shape in zip(outs, shapes)]


class RingGather:
    def __init__(self, value, n, split=True):
        self.n, self.split, self.done = n, split, 0
        self.value = value
        self.last = (value, value)
        self.ahead, self.back = [], []

    def keep(self):
        if self.done:
            self.ahead.append(self.last[0])
            if self.done < self.n // 2:
                self.back.append(self.last[1])

    def step(self):
        self.keep()
        self.done += 1
        f, b = self.last
        rows = self.value.shape[0] // 2
        if self.done < self.n // 2:
            self.last = (ring_shift(f, self.n, 1), ring_shift(b, self.n, -1))
        elif self.split:
            parts = ring_shift(f[:rows], self.n, 1), ring_shift(b[rows:], self.n, -1)
            self.last = (jnp.concatenate(parts, axis=0),)
        else:
            self.last = (ring_shift(f, self.n, 1),)

    def pieces(self):
        self.keep()
        return [self.value] + self.ahead + self.back


class RingReduce:
    def __init__(self, local, rank, n):
        self.local, self.rank, self.n, self.done = local, rank, n, 0
        self.last = None

    def part(self, step):
        return lax.dynamic_index_in_dim(
            self.local, (self.rank + step) % self.n, 0, keepdims=False
        )

    def step(self):
        half = self.n // 2
        if self.done == 0:
            f, b = self.part(half), self.part(1 - half)
        else:
            f, b = self.last
            f = (f.astype(WIDE) + self.part(half - self.done).astype(WIDE)).astype(LOW)
            if self.done < half - 1:
                b = (b.astype(WIDE) + self.part(1 - half + self.done).astype(WIDE)).astype(LOW)
        f = ring_shift(f, self.n, 1)
        if self.done < half - 1:
            b = ring_shift(b, self.n, -1)
        self.last = (f, b)
        self.done += 1

    def total(self):
        f, b = self.last
        return f.astype(WIDE) + b.astype(WIDE) + self.part(0).astype(WIDE)


def pad_group(block):
    return jnp.pad(block, ((0, 0), (0, PAD - block.shape[1])))


def on_device(
    n,
    tokens,
    block_order,
    seq_lengths,
    cotangent,
    query_matrix,
    key_matrix,
    value_matrix,
    output_matrix,
    expand_matrix,
    reduce_matrix,
    query_bias,
    value_bias,
    output_bias,
    expand_bias,
    reduce_bias,
    first_gain,
    first_shift,
    second_gain,
    second_shift,
):
    w = lax.axis_index("wsh")
    c = lax.axis_index("ctx")
    barrier = lax.optimization_barrier
    order = ring_of(n)
    rank = jnp.asarray([order.index(i) for i in range(n)], jnp.int32)[c]
    width = tokens.shape[1]
    share = width // 4
    tokens_all = n * 4 * BLOCK

    other = wsh_swap(tokens, 2)
    both = jnp.concatenate([tokens, other], axis=0)
    (
        query_matrix,
        key_matrix,
        value_matrix,
        output_matrix,
        expand_matrix,
        reduce_matrix,
        output_bias,
        reduce_bias,
        expand_bias,
        first_gain,
        first_shift,
        second_gain,
        second_shift,
        other,
    ) = lax.optimization_barrier(
        (
            query_matrix,
            key_matrix,
            value_matrix,
            output_matrix,
            expand_matrix,
            reduce_matrix,
            output_bias,
            reduce_bias,
            expand_bias,
            first_gain,
            first_shift,
            second_gain,
            second_shift,
            other,
        )
    )

    def columns(matrix, group):
        low = matrix.astype(LOW)
        return [group(low[:, i * share : (i + 1) * share]) for i in range(4)]

    qkv_blocks = jnp.stack(
        [
            jnp.concatenate(parts, axis=1)
            for parts in zip(
                columns(query_matrix, pad_group),
                columns(key_matrix, pad_group),
                columns(value_matrix, pad_group),
            )
        ]
    )
    def deal(blocks):
        return lax.all_to_all(blocks, "wsh", 0, 0).reshape(-1, blocks.shape[2])

    qkv_matrix = deal(qkv_blocks)
    vectors = jnp.stack(
        [output_bias, reduce_bias, first_gain, first_shift, second_gain, second_shift]
    )
    vectors = jnp.concatenate([vectors, expand_bias.reshape(4, share)], axis=0).astype(LOW)
    nothing = jnp.zeros((PAD,), LOW)
    fill = jnp.zeros((PAD - share,), LOW)
    qkv_add = jnp.concatenate(
        [query_bias.astype(LOW), fill, nothing, value_bias.astype(LOW), fill]
    ).astype(WIDE)[None, :]
    output_low = output_matrix.astype(LOW)
    output_rows = jnp.pad(output_low, ((0, PAD - share), (0, 0)))

    ends = jnp.cumsum(seq_lengths)
    steps = jnp.asarray(slot_steps(n), jnp.int32)
    from_ctx = jnp.asarray(order, jnp.int32)[(rank + steps) % n]
    blocks = (from_ctx[:, None] * 4 + (w ^ jnp.asarray(ORDER, jnp.int32))[None, :]).reshape(-1)
    places = block_order[blocks]
    first = places[:4] * BLOCK
    low = jnp.max(jnp.where(ends[None, :] <= first[:, None], ends[None, :], 0), axis=1)
    last = first + BLOCK - 1
    high = jnp.min(jnp.where(ends[None, :] > last[:, None], ends[None, :], tokens_all), axis=1)
    low_block = low // BLOCK
    count = (high - low_block * BLOCK + CHUNK - 1) // CHUNK
    tab = jnp.concatenate([places, low_block, count]).astype(jnp.int32)
    seqs = seq_lengths.shape[0]
    seq_rows = jnp.pad(
        jnp.stack([ends - seq_lengths, ends]), ((0, 6), (SEQ_LANE, PAD - SEQ_LANE - seqs))
    ).astype(jnp.int32)

    expand_low, reduce_low = expand_matrix.astype(LOW), reduce_matrix.astype(LOW)
    middle_rows = reduce_matrix.shape[0] // 2
    side = c & 1
    reduce_half = lax.dynamic_slice_in_dim(reduce_low, side * middle_rows, middle_rows)
    ring = RingGather(both, n)
    half = n // 2
    for step in range(1, half + 1):
        ring.step()
        if step == 1:
            ring.last, vectors = barrier((ring.last, vectors))
            vector_pieces = [vectors] + [wsh_swap(vectors, j) for j in ORDER[1:]]
        elif step == 2:
            ready = (tab, seq_rows, qkv_add, output_rows, expand_low, reduce_low, reduce_half)
            ring.last, qkv_matrix, ready, vector_pieces = barrier(
                (ring.last, qkv_matrix, ready, vector_pieces)
            )
            tab, seq_rows, qkv_add, output_rows, expand_low, reduce_low, reduce_half = ready
            reduce_near = wsh_swap(reduce_half, 2)
        elif step == 3:
            ring.last, reduce_near = barrier((ring.last, reduce_near))
    reduce_far = exchange(reduce_near, "ctx", n, 1)
    expand_other = wsh_swap(expand_low, 2)
    token_pieces = []
    for piece in ring.pieces():
        token_pieces += [piece, wsh_swap(piece, 1)]
    expand_mate, reduce_mate = wsh_swap(expand_low, 1), wsh_swap(reduce_low, 1)
    reduce_last = [wsh_swap(reduce_near, 1)]
    attn, attended, keep, send, packed_queries, packed_keys, packed_values = attend(
        tab, seq_rows, qkv_matrix, qkv_add, output_rows, token_pieces, tokens_all
    )
    from_mate = wsh_swap(send, 1)
    branch_sum = (keep[BLOCK:] + from_mate[BLOCK:].astype(WIDE)).astype(LOW)
    from_other = wsh_swap(branch_sum, 2)
    expand_other, reduce_far, unused = barrier((expand_other, reduce_far, from_mate))
    reduce_last += [wsh_swap(reduce_far, 1)]
    expand_parts = [
        (expand_low, 0, 0),
        (expand_mate, 2, 0),
        (expand_other, 1, 0),
        (wsh_swap(expand_other, 1), 3, 0),
    ]
    reduce_parts = [(reduce_low, 0, 0), (reduce_mate, 2, 0)]
    for i, part in enumerate((reduce_near, reduce_far)):
        reduce_parts += [(part, 1, (4 + i,)), (reduce_last[i], 3, (4 + i,))]
    group = jnp.concatenate(
        [
            (w ^ jnp.asarray(ORDER, jnp.int32)).astype(jnp.int32),
            jnp.stack([side, 1 - side]).astype(jnp.int32) * middle_rows,
        ]
    )
    layer_out, grad_hidden, branch_in, pair, lows = middle(
        group,
        tokens,
        keep,
        from_mate,
        from_other,
        cotangent,
        vector_pieces,
        expand_parts,
        reduce_parts,
    )
    branch_pieces = group_pieces(branch_in)
    branch_all = jnp.concatenate(branch_pieces, axis=0)
    outgrad = attend_outgrad(branch_all, output_rows, attn)
    grad_output = lax.dot_general(
        attended[:, :share], branch_all, (((0,), (0,)), ((), ())), preferred_element_type=WIDE
    ).astype(LOW)

    def rows_dot(left, right):
        return lax.dot_general(
            left, right, (((0,), (0,)), ((), ())), preferred_element_type=WIDE
        ).astype(LOW)

    def redeal(chunk):
        lines = chunk.shape[0] // 4
        return lax.all_to_all(chunk.astype(LOW).reshape(4, lines, -1), "wsh", 0, 0)

    def by_place(matrix):
        cols = matrix.shape[1]
        return matrix.reshape(4, n, share // n, cols).transpose(1, 0, 2, 3).reshape(n, -1, cols)

    def joined(dealt, first):
        return jnp.concatenate([dealt[i, :, first : first + share] for i in range(4)], axis=1)

    shard = reduce_matrix.shape[0]
    lines = share // n
    pair, lows, branch_pieces[1] = barrier((pair, lows, branch_pieces[1]))
    pair = lax.all_to_all(pair, "wsh", 0, 0)
    lows = [lows, wsh_swap(lows, 2)]
    grad_ring = RingGather(outgrad, n, split=False)
    grad_ring.step()
    grad_ring.last, outgrad, grad_output = barrier((grad_ring.last, outgrad, grad_output))
    grad_ring.step()
    grad_query = query_back(tab, outgrad, packed_queries, packed_keys, packed_values, tokens_all)
    grad_ring.last, grad_query, pair, lows = barrier((grad_ring.last, grad_query, pair, lows))
    lows = to_absolute([lows[0], wsh_swap(lows[0], 1), lows[1], wsh_swap(lows[1], 1)], w)
    reduce_all = jnp.concatenate([low[:BLOCK] for low in lows], axis=0)
    normed_all = jnp.concatenate([low[BLOCK:] for low in lows], axis=0)
    grad_reduce = rows_dot(pair[:, :BLOCK].reshape(4 * BLOCK, -1), reduce_all)
    grad_expand = rows_dot(normed_all, pair[:, BLOCK : 2 * BLOCK].reshape(4 * BLOCK, -1))
    sums = pair[:, 2 * BLOCK :, :share]
    early = jnp.concatenate(
        [grad_reduce.reshape(n, shard // n, width), by_place(grad_expand)], axis=1
    )
    grad_ring.step()
    grad_ring.last, early, sums = barrier((grad_ring.last, early, sums))
    for step in range(3, half):
        grad_ring.step()
        grad_ring.last, sums = barrier((grad_ring.last, sums))

    early_ring = RingReduce(early, rank, n)
    early_ring.step()
    grad_kv, late = key_back(
        tab,
        token_pieces[:2],
        grad_query,
        grad_output,
        sums,
        grad_ring.pieces(),
        (packed_queries, packed_keys, packed_values),
        tokens_all,
    )
    early_ring.last, grad_kv, late = barrier((early_ring.last, grad_kv, late))
    late_ring = RingReduce(late, rank, n)
    for step in range(1, half):
        late_ring.step()
        early_ring.step()
        late_ring.last, early_ring.last = barrier((late_ring.last, early_ring.last))
    late_ring.step()
    early = early_ring.total()
    early = jnp.concatenate(
        [early[: shard // n].astype(LOW), redeal(early[shard // n :]).reshape(4 * lines, width)],
        axis=0,
    )
    late_ring.last, early = barrier((late_ring.last, early))

    early_gather = RingGather(early, n, split=False)
    early_gather.step()
    late = late_ring.total()
    extra = late[4 * lines :].astype(LOW)
    own_output = late[: 4 * lines, 3 * share :].astype(LOW).reshape(4, lines, share)
    dealt = redeal(late[: 4 * lines, : 3 * share])
    late = jnp.concatenate(
        [joined(dealt, i * share) for i in range(3)] + [joined(own_output, 0), extra], axis=0
    )
    late, early_gather.last = barrier((late, early_gather.last))
    chunks = (rank + steps) % n
    late_gather = RingGather(late, n, split=False)
    for step in range(1, half):
        late_gather.step()
        early_gather.step()
        late_gather.last, early_gather.last = barrier((late_gather.last, early_gather.last))
    late_gather.step()
    out_reduce, out_expand = assemble(
        chunks,
        early_gather.pieces(),
        ((0, shard // n, 1), (shard // n, lines, 4)),
        ((shard, width), (share, 4 * width)),
    )
    late_gather.last, out_reduce, out_expand = barrier((late_gather.last, out_reduce, out_expand))
    tokens_grad = (
        scatter_group(
            dot_nt(grad_query, qkv_matrix[:, :PAD]) + dot_nt(grad_kv, qkv_matrix[:, PAD:])
        )
        + grad_hidden
    ).astype(LOW)
    out_query, out_key, out_value, out_output, small = assemble(
        chunks,
        late_gather.pieces(),
        tuple((i * lines, lines, 1) for i in range(4)) + ((4 * lines, 8, 1),),
        ((share, width),) * 4 + ((8 * n, width),),
    )
    small = small.reshape(n, 8, width)[:, : vector_rows(n), :share].reshape(-1, share)
    out_expand_bias = small[6:10].reshape(-1)
    return (
        layer_out,
        tokens_grad,
        out_query,
        out_key,
        out_value,
        out_output,
        out_expand,
        out_reduce,
        small[10],
        small[11],
        small[4],
        out_expand_bias,
        small[5],
        small[0],
        small[1],
        small[2],
        small[3],
    )


def solution(mesh):
    n = mesh.shape["ctx"]
    rows = P(("ctx", "wsh"), None)
    in_specs = (rows, P(), P(), rows) + (P("wsh", None),) * 6 + (P("wsh"),) * 9
    out_specs = (rows, rows) + (P("wsh", None),) * 6 + (P("wsh"),) * 9

    def run(*args):
        return on_device(n, *args)

    return jax.shard_map(run, mesh=mesh, in_specs=in_specs, out_specs=out_specs, check_vma=False)
```

```python
import math

import jax
import jax.numpy as jnp
from jax import lax
from jax.experimental import pallas as pl
from jax.experimental.pallas import tpu as pltpu
from jax.sharding import PartitionSpec as P

HDIM = 64
BLOCK = 128
EPSILON = 1e-12
LOW = jnp.bfloat16
WIDE = jnp.float32

ORDER = (0, 2, 1, 3)

PAD = 256
DELTA_LANE = 192
LSE_LANE = 201
SEQ_LANE = 216
BIG = 1e30
CHUNK = 1024
REST = 256


def ring_of(n):
    return list(range(0, n, 2)) + list(range(n - 1, 0, -2))


def exchange(value, axis, size, flip):
    return lax.ppermute(value, axis, [(i, i ^ flip) for i in range(size)])


def wsh_swap(value, flip):
    return exchange(value, "wsh", 4, flip)


def to_absolute(pieces, w):
    one = (w & 1) == 1
    two = (w & 2) == 2
    a = [jnp.where(one, pieces[j ^ 1], pieces[j]) for j in range(4)]
    return [jnp.where(two, a[j ^ 2], a[j]) for j in range(4)]


def group_pieces(value):
    other = wsh_swap(value, 2)
    return [value, other, wsh_swap(value, 1), wsh_swap(other, 1)]


def scatter_group(parts):
    rows = parts.shape[0] // 4
    mine, other, mate, last = [parts[i * rows : (i + 1) * rows] for i in range(4)]
    got = wsh_swap(jnp.concatenate([mate, last], axis=0).astype(LOW), 1).astype(WIDE)
    mine = mine + got[:rows]
    other = other + got[rows:]
    return mine + wsh_swap(other.astype(LOW), 2).astype(WIDE)


def ring_shift(value, n, step):
    ring = ring_of(n)
    return lax.ppermute(value, "ctx", [(ring[i], ring[(i + step) % n]) for i in range(n)])


def ring_gather(value, n, split=True, tie=None):
    half = n // 2
    rows = value.shape[0]
    ahead, back = [], []
    f = b = value
    tied = None
    for step in range(1, half + 1):
        if tie is not None and step == tie[0]:
            f, b, tied = lax.optimization_barrier((f, b, tie[1]))
        if step < half:
            f = ring_shift(f, n, 1)
            b = ring_shift(b, n, -1)
            ahead.append(f)
            back.append(b)
        elif not split:
            ahead.append(ring_shift(f, n, 1))
        else:
            first = ring_shift(f[: rows // 2], n, 1)
            second = ring_shift(b[rows // 2 :], n, -1)
            ahead.append(jnp.concatenate([first, second], axis=0))
    pieces = [value] + ahead + back
    return pieces if tie is None else (pieces, tied)


def slot_steps(n):
    half = n // 2
    return [0] + [-s for s in range(1, half + 1)] + list(range(1, half))


def lanes_of(head, lane):
    keep = (lane >= head * HDIM) & (lane < (head + 1) * HDIM)
    return keep


def stack_heads(value):
    lane = lax.broadcasted_iota(jnp.int32, value.shape, 1)
    out = []
    for head in range(3):
        keep = (
            lanes_of(head, lane)
            | ((lane >= DELTA_LANE + 3 * head) & (lane < DELTA_LANE + 3 * head + 3))
            | ((lane >= LSE_LANE + 3 * head) & (lane < LSE_LANE + 3 * head + 3))
            | (lane >= SEQ_LANE)
        )
        out.append(jnp.where(keep, value, jnp.zeros_like(value)))
    return jnp.concatenate(out, axis=0)


def pick_heads(value):
    lane = lax.broadcasted_iota(jnp.int32, (BLOCK, PAD), 1)
    total = jnp.zeros((BLOCK, PAD), WIDE)
    for head in range(3):
        total = jnp.where(lanes_of(head, lane), value[head * BLOCK : (head + 1) * BLOCK], total)
    return total


def dot_nt(a, b):
    return lax.dot_general(a, b, (((1,), (1,)), ((), ())), preferred_element_type=WIDE)


def dot_nn(a, b):
    return jnp.dot(a, b, preferred_element_type=WIDE)


def over_chunks(low, count, visit, state):
    large, small = CHUNK // BLOCK, REST // BLOCK

    def at(first, size):
        return pl.ds(pl.multiple_of(first * BLOCK, BLOCK), size)

    whole = count // large
    state = lax.fori_loop(
        0, whole, lambda c, now: visit(at(low + c * large, CHUNK), now), state
    )
    first = low + whole * large
    rest = (count - whole * large + small - 1) // small
    return lax.fori_loop(0, rest, lambda c, now: visit(at(first + c * small, REST), now), state)


def seq_marks(seq_ref, place):
    spot = place * BLOCK + lax.broadcasted_iota(jnp.int32, (BLOCK, PAD), 0)
    return (spot >= seq_ref[0:1, :]) & (spot < seq_ref[1:2, :])


def key_lanes(seq_ref, place, value):
    lane = lax.broadcasted_iota(jnp.int32, (BLOCK, PAD), 1)
    marks = seq_marks(seq_ref, place)
    minus = (lane >= LSE_LANE) & (lane < LSE_LANE + 9)
    out = jnp.where(minus, -1.0, value.astype(WIDE))
    return jnp.where((lane >= SEQ_LANE) & ~marks, -BIG, out).astype(LOW)


def query_lanes(seq_ref, place, value):
    return jnp.where(seq_marks(seq_ref, place), 1.0, value.astype(WIDE)).astype(LOW)


def value_lanes(value):
    lane = lax.broadcasted_iota(jnp.int32, (BLOCK, PAD), 1)
    minus = (lane >= DELTA_LANE) & (lane < DELTA_LANE + 9)
    return jnp.where(minus, -1.0, value.astype(WIDE)).astype(LOW)


def parts_of(column):
    high = column.astype(LOW).astype(WIDE)
    rest = column - high
    mid = rest.astype(LOW).astype(WIDE)
    return high, mid, (rest - mid).astype(LOW).astype(WIDE)


def end_rows(seq_value):
    lane = lax.broadcasted_iota(jnp.int32, (CHUNK, PAD), 1)
    return jnp.where(lane >= SEQ_LANE, seq_value, 0.0).astype(LOW)


def attend_kernel(pieces, tokens_all, tab_ref, seq_ref, matrix_ref, add_ref, output_ref, *refs):
    tokens = refs[:pieces]
    (
        out_ref,
        low_ref,
        keep_ref,
        send_ref,
        query_out,
        key_out,
        value_out,
        token_ref,
        query_ref,
        key_ref,
        value_ref,
        token_sems,
        sems,
    ) = refs[pieces:]
    per = tokens[0].shape[0] // BLOCK
    many = tokens[0].shape[0]
    copies = [
        pltpu.make_async_copy(tokens[i], token_ref.at[pl.ds(i * many, many)], token_sems.at[i])
        for i in range(pieces)
    ]
    for copy in copies:
        copy.start()
    base = tokens_all // BLOCK
    rest = pl.ds(tokens_all, CHUNK)
    key_ref[rest, :] = end_rows(-BIG)
    query_ref[rest, :] = end_rows(1.0)
    value_ref[rest, :] = jnp.zeros((CHUNK, PAD), LOW)

    def project(i, unused):
        rows = pl.ds(pl.multiple_of(i * 2 * many, BLOCK), 2 * many)
        for j in range(2):
            spot = token_ref.at[pl.ds(pl.multiple_of((i * 2 + j) * many, BLOCK), many)]
            pltpu.make_async_copy(spot, spot, token_sems.at[i * 2 + j]).wait()
        wide = dot_nn(token_ref[rows, :], matrix_ref[...]) + add_ref[...]
        low = wide.astype(LOW)
        for j in range(2 * per):
            place = tab_ref[i * 2 * per + j]
            spot = pl.ds(pl.multiple_of(place * BLOCK, BLOCK), BLOCK)
            block = low[j * BLOCK : (j + 1) * BLOCK]
            query = block[:, :PAD].astype(WIDE) * HDIM ** (-0.5)
            query_ref[spot, :] = query_lanes(seq_ref, place, query)
            key_ref[spot, :] = key_lanes(seq_ref, place, block[:, PAD : 2 * PAD])
            value_ref[spot, :] = value_lanes(block[:, 2 * PAD :])
        return unused

    lax.fori_loop(0, pieces // 2, project, 0)
    stores = [
        pltpu.make_async_copy(source, target, sems.at[i])
        for i, (source, target) in enumerate(
            ((query_ref, query_out), (key_ref, key_out), (value_ref, value_out))
        )
    ]
    for store in stores:
        store.start()
    lane = lax.broadcasted_iota(jnp.int32, (BLOCK, PAD), 1)

    def block(i, unused):
        rows = pl.ds(pl.multiple_of(i * BLOCK, BLOCK), BLOCK)
        own = pl.ds(pl.multiple_of(tab_ref[i] * BLOCK, BLOCK), BLOCK)
        low = tab_ref[base + i]
        count = tab_ref[base + 4 + i]
        queries = stack_heads(query_ref[own, :])

        def visit(spot, state):
            top, total, accum = state
            scores = dot_nt(queries, key_ref[spot, :])
            top_new = jnp.maximum(top, jnp.max(scores, axis=1, keepdims=True))
            weights = jnp.exp(scores - top_new)
            factor = jnp.exp(top - top_new)
            total = total * factor + jnp.sum(weights, axis=1, keepdims=True)
            accum = accum * factor + dot_nn(weights.astype(LOW), value_ref[spot, :])
            return top_new, total, accum

        top, total, accum = over_chunks(
            low,
            count,
            visit,
            (
                jnp.full((3 * BLOCK, 1), -2 * BIG, WIDE),
                jnp.zeros((3 * BLOCK, 1), WIDE),
                jnp.zeros((3 * BLOCK, PAD), WIDE),
            ),
        )
        result = pick_heads(accum / total)
        logsum = top + jnp.log(total)
        for head in range(3):
            result = jnp.where(
                lane == DELTA_LANE + head, logsum[head * BLOCK : (head + 1) * BLOCK], result
            )
        out_ref[rows, :] = result
        return unused

    lax.fori_loop(0, 4, block, 0)
    low = out_ref[...].astype(LOW)
    low_ref[...] = low
    half = 2 * BLOCK
    keep_ref[...] = dot_nn(low[:half], output_ref[...])
    send_ref[...] = dot_nn(low[half:], output_ref[...]).astype(LOW)
    for store in stores:
        store.wait()


def row_mean(values):
    return jnp.sum(values, axis=1, keepdims=True) * (1.0 / values.shape[1])


def norm_parts(values):
    centred = values - row_mean(values)
    scale = lax.rsqrt(row_mean(centred * centred) + EPSILON)
    return centred * scale, scale


def norm_back(upstream, normal, scale):
    return scale * (upstream - row_mean(upstream) - normal * row_mean(upstream * normal))


def middle_kernel(
    expand_spots,
    reduce_spots,
    share,
    place_ref,
    tokens_ref,
    mine_ref,
    mate_ref,
    other_ref,
    cotangent_ref,
    *refs,
):
    parts = len(expand_spots)
    vectors, refs = refs[:4], refs[4:]
    matrices = refs[: parts + len(reduce_spots)]
    (
        layer_ref,
        hidden_grad_ref,
        branch_ref,
        pair_ref,
        low_ref,
        expand_ref,
        reduce_ref,
        slope_ref,
        sums_ref,
        vector_ref,
        sems,
    ) = refs[len(matrices) :]
    copies = []
    for i, (part, (index, first)) in enumerate(zip(matrices, expand_spots + reduce_spots)):
        target, rows = (expand_ref, share) if i < parts else (reduce_ref, reduce_ref.shape[0] // 4)
        if isinstance(first, tuple):
            first = place_ref[first[0]]
        spot = pl.ds(pl.multiple_of(place_ref[index] * rows + first, 8), part.shape[0])
        copies.append(pltpu.make_async_copy(part, target.at[spot], sems.at[i]))
    for copy in copies:
        copy.start()
    for i, piece in enumerate(vectors):
        vector_ref[place_ref[i]] = piece[...].astype(WIDE)
    by_device = [vector_ref[j] for j in range(4)]
    output_add, reduce_add, first_scale, first_move, second_scale, second_move = [
        jnp.concatenate([rows[i : i + 1] for rows in by_device], axis=1) for i in range(6)
    ]
    expand_add = [
        jnp.concatenate([rows[i : i + 1] for i in range(6, 10)], axis=1) for rows in by_device
    ]
    own = pl.ds(0, BLOCK)
    branch = mine_ref[own, :] + mate_ref[own, :].astype(WIDE) + other_ref[...].astype(WIDE)
    hidden = tokens_ref[...].astype(WIDE) + (branch + output_add)
    first_normal, first_rate = norm_parts(hidden)
    normed = first_normal * first_scale + first_move
    normed_low = normed.astype(LOW)
    low_ref[pl.ds(BLOCK, BLOCK), :] = normed_low
    for copy in copies[:parts]:
        copy.wait()
    width = normed.shape[1]
    reduced = jnp.zeros(normed.shape, WIDE)
    for j in range(4):
        cols = pl.ds(j * width, width)
        expanded = dot_nn(normed_low, expand_ref[:, cols]) + expand_add[j]
        phi_cdf = 0.5 * (1.0 + lax.erf(expanded * (2.0**-0.5)))
        slope_ref[:, cols] = phi_cdf + expanded * (
            jnp.exp(-0.5 * expanded * expanded) * (2.0 * math.pi) ** -0.5
        )
        activated = (expanded * phi_cdf).astype(LOW)
        pair_ref[j, pl.ds(0, BLOCK), :] = activated
        if j == 0:
            for copy in copies[parts:]:
                copy.wait()
        reduced = reduced + dot_nn(activated, reduce_ref[cols, :])
    summed = normed + (reduced + reduce_add)
    second_normal, second_rate = norm_parts(summed)
    layer_ref[...] = (second_normal * second_scale + second_move).astype(LOW)
    upstream = cotangent_ref[...].astype(WIDE)

    def column_sum(row, values):
        sums_ref[row : row + 1, :] = jnp.sum(values, axis=0, keepdims=True)

    column_sum(2, upstream * second_normal)
    column_sum(3, upstream)
    grad_summed = norm_back(upstream * second_scale, second_normal, second_rate)
    reduce_in = grad_summed.astype(LOW)
    low_ref[pl.ds(0, BLOCK), :] = reduce_in
    column_sum(5, reduce_in.astype(WIDE))
    grad_normed = grad_summed
    for j in range(4):
        cols = pl.ds(j * width, width)
        expand_in = (dot_nt(reduce_in, reduce_ref[cols, :]) * slope_ref[:, cols]).astype(LOW)
        pair_ref[j, pl.ds(BLOCK, BLOCK), :] = expand_in
        column_sum(6 + j, expand_in.astype(WIDE))
        grad_normed = grad_normed + dot_nt(expand_in, expand_ref[:, cols])
    column_sum(0, grad_normed * first_normal)
    column_sum(1, grad_normed)
    grad_hidden = norm_back(grad_normed * first_scale, first_normal, first_rate)
    hidden_grad_ref[...] = grad_hidden
    branch_in = grad_hidden.astype(LOW)
    branch_ref[...] = branch_in
    column_sum(4, branch_in.astype(WIDE))
    for j in range(4):
        rows = [sums_ref[0:6, j * share : (j + 1) * share]]
        rows += [sums_ref[6 + j : 7 + j, k * share : (k + 1) * share] for k in range(4)]
        rows = jnp.concatenate(rows + [jnp.zeros((6, share), WIDE)], axis=0)
        pair_ref[j, pl.ds(2 * BLOCK, 16), :] = jnp.zeros((16, width), LOW)
        pair_ref[j, pl.ds(2 * BLOCK, 16), pl.ds(0, share)] = rows.astype(LOW)


def outgrad_kernel(branch_ref, matrix_ref, attn_ref, out_ref):
    grad = dot_nt(branch_ref[...], matrix_ref[...]).astype(LOW).astype(WIDE)
    attn = attn_ref[...]
    lane = lax.broadcasted_iota(jnp.int32, grad.shape, 1)
    product = grad * attn
    out = jnp.where(lane < DELTA_LANE, grad, 0.0)
    for head in range(3):
        delta = jnp.sum(jnp.where(lanes_of(head, lane), product, 0.0), axis=1, keepdims=True)
        logsum = jnp.sum(jnp.where(lane == DELTA_LANE + head, attn, 0.0), axis=1, keepdims=True)
        for first, column in ((DELTA_LANE, delta), (LSE_LANE, logsum)):
            for i, part in enumerate(parts_of(column)):
                out = jnp.where(lane == first + 3 * head + i, part, out)
    out_ref[...] = out.astype(LOW)


def lse_lanes(query, outgrad):
    lane = lax.broadcasted_iota(jnp.int32, query.shape, 1)
    return jnp.where((lane >= LSE_LANE) & (lane < LSE_LANE + 9), outgrad, query)


def own_blocks(tab_ref, packed, target, sem):
    for i in range(4):
        own = pl.ds(pl.multiple_of(tab_ref[i] * BLOCK, BLOCK), BLOCK)
        pltpu.make_async_copy(packed.at[own], target.at[pl.ds(i * BLOCK, BLOCK)], sem).start()


def own_wait(target, sem):
    pltpu.make_async_copy(target, target, sem).wait()


def query_back_kernel(
    tokens_all, tab_ref, grad_ref, query_all, key_ref, value_ref, out_ref, own_ref, sems
):
    own_blocks(tab_ref, query_all, own_ref, sems.at[0])
    base = tokens_all // BLOCK
    own_wait(own_ref, sems.at[0])

    def block(i, unused):
        rows = pl.ds(pl.multiple_of(i * BLOCK, BLOCK), BLOCK)
        low = tab_ref[base + i]
        outgrad = grad_ref[rows, :]
        left = stack_heads(lse_lanes(own_ref[rows, :], outgrad))
        right = stack_heads(outgrad)

        def visit(spot, accum):
            keys = key_ref[spot, :]
            probs = jnp.exp(dot_nt(left, keys))
            slopes = (probs * dot_nt(right, value_ref[spot, :])).astype(LOW)
            return accum + dot_nn(slopes, keys)

        accum = over_chunks(
            low, tab_ref[base + 4 + i], visit, jnp.zeros((3 * BLOCK, PAD), WIDE)
        )
        out_ref[rows, :] = (pick_heads(accum) * HDIM ** (-0.5)).astype(LOW)
        return unused

    lax.fori_loop(0, 4, block, 0)


def vector_rows(n):
    return max(1, 16 // n)


def key_back_kernel(pieces, n, tokens_all, tab_ref, first_ref, last_ref, dq_ref, side_ref, sums_ref, *refs):
    grads = refs[:pieces]
    (
        query_all,
        key_all,
        value_all,
        out_ref,
        late_ref,
        ahead_ref,
        behind_ref,
        query_ref,
        grad_ref,
        key_ref,
        value_ref,
        sems,
    ) = refs[pieces:]
    query_copy = pltpu.make_async_copy(query_all, query_ref, sems.at[0])
    query_copy.start()
    for i, array in enumerate(grads):
        for j in range(4):
            place = pl.multiple_of(tab_ref[i * 4 + j] * BLOCK, BLOCK)
            pltpu.make_async_copy(
                array.at[pl.ds(j * BLOCK, BLOCK)], grad_ref.at[pl.ds(place, BLOCK)], sems.at[1]
            ).start()
    own_blocks(tab_ref, key_all, key_ref, sems.at[2])
    own_blocks(tab_ref, value_all, value_ref, sems.at[3])
    base = tokens_all // BLOCK
    grad_ref[pl.ds(tokens_all, CHUNK), :] = jnp.zeros((CHUNK, PAD), LOW)
    query_copy.wait()
    whole = grad_ref.at[pl.ds(0, tokens_all)]
    pltpu.make_async_copy(whole, whole, sems.at[1]).wait()
    own_wait(key_ref, sems.at[2])
    own_wait(value_ref, sems.at[3])

    def fix(place, unused):
        rows = pl.ds(pl.multiple_of(place * BLOCK, BLOCK), BLOCK)
        query_ref[rows, :] = lse_lanes(query_ref[rows, :], grad_ref[rows, :])
        return unused

    lax.fori_loop(0, base, fix, 0)

    def block(i, unused):
        rows = pl.ds(pl.multiple_of(i * BLOCK, BLOCK), BLOCK)
        low = tab_ref[base + i]
        zeros = jnp.zeros((3 * BLOCK, PAD), WIDE)
        key_left = stack_heads(key_ref[rows, :])
        value_right = stack_heads(value_ref[rows, :])

        def visit(spot, state):
            key_accum, value_accum = state
            queries = query_ref[spot, :]
            outgrads = grad_ref[spot, :]
            probs = jnp.exp(dot_nt(key_left, queries))
            slopes = (probs * dot_nt(value_right, outgrads)).astype(LOW)
            value_accum = value_accum + dot_nn(probs.astype(LOW), outgrads)
            key_accum = key_accum + dot_nn(slopes, queries)
            return key_accum, value_accum

        key_accum, value_accum = over_chunks(
            low, tab_ref[base + 4 + i], visit, (zeros, zeros)
        )
        out_ref[rows, pl.ds(0, PAD)] = pick_heads(key_accum).astype(LOW)
        out_ref[rows, pl.ds(PAD, PAD)] = pick_heads(value_accum).astype(LOW)
        return unused

    lax.fori_loop(0, 4, block, 0)
    share = DELTA_LANE
    lines = share // n
    many = first_ref.shape[0]
    dkv = out_ref[...]
    columns = [dq_ref[:, :share], dkv[:, :share], dkv[:, PAD : PAD + share]]
    grad_all = jnp.concatenate([dq_ref[...], dkv], axis=1)

    def turned(left, right):
        return lax.dot_general(
            left, right, (((0,), (0,)), ((), ())), preferred_element_type=WIDE
        )

    grad = turned(first_ref[...], grad_all[:many]) + turned(last_ref[...], grad_all[many:])
    for i in range(3):
        column = grad[:, i * PAD : i * PAD + share].astype(LOW)
        for place in range(n):
            for group in range(4):
                row = group * share + place * lines
                late_ref[
                    place, pl.ds(group * lines, lines), pl.ds(i * share, share)
                ] = column[row : row + lines]
    side = side_ref[...]
    for place in range(n):
        for group in range(4):
            late_ref[place, pl.ds(group * lines, lines), pl.ds(3 * share, share)] = side[
                place * lines : (place + 1) * lines, group * share : (group + 1) * share
            ]
    few = vector_rows(n)
    rows = jnp.concatenate(
        [
            jnp.sum(sums_ref[...].astype(WIDE), axis=0)[0:10],
            jnp.sum(columns[0].astype(WIDE), axis=0, keepdims=True),
            jnp.sum(columns[2].astype(WIDE), axis=0, keepdims=True),
            jnp.zeros((few * n - 12, share), WIDE),
        ],
        axis=0,
    ).astype(LOW)
    for place in range(n):
        late_ref[place, pl.ds(4 * lines, 16), :] = jnp.zeros((16, late_ref.shape[2]), LOW)
        late_ref[place, pl.ds(4 * lines, few), pl.ds(0, share)] = rows[
            place * few : (place + 1) * few
        ]
    ahead_ref[...] = late_ref[tab_ref[base + 8]]
    behind_ref[...] = late_ref[tab_ref[base + 9]]


def assemble_kernel(n, layout, tab_ref, *refs):
    pieces = refs[:n]
    outs = refs[n:]
    for i, piece in enumerate(pieces):
        chunk = tab_ref[i]
        for out_ref, (first, rows, blocks) in zip(outs, layout):
            wide = out_ref.shape[2] // blocks
            for j in range(blocks):
                out_ref[chunk, :, pl.ds(j * wide, wide)] = piece[
                    pl.ds(first + j * rows, rows), :
                ].astype(WIDE)


def lasting(micros):
    return pl.CostEstimate(flops=0, transcendentals=0, bytes_accessed=int(micros * 3_000_000))


def whole_spec():
    return pl.BlockSpec(memory_space=pltpu.VMEM)


def any_spec():
    return pl.BlockSpec(memory_space=pl.ANY)


def smem_spec():
    return pl.BlockSpec(memory_space=pltpu.SMEM)


PARAMS = pltpu.CompilerParams(vmem_limit_bytes=60 << 20)


def attend(tab, seq_rows, matrix, add, output_rows, token_pieces, tokens_all):
    pieces = len(token_pieces)

    def kernel(*refs):
        attend_kernel(pieces, tokens_all, *refs)

    packed = jax.ShapeDtypeStruct((tokens_all + CHUNK, PAD), LOW)
    width = output_rows.shape[1]
    return pl.pallas_call(
        kernel,
        name="attend",
        cost_estimate=lasting(18),
        out_shape=(
            jax.ShapeDtypeStruct((4 * BLOCK, PAD), WIDE),
            jax.ShapeDtypeStruct((4 * BLOCK, PAD), LOW),
            jax.ShapeDtypeStruct((2 * BLOCK, width), WIDE),
            jax.ShapeDtypeStruct((2 * BLOCK, width), LOW),
            packed,
            packed,
            packed,
        ),
        in_specs=[smem_spec()] + [whole_spec()] * 4 + [any_spec()] * pieces,
        out_specs=(whole_spec(),) * 4 + (any_spec(),) * 3,
        scratch_shapes=[pltpu.VMEM((tokens_all, matrix.shape[0]), LOW)]
        + [pltpu.VMEM((tokens_all + CHUNK, PAD), LOW)] * 3
        + [pltpu.SemaphoreType.DMA((pieces,)), pltpu.SemaphoreType.DMA((3,))],
        compiler_params=PARAMS,
    )(tab, seq_rows, matrix, add, output_rows, *token_pieces)


def query_back(tab, outgrad, queries, keys, values, tokens_all):
    def kernel(*refs):
        query_back_kernel(tokens_all, *refs)

    return pl.pallas_call(
        kernel,
        name="query_back",
        cost_estimate=lasting(11),
        out_shape=jax.ShapeDtypeStruct((4 * BLOCK, PAD), LOW),
        in_specs=[smem_spec(), whole_spec(), any_spec(), whole_spec(), whole_spec()],
        out_specs=whole_spec(),
        scratch_shapes=[pltpu.VMEM((4 * BLOCK, PAD), LOW), pltpu.SemaphoreType.DMA((1,))],
        compiler_params=PARAMS,
    )(tab, outgrad, queries, keys, values)


def key_back(tab, token_pieces, grad_query, side, sums, grad_pieces, packed, tokens_all):
    pieces = len(grad_pieces)
    n = tokens_all // (4 * BLOCK)
    width = token_pieces[0].shape[1]

    def kernel(*refs):
        key_back_kernel(pieces, n, tokens_all, *refs)

    return pl.pallas_call(
        kernel,
        name="key_back",
        cost_estimate=lasting(16),
        out_shape=(
            jax.ShapeDtypeStruct((4 * BLOCK, 2 * PAD), LOW),
            jax.ShapeDtypeStruct((n, width // n + 16, width), LOW),
            jax.ShapeDtypeStruct((width // n + 16, width), LOW),
            jax.ShapeDtypeStruct((width // n + 16, width), LOW),
        ),
        in_specs=[smem_spec()] + [whole_spec()] * 5 + [any_spec()] * (pieces + 3),
        out_specs=(whole_spec(),) * 4,
        scratch_shapes=[pltpu.VMEM((tokens_all + CHUNK, PAD), LOW)] * 2
        + [pltpu.VMEM((4 * BLOCK, PAD), LOW)] * 2
        + [pltpu.SemaphoreType.DMA((4,))],
        compiler_params=PARAMS,
    )(tab, *token_pieces, grad_query, side, sums, *grad_pieces, *packed)


def middle(places, tokens, mine, mate, other, cotangent, vectors, expands, reduces):
    rows, width = tokens.shape
    hidden = expands[0][0].shape[1]
    matrices = [part[0] for part in expands + reduces]
    expand_spots = [part[1:] for part in expands]
    reduce_spots = [part[1:] for part in reduces]

    def kernel(*refs):
        middle_kernel(expand_spots, reduce_spots, width // 4, *refs)

    return pl.pallas_call(
        kernel,
        name="middle",
        cost_estimate=lasting(11),
        out_shape=(
            jax.ShapeDtypeStruct((rows, width), LOW),
            jax.ShapeDtypeStruct((rows, width), WIDE),
            jax.ShapeDtypeStruct((rows, width), LOW),
            jax.ShapeDtypeStruct((4, 2 * rows + 16, hidden // 4), LOW),
            jax.ShapeDtypeStruct((2 * rows, width), LOW),
        ),
        in_specs=[smem_spec()] + [whole_spec()] * 9 + [any_spec()] * len(matrices),
        out_specs=(whole_spec(),) * 5,
        scratch_shapes=[
            pltpu.VMEM((width, hidden), LOW),
            pltpu.VMEM((hidden, width), LOW),
            pltpu.VMEM((rows, hidden), WIDE),
            pltpu.VMEM((16, width), WIDE),
            pltpu.VMEM((4,) + vectors[0].shape, WIDE),
            pltpu.SemaphoreType.DMA((len(matrices),)),
        ],
        compiler_params=PARAMS,
    )(places, tokens, mine, mate, other, cotangent, *vectors, *matrices)


def attend_outgrad(branch, matrix, attn):
    return pl.pallas_call(
        outgrad_kernel,
        name="outgrad",
        cost_estimate=lasting(3),
        out_shape=jax.ShapeDtypeStruct((4 * BLOCK, PAD), LOW),
        in_specs=[whole_spec()] * 3,
        out_specs=whole_spec(),
    )(branch, matrix, attn)


def assemble(chunks, pieces, layout, shapes):
    n = len(pieces)

    def kernel(*refs):
        assemble_kernel(n, layout, *refs)

    outs = pl.pallas_call(
        kernel,
        name="assemble",
        cost_estimate=lasting(4),
        out_shape=tuple(
            jax.ShapeDtypeStruct((n, shape[0] // n, shape[1]), WIDE) for shape in shapes
        ),
        in_specs=[smem_spec()] + [whole_spec()] * n,
        out_specs=tuple(whole_spec() for _ in shapes),
        compiler_params=PARAMS,
    )(chunks, *pieces)
    return [out.reshape(shape) for out, shape in zip(outs, shapes)]


class RingGather:
    def __init__(self, value, n, split=True):
        self.n, self.split, self.done = n, split, 0
        self.value = value
        self.last = (value, value)
        self.ahead, self.back = [], []

    def keep(self):
        if self.done:
            self.ahead.append(self.last[0])
            if self.done < self.n // 2:
                self.back.append(self.last[1])

    def step(self):
        self.keep()
        self.done += 1
        f, b = self.last
        rows = self.value.shape[0] // 2
        if self.done < self.n // 2:
            self.last = (ring_shift(f, self.n, 1), ring_shift(b, self.n, -1))
        elif self.split:
            parts = ring_shift(f[:rows], self.n, 1), ring_shift(b[rows:], self.n, -1)
            self.last = (jnp.concatenate(parts, axis=0),)
        else:
            self.last = (ring_shift(f, self.n, 1),)

    def pieces(self):
        self.keep()
        return [self.value] + self.ahead + self.back


class RingReduce:
    def __init__(self, local, rank, n, first=None):
        self.local, self.rank, self.n, self.done = local, rank, n, 0
        self.first, self.last = first, None

    def part(self, step):
        return lax.dynamic_index_in_dim(
            self.local, (self.rank + step) % self.n, 0, keepdims=False
        )

    def step(self):
        half = self.n // 2
        if self.done == 0:
            f, b = self.first or (self.part(half), self.part(1 - half))
        else:
            f, b = self.last
            f = (f.astype(WIDE) + self.part(half - self.done).astype(WIDE)).astype(LOW)
            if self.done < half - 1:
                b = (b.astype(WIDE) + self.part(1 - half + self.done).astype(WIDE)).astype(LOW)
        f = ring_shift(f, self.n, 1)
        if self.done < half - 1:
            b = ring_shift(b, self.n, -1)
        self.last = (f, b)
        self.done += 1

    def total(self):
        f, b = self.last
        return f.astype(WIDE) + b.astype(WIDE) + self.part(0).astype(WIDE)


def pad_group(block):
    return jnp.pad(block, ((0, 0), (0, PAD - block.shape[1])))


def on_device(
    n,
    tokens,
    block_order,
    seq_lengths,
    cotangent,
    query_matrix,
    key_matrix,
    value_matrix,
    output_matrix,
    expand_matrix,
    reduce_matrix,
    query_bias,
    value_bias,
    output_bias,
    expand_bias,
    reduce_bias,
    first_gain,
    first_shift,
    second_gain,
    second_shift,
):
    w = lax.axis_index("wsh")
    c = lax.axis_index("ctx")
    barrier = lax.optimization_barrier
    order = ring_of(n)
    rank = jnp.asarray([order.index(i) for i in range(n)], jnp.int32)[c]
    width = tokens.shape[1]
    share = width // 4
    tokens_all = n * 4 * BLOCK

    other = wsh_swap(tokens, 2)
    both = jnp.concatenate([tokens, other], axis=0)
    (
        query_matrix,
        key_matrix,
        value_matrix,
        output_matrix,
        expand_matrix,
        reduce_matrix,
        output_bias,
        reduce_bias,
        expand_bias,
        first_gain,
        first_shift,
        second_gain,
        second_shift,
        other,
    ) = lax.optimization_barrier(
        (
            query_matrix,
            key_matrix,
            value_matrix,
            output_matrix,
            expand_matrix,
            reduce_matrix,
            output_bias,
            reduce_bias,
            expand_bias,
            first_gain,
            first_shift,
            second_gain,
            second_shift,
            other,
        )
    )

    def columns(matrix, group):
        low = matrix.astype(LOW)
        return [group(low[:, i * share : (i + 1) * share]) for i in range(4)]

    qkv_blocks = jnp.stack(
        [
            jnp.concatenate(parts, axis=1)
            for parts in zip(
                columns(query_matrix, pad_group),
                columns(key_matrix, pad_group),
                columns(value_matrix, pad_group),
            )
        ]
    )
    def deal(blocks):
        return lax.all_to_all(blocks, "wsh", 0, 0).reshape(-1, blocks.shape[2])

    qkv_matrix = deal(qkv_blocks)
    vectors = jnp.stack(
        [output_bias, reduce_bias, first_gain, first_shift, second_gain, second_shift]
    )
    vectors = jnp.concatenate([vectors, expand_bias.reshape(4, share)], axis=0).astype(LOW)
    nothing = jnp.zeros((PAD,), LOW)
    fill = jnp.zeros((PAD - share,), LOW)
    qkv_add = jnp.concatenate(
        [query_bias.astype(LOW), fill, nothing, value_bias.astype(LOW), fill]
    ).astype(WIDE)[None, :]
    output_low = output_matrix.astype(LOW)
    output_rows = jnp.pad(output_low, ((0, PAD - share), (0, 0)))

    ends = jnp.cumsum(seq_lengths)
    steps = jnp.asarray(slot_steps(n), jnp.int32)
    from_ctx = jnp.asarray(order, jnp.int32)[(rank + steps) % n]
    blocks = (from_ctx[:, None] * 4 + (w ^ jnp.asarray(ORDER, jnp.int32))[None, :]).reshape(-1)
    places = block_order[blocks]
    first = places[:4] * BLOCK
    low = jnp.max(jnp.where(ends[None, :] <= first[:, None], ends[None, :], 0), axis=1)
    last = first + BLOCK - 1
    high = jnp.min(jnp.where(ends[None, :] > last[:, None], ends[None, :], tokens_all), axis=1)
    low_block = low // BLOCK
    count = (high - low_block * BLOCK + BLOCK - 1) // BLOCK
    sends = (rank + jnp.asarray([n // 2, 1 - n // 2], jnp.int32)) % n
    tab = jnp.concatenate([places, low_block, count, sends]).astype(jnp.int32)
    seqs = seq_lengths.shape[0]
    seq_rows = jnp.pad(
        jnp.stack([ends - seq_lengths, ends]), ((0, 6), (SEQ_LANE, PAD - SEQ_LANE - seqs))
    ).astype(jnp.int32)

    expand_low, reduce_low = expand_matrix.astype(LOW), reduce_matrix.astype(LOW)
    middle_rows = reduce_matrix.shape[0] // 2
    side = c & 1
    reduce_half = lax.dynamic_slice_in_dim(reduce_low, side * middle_rows, middle_rows)
    ring = RingGather(both, n)
    half = n // 2
    for step in range(1, half + 1):
        ring.step()
        if step == 1:
            ring.last, vectors = barrier((ring.last, vectors))
            vector_pieces = [vectors] + [wsh_swap(vectors, j) for j in ORDER[1:]]
        elif step == 2:
            ready = (tab, seq_rows, qkv_add, output_rows, expand_low, reduce_low, reduce_half)
            ring.last, qkv_matrix, ready, vector_pieces = barrier(
                (ring.last, qkv_matrix, ready, vector_pieces)
            )
            tab, seq_rows, qkv_add, output_rows, expand_low, reduce_low, reduce_half = ready
            reduce_near = wsh_swap(reduce_half, 2)
        elif step == 3:
            ring.last, reduce_near = barrier((ring.last, reduce_near))
    reduce_far = exchange(reduce_near, "ctx", n, 1)
    expand_other = wsh_swap(expand_low, 2)
    token_pieces = []
    for piece in ring.pieces():
        token_pieces += [piece, wsh_swap(piece, 1)]
    expand_mate, reduce_mate = wsh_swap(expand_low, 1), wsh_swap(reduce_low, 1)
    reduce_last = [wsh_swap(reduce_near, 1)]
    attn, attended, keep, send, packed_queries, packed_keys, packed_values = attend(
        tab, seq_rows, qkv_matrix, qkv_add, output_rows, token_pieces, tokens_all
    )
    from_mate = wsh_swap(send, 1)
    branch_sum = (keep[BLOCK:] + from_mate[BLOCK:].astype(WIDE)).astype(LOW)
    from_other = wsh_swap(branch_sum, 2)
    expand_other, reduce_far, unused = barrier((expand_other, reduce_far, from_mate))
    reduce_last += [wsh_swap(reduce_far, 1)]
    expand_parts = [
        (expand_low, 0, 0),
        (expand_mate, 2, 0),
        (expand_other, 1, 0),
        (wsh_swap(expand_other, 1), 3, 0),
    ]
    reduce_parts = [(reduce_low, 0, 0), (reduce_mate, 2, 0)]
    for i, part in enumerate((reduce_near, reduce_far)):
        reduce_parts += [(part, 1, (4 + i,)), (reduce_last[i], 3, (4 + i,))]
    group = jnp.concatenate(
        [
            (w ^ jnp.asarray(ORDER, jnp.int32)).astype(jnp.int32),
            jnp.stack([side, 1 - side]).astype(jnp.int32) * middle_rows,
        ]
    )
    layer_out, grad_hidden, branch_in, pair, lows = middle(
        group,
        tokens,
        keep,
        from_mate,
        from_other,
        cotangent,
        vector_pieces,
        expand_parts,
        reduce_parts,
    )
    branch_pieces = group_pieces(branch_in)
    branch_all = jnp.concatenate(branch_pieces, axis=0)
    outgrad = attend_outgrad(branch_all, output_rows, attn)
    grad_output = lax.dot_general(
        attended[:, :share], branch_all, (((0,), (0,)), ((), ())), preferred_element_type=WIDE
    ).astype(LOW)

    def rows_dot(left, right):
        return lax.dot_general(
            left, right, (((0,), (0,)), ((), ())), preferred_element_type=WIDE
        ).astype(LOW)

    def redeal(chunk):
        lines = chunk.shape[0] // 4
        return lax.all_to_all(chunk.astype(LOW).reshape(4, lines, -1), "wsh", 0, 0)

    def by_place(matrix):
        cols = matrix.shape[1]
        return matrix.reshape(4, n, share // n, cols).transpose(1, 0, 2, 3).reshape(n, -1, cols)

    def joined(dealt, first):
        return jnp.concatenate([dealt[i, :, first : first + share] for i in range(4)], axis=1)

    shard = reduce_matrix.shape[0]
    lines = share // n
    pair, lows, outgrad = barrier((pair, lows, outgrad))
    pair = lax.all_to_all(pair, "wsh", 0, 0)
    lows = [lows, wsh_swap(lows, 2)]
    grad_ring = RingGather(outgrad, n, split=False)
    grad_ring.step()
    grad_ring.last, outgrad, grad_output = barrier((grad_ring.last, outgrad, grad_output))
    grad_ring.step()
    grad_query = query_back(tab, outgrad, packed_queries, packed_keys, packed_values, tokens_all)
    grad_ring.last, grad_query = barrier((grad_ring.last, grad_query))
    grad_ring.step()
    grad_ring.last, pair, lows = barrier((grad_ring.last, pair, lows))
    lows = to_absolute([lows[0], wsh_swap(lows[0], 1), lows[1], wsh_swap(lows[1], 1)], w)
    reduce_all = jnp.concatenate([low[:BLOCK] for low in lows], axis=0)
    normed_all = jnp.concatenate([low[BLOCK:] for low in lows], axis=0)
    grad_reduce = rows_dot(pair[:, :BLOCK].reshape(4 * BLOCK, -1), reduce_all)
    grad_expand = rows_dot(normed_all, pair[:, BLOCK : 2 * BLOCK].reshape(4 * BLOCK, -1))
    sums = pair[:, 2 * BLOCK :, :share]
    early = jnp.concatenate(
        [grad_reduce.reshape(n, shard // n, width), by_place(grad_expand)], axis=1
    )
    for step in range(3, half):
        grad_ring.step()
        grad_ring.last, early, sums = barrier((grad_ring.last, early, sums))

    early_ring = RingReduce(early, rank, n)
    early_ring.step()
    grad_kv, late, ahead, behind = key_back(
        tab,
        token_pieces[:2],
        grad_query,
        grad_output,
        sums,
        grad_ring.pieces(),
        (packed_queries, packed_keys, packed_values),
        tokens_all,
    )
    early_ring.last, grad_kv, late, ahead, behind = barrier(
        (early_ring.last, grad_kv, late, ahead, behind)
    )
    late_ring = RingReduce(late, rank, n, (ahead, behind))
    for step in range(1, half):
        late_ring.step()
        early_ring.step()
        late_ring.last, early_ring.last = barrier((late_ring.last, early_ring.last))
    late_ring.step()
    early = early_ring.total()
    early = jnp.concatenate(
        [early[: shard // n].astype(LOW), redeal(early[shard // n :]).reshape(4 * lines, width)],
        axis=0,
    )
    late_ring.last, early = barrier((late_ring.last, early))

    early_gather = RingGather(early, n, split=False)
    early_gather.step()
    late = late_ring.total()
    extra = late[4 * lines :].astype(LOW)
    own_output = late[: 4 * lines, 3 * share :].astype(LOW).reshape(4, lines, share)
    dealt = redeal(late[: 4 * lines, : 3 * share])
    late = jnp.concatenate(
        [joined(dealt, i * share) for i in range(3)] + [joined(own_output, 0), extra], axis=0
    )
    chunks = (rank + steps) % n
    late_gather = RingGather(late, n, split=False)
    for step in range(1, half):
        late_gather.step()
        early_gather.step()
        late_gather.last, early_gather.last = barrier((late_gather.last, early_gather.last))
    late_gather.step()
    out_reduce, out_expand = assemble(
        chunks,
        early_gather.pieces(),
        ((0, shard // n, 1), (shard // n, lines, 4)),
        ((shard, width), (share, 4 * width)),
    )
    late_gather.last, out_reduce, out_expand = barrier((late_gather.last, out_reduce, out_expand))
    tokens_grad = (
        scatter_group(
            dot_nt(grad_query, qkv_matrix[:, :PAD]) + dot_nt(grad_kv, qkv_matrix[:, PAD:])
        )
        + grad_hidden
    ).astype(LOW)
    out_query, out_key, out_value, out_output, small = assemble(
        chunks,
        late_gather.pieces(),
        tuple((i * lines, lines, 1) for i in range(4)) + ((4 * lines, 8, 1),),
        ((share, width),) * 4 + ((8 * n, width),),
    )
    small = small.reshape(n, 8, width)[:, : vector_rows(n), :share].reshape(-1, share)
    out_expand_bias = small[6:10].reshape(-1)
    return (
        layer_out,
        tokens_grad,
        out_query,
        out_key,
        out_value,
        out_output,
        out_expand,
        out_reduce,
        small[10],
        small[11],
        small[4],
        out_expand_bias,
        small[5],
        small[0],
        small[1],
        small[2],
        small[3],
    )


def solution(mesh):
    n = mesh.shape["ctx"]
    rows = P(("ctx", "wsh"), None)
    in_specs = (rows, P(), P(), rows) + (P("wsh", None),) * 6 + (P("wsh"),) * 9
    out_specs = (rows, rows) + (P("wsh", None),) * 6 + (P("wsh"),) * 9

    def run(*args):
        return on_device(n, *args)

    return jax.shard_map(run, mesh=mesh, in_specs=in_specs, out_specs=out_specs, check_vma=False)
```

```python
import math

import jax
import jax.numpy as jnp
from jax import lax
from jax.experimental import pallas as pl
from jax.experimental.pallas import tpu as pltpu
from jax.sharding import PartitionSpec as P

HDIM = 64
BLOCK = 128
EPSILON = 1e-12
LOW = jnp.bfloat16
WIDE = jnp.float32

ORDER = (0, 2, 1, 3)

PAD = 256
DELTA_LANE = 192
LSE_LANE = 201
SEQ_LANE = 216
BIG = 1e30
CHUNK = 1024
REST = 256


def ring_of(n):
    return list(range(0, n, 2)) + list(range(n - 1, 0, -2))


def exchange(value, axis, size, flip):
    return lax.ppermute(value, axis, [(i, i ^ flip) for i in range(size)])


def wsh_swap(value, flip):
    return exchange(value, "wsh", 4, flip)


def to_absolute(pieces, w):
    one = (w & 1) == 1
    two = (w & 2) == 2
    a = [jnp.where(one, pieces[j ^ 1], pieces[j]) for j in range(4)]
    return [jnp.where(two, a[j ^ 2], a[j]) for j in range(4)]


def group_pieces(value):
    other = wsh_swap(value, 2)
    return [value, other, wsh_swap(value, 1), wsh_swap(other, 1)]


def scatter_group(parts):
    rows = parts.shape[0] // 4
    mine, other, mate, last = [parts[i * rows : (i + 1) * rows] for i in range(4)]
    got = wsh_swap(jnp.concatenate([mate, last], axis=0).astype(LOW), 1).astype(WIDE)
    mine = mine + got[:rows]
    other = other + got[rows:]
    return mine + wsh_swap(other.astype(LOW), 2).astype(WIDE)


def ring_shift(value, n, step):
    ring = ring_of(n)
    return lax.ppermute(value, "ctx", [(ring[i], ring[(i + step) % n]) for i in range(n)])


def ring_gather(value, n, split=True, tie=None):
    half = n // 2
    rows = value.shape[0]
    ahead, back = [], []
    f = b = value
    tied = None
    for step in range(1, half + 1):
        if tie is not None and step == tie[0]:
            f, b, tied = lax.optimization_barrier((f, b, tie[1]))
        if step < half:
            f = ring_shift(f, n, 1)
            b = ring_shift(b, n, -1)
            ahead.append(f)
            back.append(b)
        elif not split:
            ahead.append(ring_shift(f, n, 1))
        else:
            first = ring_shift(f[: rows // 2], n, 1)
            second = ring_shift(b[rows // 2 :], n, -1)
            ahead.append(jnp.concatenate([first, second], axis=0))
    pieces = [value] + ahead + back
    return pieces if tie is None else (pieces, tied)


def slot_steps(n):
    half = n // 2
    return [0] + [-s for s in range(1, half + 1)] + list(range(1, half))


def lanes_of(head, lane):
    keep = (lane >= head * HDIM) & (lane < (head + 1) * HDIM)
    return keep


def stack_heads(value):
    lane = lax.broadcasted_iota(jnp.int32, value.shape, 1)
    out = []
    for head in range(3):
        keep = (
            lanes_of(head, lane)
            | ((lane >= DELTA_LANE + 3 * head) & (lane < DELTA_LANE + 3 * head + 3))
            | ((lane >= LSE_LANE + 3 * head) & (lane < LSE_LANE + 3 * head + 3))
            | (lane >= SEQ_LANE)
        )
        out.append(jnp.where(keep, value, jnp.zeros_like(value)))
    return jnp.concatenate(out, axis=0)


def pick_heads(value):
    lane = lax.broadcasted_iota(jnp.int32, (BLOCK, PAD), 1)
    total = jnp.zeros((BLOCK, PAD), WIDE)
    for head in range(3):
        total = jnp.where(lanes_of(head, lane), value[head * BLOCK : (head + 1) * BLOCK], total)
    return total


def dot_nt(a, b):
    return lax.dot_general(a, b, (((1,), (1,)), ((), ())), preferred_element_type=WIDE)


def dot_nn(a, b):
    return jnp.dot(a, b, preferred_element_type=WIDE)


def over_chunks(low, count, visit, state):
    large, small = CHUNK // BLOCK, REST // BLOCK

    def at(first, size):
        return pl.ds(pl.multiple_of(first * BLOCK, BLOCK), size)

    whole = count // large
    state = lax.fori_loop(
        0, whole, lambda c, now: visit(at(low + c * large, CHUNK), now), state
    )
    first = low + whole * large
    rest = (count - whole * large + small - 1) // small
    return lax.fori_loop(0, rest, lambda c, now: visit(at(first + c * small, REST), now), state)


def seq_marks(seq_ref, place):
    spot = place * BLOCK + lax.broadcasted_iota(jnp.int32, (BLOCK, PAD), 0)
    return (spot >= seq_ref[0:1, :]) & (spot < seq_ref[1:2, :])


def key_lanes(seq_ref, place, value):
    lane = lax.broadcasted_iota(jnp.int32, (BLOCK, PAD), 1)
    marks = seq_marks(seq_ref, place)
    minus = (lane >= LSE_LANE) & (lane < LSE_LANE + 9)
    out = jnp.where(minus, -1.0, value.astype(WIDE))
    return jnp.where((lane >= SEQ_LANE) & ~marks, -BIG, out).astype(LOW)


def query_lanes(seq_ref, place, value):
    return jnp.where(seq_marks(seq_ref, place), 1.0, value.astype(WIDE)).astype(LOW)


def value_lanes(value):
    lane = lax.broadcasted_iota(jnp.int32, (BLOCK, PAD), 1)
    minus = (lane >= DELTA_LANE) & (lane < DELTA_LANE + 9)
    return jnp.where(minus, -1.0, value.astype(WIDE)).astype(LOW)


def parts_of(column):
    high = column.astype(LOW).astype(WIDE)
    rest = column - high
    mid = rest.astype(LOW).astype(WIDE)
    return high, mid, (rest - mid).astype(LOW).astype(WIDE)


def end_rows(seq_value):
    lane = lax.broadcasted_iota(jnp.int32, (CHUNK, PAD), 1)
    return jnp.where(lane >= SEQ_LANE, seq_value, 0.0).astype(LOW)


def attend_kernel(pieces, tokens_all, tab_ref, seq_ref, matrix_ref, add_ref, output_ref, *refs):
    tokens = refs[:pieces]
    (
        out_ref,
        low_ref,
        keep_ref,
        send_ref,
        query_out,
        key_out,
        value_out,
        token_ref,
        query_ref,
        key_ref,
        value_ref,
        token_sems,
        sems,
    ) = refs[pieces:]
    per = tokens[0].shape[0] // BLOCK
    many = tokens[0].shape[0]
    copies = [
        pltpu.make_async_copy(tokens[i], token_ref.at[pl.ds(i * many, many)], token_sems.at[i])
        for i in range(pieces)
    ]
    for copy in copies:
        copy.start()
    base = tokens_all // BLOCK
    rest = pl.ds(tokens_all, CHUNK)
    key_ref[rest, :] = end_rows(-BIG)
    query_ref[rest, :] = end_rows(1.0)
    value_ref[rest, :] = jnp.zeros((CHUNK, PAD), LOW)

    def project(i, unused):
        rows = pl.ds(pl.multiple_of(i * 2 * many, BLOCK), 2 * many)
        for j in range(2):
            spot = token_ref.at[pl.ds(pl.multiple_of((i * 2 + j) * many, BLOCK), many)]
            pltpu.make_async_copy(spot, spot, token_sems.at[i * 2 + j]).wait()
        wide = dot_nn(token_ref[rows, :], matrix_ref[...]) + add_ref[...]
        low = wide.astype(LOW)
        for j in range(2 * per):
            place = tab_ref[i * 2 * per + j]
            spot = pl.ds(pl.multiple_of(place * BLOCK, BLOCK), BLOCK)
            block = low[j * BLOCK : (j + 1) * BLOCK]
            query = block[:, :PAD].astype(WIDE) * HDIM ** (-0.5)
            query_ref[spot, :] = query_lanes(seq_ref, place, query)
            key_ref[spot, :] = key_lanes(seq_ref, place, block[:, PAD : 2 * PAD])
            value_ref[spot, :] = value_lanes(block[:, 2 * PAD :])
        return unused

    lax.fori_loop(0, pieces // 2, project, 0)
    stores = [
        pltpu.make_async_copy(source, target, sems.at[i])
        for i, (source, target) in enumerate(
            ((query_ref, query_out), (key_ref, key_out), (value_ref, value_out))
        )
    ]
    for store in stores:
        store.start()
    lane = lax.broadcasted_iota(jnp.int32, (BLOCK, PAD), 1)

    def block(i, unused):
        rows = pl.ds(pl.multiple_of(i * BLOCK, BLOCK), BLOCK)
        own = pl.ds(pl.multiple_of(tab_ref[i] * BLOCK, BLOCK), BLOCK)
        low = tab_ref[base + i]
        count = tab_ref[base + 4 + i]
        queries = stack_heads(query_ref[own, :])

        def visit(spot, state):
            top, total, accum = state
            scores = dot_nt(queries, key_ref[spot, :])
            top_new = jnp.maximum(top, jnp.max(scores, axis=1, keepdims=True))
            weights = jnp.exp(scores - top_new)
            factor = jnp.exp(top - top_new)
            total = total * factor + jnp.sum(weights, axis=1, keepdims=True)
            accum = accum * factor + dot_nn(weights.astype(LOW), value_ref[spot, :])
            return top_new, total, accum

        top, total, accum = over_chunks(
            low,
            count,
            visit,
            (
                jnp.full((3 * BLOCK, 1), -2 * BIG, WIDE),
                jnp.zeros((3 * BLOCK, 1), WIDE),
                jnp.zeros((3 * BLOCK, PAD), WIDE),
            ),
        )
        result = pick_heads(accum / total)
        logsum = top + jnp.log(total)
        for head in range(3):
            result = jnp.where(
                lane == DELTA_LANE + head, logsum[head * BLOCK : (head + 1) * BLOCK], result
            )
        out_ref[rows, :] = result
        return unused

    lax.fori_loop(0, 4, block, 0)
    low = out_ref[...].astype(LOW)
    low_ref[...] = low
    half = 2 * BLOCK
    keep_ref[...] = dot_nn(low[:half], output_ref[...])
    send_ref[...] = dot_nn(low[half:], output_ref[...]).astype(LOW)
    for store in stores:
        store.wait()


def row_mean(values):
    return jnp.sum(values, axis=1, keepdims=True) * (1.0 / values.shape[1])


def norm_parts(values):
    centred = values - row_mean(values)
    scale = lax.rsqrt(row_mean(centred * centred) + EPSILON)
    return centred * scale, scale


def norm_back(upstream, normal, scale):
    return scale * (upstream - row_mean(upstream) - normal * row_mean(upstream * normal))


def middle_kernel(
    expand_spots,
    reduce_spots,
    share,
    place_ref,
    tokens_ref,
    mine_ref,
    mate_ref,
    other_ref,
    cotangent_ref,
    *refs,
):
    parts = len(expand_spots)
    vectors, refs = refs[:4], refs[4:]
    matrices = refs[: parts + len(reduce_spots)]
    (
        layer_ref,
        hidden_grad_ref,
        branch_ref,
        pair_ref,
        low_ref,
        expand_ref,
        reduce_ref,
        slope_ref,
        sums_ref,
        vector_ref,
        sems,
    ) = refs[len(matrices) :]
    copies = []
    for i, (part, (index, first)) in enumerate(zip(matrices, expand_spots + reduce_spots)):
        target, rows = (expand_ref, share) if i < parts else (reduce_ref, reduce_ref.shape[0] // 4)
        if isinstance(first, tuple):
            first = place_ref[first[0]]
        spot = pl.ds(pl.multiple_of(place_ref[index] * rows + first, 8), part.shape[0])
        copies.append(pltpu.make_async_copy(part, target.at[spot], sems.at[i]))
    for copy in copies:
        copy.start()
    for i, piece in enumerate(vectors):
        vector_ref[place_ref[i]] = piece[...].astype(WIDE)
    by_device = [vector_ref[j] for j in range(4)]
    output_add, reduce_add, first_scale, first_move, second_scale, second_move = [
        jnp.concatenate([rows[i : i + 1] for rows in by_device], axis=1) for i in range(6)
    ]
    expand_add = [
        jnp.concatenate([rows[i : i + 1] for i in range(6, 10)], axis=1) for rows in by_device
    ]
    own = pl.ds(0, BLOCK)
    branch = mine_ref[own, :] + mate_ref[own, :].astype(WIDE) + other_ref[...].astype(WIDE)
    hidden = tokens_ref[...].astype(WIDE) + (branch + output_add)
    first_normal, first_rate = norm_parts(hidden)
    normed = first_normal * first_scale + first_move
    normed_low = normed.astype(LOW)
    low_ref[pl.ds(BLOCK, BLOCK), :] = normed_low
    for copy in copies[:parts]:
        copy.wait()
    width = normed.shape[1]
    reduced = jnp.zeros(normed.shape, WIDE)
    for j in range(4):
        cols = pl.ds(j * width, width)
        expanded = dot_nn(normed_low, expand_ref[:, cols]) + expand_add[j]
        phi_cdf = 0.5 * (1.0 + lax.erf(expanded * (2.0**-0.5)))
        slope_ref[:, cols] = phi_cdf + expanded * (
            jnp.exp(-0.5 * expanded * expanded) * (2.0 * math.pi) ** -0.5
        )
        activated = (expanded * phi_cdf).astype(LOW)
        pair_ref[j, pl.ds(0, BLOCK), :] = activated
        if j == 0:
            for copy in copies[parts:]:
                copy.wait()
        reduced = reduced + dot_nn(activated, reduce_ref[cols, :])
    summed = normed + (reduced + reduce_add)
    second_normal, second_rate = norm_parts(summed)
    layer_ref[...] = (second_normal * second_scale + second_move).astype(LOW)
    upstream = cotangent_ref[...].astype(WIDE)

    def column_sum(row, values):
        sums_ref[row : row + 1, :] = jnp.sum(values, axis=0, keepdims=True)

    column_sum(2, upstream * second_normal)
    column_sum(3, upstream)
    grad_summed = norm_back(upstream * second_scale, second_normal, second_rate)
    reduce_in = grad_summed.astype(LOW)
    low_ref[pl.ds(0, BLOCK), :] = reduce_in
    column_sum(5, reduce_in.astype(WIDE))
    grad_normed = grad_summed
    for j in range(4):
        cols = pl.ds(j * width, width)
        expand_in = (dot_nt(reduce_in, reduce_ref[cols, :]) * slope_ref[:, cols]).astype(LOW)
        pair_ref[j, pl.ds(BLOCK, BLOCK), :] = expand_in
        column_sum(6 + j, expand_in.astype(WIDE))
        grad_normed = grad_normed + dot_nt(expand_in, expand_ref[:, cols])
    column_sum(0, grad_normed * first_normal)
    column_sum(1, grad_normed)
    grad_hidden = norm_back(grad_normed * first_scale, first_normal, first_rate)
    hidden_grad_ref[...] = grad_hidden
    branch_in = grad_hidden.astype(LOW)
    branch_ref[...] = branch_in
    column_sum(4, branch_in.astype(WIDE))
    for j in range(4):
        rows = [sums_ref[0:6, j * share : (j + 1) * share]]
        rows += [sums_ref[6 + j : 7 + j, k * share : (k + 1) * share] for k in range(4)]
        rows = jnp.concatenate(rows + [jnp.zeros((6, share), WIDE)], axis=0)
        pair_ref[j, pl.ds(2 * BLOCK, 16), :] = jnp.zeros((16, width), LOW)
        pair_ref[j, pl.ds(2 * BLOCK, 16), pl.ds(0, share)] = rows.astype(LOW)


def outgrad_kernel(branch_ref, matrix_ref, attn_ref, out_ref):
    grad = dot_nt(branch_ref[...], matrix_ref[...]).astype(LOW).astype(WIDE)
    attn = attn_ref[...]
    lane = lax.broadcasted_iota(jnp.int32, grad.shape, 1)
    product = grad * attn
    out = jnp.where(lane < DELTA_LANE, grad, 0.0)
    for head in range(3):
        delta = jnp.sum(jnp.where(lanes_of(head, lane), product, 0.0), axis=1, keepdims=True)
        logsum = jnp.sum(jnp.where(lane == DELTA_LANE + head, attn, 0.0), axis=1, keepdims=True)
        for first, column in ((DELTA_LANE, delta), (LSE_LANE, logsum)):
            for i, part in enumerate(parts_of(column)):
                out = jnp.where(lane == first + 3 * head + i, part, out)
    out_ref[...] = out.astype(LOW)


def lse_lanes(query, outgrad):
    lane = lax.broadcasted_iota(jnp.int32, query.shape, 1)
    return jnp.where((lane >= LSE_LANE) & (lane < LSE_LANE + 9), outgrad, query)


def own_blocks(tab_ref, packed, target, sem):
    for i in range(4):
        own = pl.ds(pl.multiple_of(tab_ref[i] * BLOCK, BLOCK), BLOCK)
        pltpu.make_async_copy(packed.at[own], target.at[pl.ds(i * BLOCK, BLOCK)], sem).start()


def own_wait(target, sem):
    pltpu.make_async_copy(target, target, sem).wait()


def query_back_kernel(
    tokens_all, tab_ref, grad_ref, query_all, key_ref, value_ref, out_ref, own_ref, sems
):
    own_blocks(tab_ref, query_all, own_ref, sems.at[0])
    base = tokens_all // BLOCK
    own_wait(own_ref, sems.at[0])

    def block(i, unused):
        rows = pl.ds(pl.multiple_of(i * BLOCK, BLOCK), BLOCK)
        low = tab_ref[base + i]
        outgrad = grad_ref[rows, :]
        left = stack_heads(lse_lanes(own_ref[rows, :], outgrad))
        right = stack_heads(outgrad)

        def visit(spot, accum):
            keys = key_ref[spot, :]
            probs = jnp.exp(dot_nt(left, keys))
            slopes = (probs * dot_nt(right, value_ref[spot, :])).astype(LOW)
            return accum + dot_nn(slopes, keys)

        accum = over_chunks(
            low, tab_ref[base + 4 + i], visit, jnp.zeros((3 * BLOCK, PAD), WIDE)
        )
        out_ref[rows, :] = (pick_heads(accum) * HDIM ** (-0.5)).astype(LOW)
        return unused

    lax.fori_loop(0, 4, block, 0)


def vector_rows(n):
    return max(1, 16 // n)


def key_back_kernel(pieces, n, tokens_all, tab_ref, first_ref, last_ref, dq_ref, side_ref, sums_ref, *refs):
    grads = refs[:pieces]
    (
        query_all,
        key_all,
        value_all,
        out_ref,
        late_ref,
        ahead_ref,
        behind_ref,
        query_ref,
        grad_ref,
        key_ref,
        value_ref,
        sems,
    ) = refs[pieces:]
    query_copy = pltpu.make_async_copy(query_all, query_ref, sems.at[0])
    query_copy.start()
    for i, array in enumerate(grads):
        for j in range(4):
            place = pl.multiple_of(tab_ref[i * 4 + j] * BLOCK, BLOCK)
            pltpu.make_async_copy(
                array.at[pl.ds(j * BLOCK, BLOCK)], grad_ref.at[pl.ds(place, BLOCK)], sems.at[1]
            ).start()
    own_blocks(tab_ref, key_all, key_ref, sems.at[2])
    own_blocks(tab_ref, value_all, value_ref, sems.at[3])
    base = tokens_all // BLOCK
    grad_ref[pl.ds(tokens_all, CHUNK), :] = jnp.zeros((CHUNK, PAD), LOW)
    query_copy.wait()
    whole = grad_ref.at[pl.ds(0, tokens_all)]
    pltpu.make_async_copy(whole, whole, sems.at[1]).wait()
    own_wait(key_ref, sems.at[2])
    own_wait(value_ref, sems.at[3])

    def fix(place, unused):
        rows = pl.ds(pl.multiple_of(place * BLOCK, BLOCK), BLOCK)
        query_ref[rows, :] = lse_lanes(query_ref[rows, :], grad_ref[rows, :])
        return unused

    lax.fori_loop(0, base, fix, 0)

    def block(i, unused):
        rows = pl.ds(pl.multiple_of(i * BLOCK, BLOCK), BLOCK)
        low = tab_ref[base + i]
        zeros = jnp.zeros((3 * BLOCK, PAD), WIDE)
        key_left = stack_heads(key_ref[rows, :])
        value_right = stack_heads(value_ref[rows, :])

        def visit(spot, state):
            key_accum, value_accum = state
            queries = query_ref[spot, :]
            outgrads = grad_ref[spot, :]
            probs = jnp.exp(dot_nt(key_left, queries))
            slopes = (probs * dot_nt(value_right, outgrads)).astype(LOW)
            value_accum = value_accum + dot_nn(probs.astype(LOW), outgrads)
            key_accum = key_accum + dot_nn(slopes, queries)
            return key_accum, value_accum

        key_accum, value_accum = over_chunks(
            low, tab_ref[base + 4 + i], visit, (zeros, zeros)
        )
        out_ref[rows, pl.ds(0, PAD)] = pick_heads(key_accum).astype(LOW)
        out_ref[rows, pl.ds(PAD, PAD)] = pick_heads(value_accum).astype(LOW)
        return unused

    lax.fori_loop(0, 4, block, 0)
    share = DELTA_LANE
    lines = share // n
    many = first_ref.shape[0]
    dkv = out_ref[...]
    columns = [dq_ref[:, :share], dkv[:, :share], dkv[:, PAD : PAD + share]]
    grad_all = jnp.concatenate([dq_ref[...], dkv], axis=1)

    def turned(left, right):
        return lax.dot_general(
            left, right, (((0,), (0,)), ((), ())), preferred_element_type=WIDE
        )

    grad = turned(first_ref[...], grad_all[:many]) + turned(last_ref[...], grad_all[many:])
    for i in range(3):
        column = grad[:, i * PAD : i * PAD + share].astype(LOW)
        for place in range(n):
            for group in range(4):
                row = group * share + place * lines
                late_ref[
                    place, pl.ds(group * lines, lines), pl.ds(i * share, share)
                ] = column[row : row + lines]
    side = side_ref[...]
    for place in range(n):
        for group in range(4):
            late_ref[place, pl.ds(group * lines, lines), pl.ds(3 * share, share)] = side[
                place * lines : (place + 1) * lines, group * share : (group + 1) * share
            ]
    few = vector_rows(n)
    rows = jnp.concatenate(
        [
            jnp.sum(sums_ref[...].astype(WIDE), axis=0)[0:10],
            jnp.sum(columns[0].astype(WIDE), axis=0, keepdims=True),
            jnp.sum(columns[2].astype(WIDE), axis=0, keepdims=True),
            jnp.zeros((few * n - 12, share), WIDE),
        ],
        axis=0,
    ).astype(LOW)
    for place in range(n):
        late_ref[place, pl.ds(4 * lines, 16), :] = jnp.zeros((16, late_ref.shape[2]), LOW)
        late_ref[place, pl.ds(4 * lines, few), pl.ds(0, share)] = rows[
            place * few : (place + 1) * few
        ]
    ahead_ref[...] = late_ref[tab_ref[base + 8]]
    behind_ref[...] = late_ref[tab_ref[base + 9]]


def assemble_kernel(slots, layout, tab_ref, *refs):
    outs = refs[len(slots) :]
    for (i, start), piece in zip(slots, refs):
        chunk = tab_ref[i]
        for out_ref, (first, rows, blocks) in zip(outs, layout):
            wide = out_ref.shape[2] // blocks
            for j in range(blocks):
                at = first + j * rows - start
                if 0 <= at and at + rows <= piece.shape[0]:
                    out_ref[chunk, :, pl.ds(j * wide, wide)] = piece[pl.ds(at, rows), :].astype(WIDE)


def lasting(micros):
    return pl.CostEstimate(flops=0, transcendentals=0, bytes_accessed=int(micros * 3_000_000))


def whole_spec():
    return pl.BlockSpec(memory_space=pltpu.VMEM)


def any_spec():
    return pl.BlockSpec(memory_space=pl.ANY)


def smem_spec():
    return pl.BlockSpec(memory_space=pltpu.SMEM)


PARAMS = pltpu.CompilerParams(vmem_limit_bytes=60 << 20)


def attend(tab, seq_rows, matrix, add, output_rows, token_pieces, tokens_all):
    pieces = len(token_pieces)

    def kernel(*refs):
        attend_kernel(pieces, tokens_all, *refs)

    packed = jax.ShapeDtypeStruct((tokens_all + CHUNK, PAD), LOW)
    width = output_rows.shape[1]
    return pl.pallas_call(
        kernel,
        name="attend",
        cost_estimate=lasting(18),
        out_shape=(
            jax.ShapeDtypeStruct((4 * BLOCK, PAD), WIDE),
            jax.ShapeDtypeStruct((4 * BLOCK, PAD), LOW),
            jax.ShapeDtypeStruct((2 * BLOCK, width), WIDE),
            jax.ShapeDtypeStruct((2 * BLOCK, width), LOW),
            packed,
            packed,
            packed,
        ),
        in_specs=[smem_spec()] + [whole_spec()] * 4 + [any_spec()] * pieces,
        out_specs=(whole_spec(),) * 4 + (any_spec(),) * 3,
        scratch_shapes=[pltpu.VMEM((tokens_all, matrix.shape[0]), LOW)]
        + [pltpu.VMEM((tokens_all + CHUNK, PAD), LOW)] * 3
        + [pltpu.SemaphoreType.DMA((pieces,)), pltpu.SemaphoreType.DMA((3,))],
        compiler_params=PARAMS,
    )(tab, seq_rows, matrix, add, output_rows, *token_pieces)


def query_back(tab, outgrad, queries, keys, values, tokens_all):
    def kernel(*refs):
        query_back_kernel(tokens_all, *refs)

    return pl.pallas_call(
        kernel,
        name="query_back",
        cost_estimate=lasting(11),
        out_shape=jax.ShapeDtypeStruct((4 * BLOCK, PAD), LOW),
        in_specs=[smem_spec(), whole_spec(), any_spec(), whole_spec(), whole_spec()],
        out_specs=whole_spec(),
        scratch_shapes=[pltpu.VMEM((4 * BLOCK, PAD), LOW), pltpu.SemaphoreType.DMA((1,))],
        compiler_params=PARAMS,
    )(tab, outgrad, queries, keys, values)


def key_back(tab, token_pieces, grad_query, side, sums, grad_pieces, packed, tokens_all):
    pieces = len(grad_pieces)
    n = tokens_all // (4 * BLOCK)
    width = token_pieces[0].shape[1]

    def kernel(*refs):
        key_back_kernel(pieces, n, tokens_all, *refs)

    return pl.pallas_call(
        kernel,
        name="key_back",
        cost_estimate=lasting(16),
        out_shape=(
            jax.ShapeDtypeStruct((4 * BLOCK, 2 * PAD), LOW),
            jax.ShapeDtypeStruct((n, width // n + 16, width), LOW),
            jax.ShapeDtypeStruct((width // n + 16, width), LOW),
            jax.ShapeDtypeStruct((width // n + 16, width), LOW),
        ),
        in_specs=[smem_spec()] + [whole_spec()] * 5 + [any_spec()] * (pieces + 3),
        out_specs=(whole_spec(),) * 4,
        scratch_shapes=[pltpu.VMEM((tokens_all + CHUNK, PAD), LOW)] * 2
        + [pltpu.VMEM((4 * BLOCK, PAD), LOW)] * 2
        + [pltpu.SemaphoreType.DMA((4,))],
        compiler_params=PARAMS,
    )(tab, *token_pieces, grad_query, side, sums, *grad_pieces, *packed)


def middle(places, tokens, mine, mate, other, cotangent, vectors, expands, reduces):
    rows, width = tokens.shape
    hidden = expands[0][0].shape[1]
    matrices = [part[0] for part in expands + reduces]
    expand_spots = [part[1:] for part in expands]
    reduce_spots = [part[1:] for part in reduces]

    def kernel(*refs):
        middle_kernel(expand_spots, reduce_spots, width // 4, *refs)

    return pl.pallas_call(
        kernel,
        name="middle",
        cost_estimate=lasting(11),
        out_shape=(
            jax.ShapeDtypeStruct((rows, width), LOW),
            jax.ShapeDtypeStruct((rows, width), WIDE),
            jax.ShapeDtypeStruct((rows, width), LOW),
            jax.ShapeDtypeStruct((4, 2 * rows + 16, hidden // 4), LOW),
            jax.ShapeDtypeStruct((2 * rows, width), LOW),
        ),
        in_specs=[smem_spec()] + [whole_spec()] * 9 + [any_spec()] * len(matrices),
        out_specs=(whole_spec(),) * 5,
        scratch_shapes=[
            pltpu.VMEM((width, hidden), LOW),
            pltpu.VMEM((hidden, width), LOW),
            pltpu.VMEM((rows, hidden), WIDE),
            pltpu.VMEM((16, width), WIDE),
            pltpu.VMEM((4,) + vectors[0].shape, WIDE),
            pltpu.SemaphoreType.DMA((len(matrices),)),
        ],
        compiler_params=PARAMS,
    )(places, tokens, mine, mate, other, cotangent, *vectors, *matrices)


def attend_outgrad(branch, matrix, attn):
    return pl.pallas_call(
        outgrad_kernel,
        name="outgrad",
        cost_estimate=lasting(3),
        out_shape=jax.ShapeDtypeStruct((4 * BLOCK, PAD), LOW),
        in_specs=[whole_spec()] * 3,
        out_specs=whole_spec(),
    )(branch, matrix, attn)


def assemble(chunks, pieces, layout, shapes):
    n = len(pieces)
    slots, arrays = [], []
    for i, piece in enumerate(pieces):
        start = 0
        for part in piece if isinstance(piece, tuple) else (piece,):
            slots.append((i, start))
            arrays.append(part)
            start += part.shape[0]

    def kernel(*refs):
        assemble_kernel(slots, layout, *refs)

    outs = pl.pallas_call(
        kernel,
        name="assemble",
        cost_estimate=lasting(4),
        out_shape=tuple(
            jax.ShapeDtypeStruct((n, shape[0] // n, shape[1]), WIDE) for shape in shapes
        ),
        in_specs=[smem_spec()] + [whole_spec()] * len(arrays),
        out_specs=tuple(whole_spec() for _ in shapes),
        compiler_params=PARAMS,
    )(chunks, *arrays)
    return [out.reshape(shape) for out, shape in zip(outs, shapes)]


class RingGather:
    def __init__(self, value, n, split=True):
        self.n, self.split, self.done = n, split, 0
        self.value = value
        self.last = (value, value)
        self.ahead, self.back = [], []

    def keep(self):
        if self.done:
            self.ahead.append(self.last[0])
            if self.done < self.n // 2:
                self.back.append(self.last[1])

    def step(self):
        self.keep()
        self.done += 1
        f, b = self.last
        rows = self.value.shape[0] // 2
        if self.done < self.n // 2:
            self.last = (ring_shift(f, self.n, 1), ring_shift(b, self.n, -1))
        elif self.split:
            parts = ring_shift(f[:rows], self.n, 1), ring_shift(b[rows:], self.n, -1)
            self.last = (parts if self.split == "halves" else jnp.concatenate(parts, axis=0),)
        else:
            self.last = (ring_shift(f, self.n, 1),)

    def pieces(self):
        self.keep()
        return [self.value] + self.ahead + self.back


class RingReduce:
    def __init__(self, local, rank, n, first=None):
        self.local, self.rank, self.n, self.done = local, rank, n, 0
        self.first, self.last = first, None

    def part(self, step):
        return lax.dynamic_index_in_dim(
            self.local, (self.rank + step) % self.n, 0, keepdims=False
        )

    def step(self):
        half = self.n // 2
        if self.done == 0:
            f, b = self.first or (self.part(half), self.part(1 - half))
        else:
            f, b = self.last
            f = (f.astype(WIDE) + self.part(half - self.done).astype(WIDE)).astype(LOW)
            if self.done < half - 1:
                b = (b.astype(WIDE) + self.part(1 - half + self.done).astype(WIDE)).astype(LOW)
        f = ring_shift(f, self.n, 1)
        if self.done < half - 1:
            b = ring_shift(b, self.n, -1)
        self.last = (f, b)
        self.done += 1

    def total(self):
        f, b = self.last
        return f.astype(WIDE) + b.astype(WIDE) + self.part(0).astype(WIDE)


def pad_group(block):
    return jnp.pad(block, ((0, 0), (0, PAD - block.shape[1])))


def on_device(
    n,
    tokens,
    block_order,
    seq_lengths,
    cotangent,
    query_matrix,
    key_matrix,
    value_matrix,
    output_matrix,
    expand_matrix,
    reduce_matrix,
    query_bias,
    value_bias,
    output_bias,
    expand_bias,
    reduce_bias,
    first_gain,
    first_shift,
    second_gain,
    second_shift,
):
    w = lax.axis_index("wsh")
    c = lax.axis_index("ctx")
    barrier = lax.optimization_barrier
    order = ring_of(n)
    rank = jnp.asarray([order.index(i) for i in range(n)], jnp.int32)[c]
    width = tokens.shape[1]
    share = width // 4
    tokens_all = n * 4 * BLOCK

    other = wsh_swap(tokens, 2)
    both = jnp.concatenate([tokens, other], axis=0)
    (
        query_matrix,
        key_matrix,
        value_matrix,
        output_matrix,
        expand_matrix,
        reduce_matrix,
        output_bias,
        reduce_bias,
        expand_bias,
        first_gain,
        first_shift,
        second_gain,
        second_shift,
        other,
    ) = lax.optimization_barrier(
        (
            query_matrix,
            key_matrix,
            value_matrix,
            output_matrix,
            expand_matrix,
            reduce_matrix,
            output_bias,
            reduce_bias,
            expand_bias,
            first_gain,
            first_shift,
            second_gain,
            second_shift,
            other,
        )
    )

    def columns(matrix, group):
        low = matrix.astype(LOW)
        return [group(low[:, i * share : (i + 1) * share]) for i in range(4)]

    qkv_blocks = jnp.stack(
        [
            jnp.concatenate(parts, axis=1)
            for parts in zip(
                columns(query_matrix, pad_group),
                columns(key_matrix, pad_group),
                columns(value_matrix, pad_group),
            )
        ]
    )
    def deal(blocks):
        return lax.all_to_all(blocks, "wsh", 0, 0).reshape(-1, blocks.shape[2])

    qkv_matrix = deal(qkv_blocks)
    vectors = jnp.stack(
        [output_bias, reduce_bias, first_gain, first_shift, second_gain, second_shift]
    )
    vectors = jnp.concatenate([vectors, expand_bias.reshape(4, share)], axis=0).astype(LOW)
    nothing = jnp.zeros((PAD,), LOW)
    fill = jnp.zeros((PAD - share,), LOW)
    qkv_add = jnp.concatenate(
        [query_bias.astype(LOW), fill, nothing, value_bias.astype(LOW), fill]
    ).astype(WIDE)[None, :]
    output_low = output_matrix.astype(LOW)
    output_rows = jnp.pad(output_low, ((0, PAD - share), (0, 0)))

    ends = jnp.cumsum(seq_lengths)
    steps = jnp.asarray(slot_steps(n), jnp.int32)
    from_ctx = jnp.asarray(order, jnp.int32)[(rank + steps) % n]
    blocks = (from_ctx[:, None] * 4 + (w ^ jnp.asarray(ORDER, jnp.int32))[None, :]).reshape(-1)
    places = block_order[blocks]
    first = places[:4] * BLOCK
    low = jnp.max(jnp.where(ends[None, :] <= first[:, None], ends[None, :], 0), axis=1)
    last = first + BLOCK - 1
    high = jnp.min(jnp.where(ends[None, :] > last[:, None], ends[None, :], tokens_all), axis=1)
    low_block = low // BLOCK
    count = (high - low_block * BLOCK + BLOCK - 1) // BLOCK
    sends = (rank + jnp.asarray([n // 2, 1 - n // 2], jnp.int32)) % n
    tab = jnp.concatenate([places, low_block, count, sends]).astype(jnp.int32)
    seqs = seq_lengths.shape[0]
    seq_rows = jnp.pad(
        jnp.stack([ends - seq_lengths, ends]), ((0, 6), (SEQ_LANE, PAD - SEQ_LANE - seqs))
    ).astype(jnp.int32)

    expand_low, reduce_low = expand_matrix.astype(LOW), reduce_matrix.astype(LOW)
    middle_rows = reduce_matrix.shape[0] // 2
    side = c & 1
    reduce_half = lax.dynamic_slice_in_dim(reduce_low, side * middle_rows, middle_rows)
    ring = RingGather(both, n)
    half = n // 2
    for step in range(1, half + 1):
        ring.step()
        if step == 1:
            ring.last, vectors = barrier((ring.last, vectors))
            vector_pieces = [vectors] + [wsh_swap(vectors, j) for j in ORDER[1:]]
        elif step == 2:
            ready = (tab, seq_rows, qkv_add, output_rows, expand_low, reduce_low, reduce_half)
            ring.last, qkv_matrix, ready, vector_pieces = barrier(
                (ring.last, qkv_matrix, ready, vector_pieces)
            )
            tab, seq_rows, qkv_add, output_rows, expand_low, reduce_low, reduce_half = ready
            reduce_near = wsh_swap(reduce_half, 2)
        elif step == 3:
            ring.last, reduce_near = barrier((ring.last, reduce_near))
    reduce_far = exchange(reduce_near, "ctx", n, 1)
    expand_other = wsh_swap(expand_low, 2)
    token_pieces = []
    for piece in ring.pieces():
        token_pieces += [piece, wsh_swap(piece, 1)]
    expand_mate, reduce_mate = wsh_swap(expand_low, 1), wsh_swap(reduce_low, 1)
    reduce_last = [wsh_swap(reduce_near, 1)]
    attn, attended, keep, send, packed_queries, packed_keys, packed_values = attend(
        tab, seq_rows, qkv_matrix, qkv_add, output_rows, token_pieces, tokens_all
    )
    from_mate = wsh_swap(send, 1)
    branch_sum = (keep[BLOCK:] + from_mate[BLOCK:].astype(WIDE)).astype(LOW)
    from_other = wsh_swap(branch_sum, 2)
    expand_other, reduce_far, unused = barrier((expand_other, reduce_far, from_mate))
    reduce_last += [wsh_swap(reduce_far, 1)]
    expand_parts = [
        (expand_low, 0, 0),
        (expand_mate, 2, 0),
        (expand_other, 1, 0),
        (wsh_swap(expand_other, 1), 3, 0),
    ]
    reduce_parts = [(reduce_low, 0, 0), (reduce_mate, 2, 0)]
    for i, part in enumerate((reduce_near, reduce_far)):
        reduce_parts += [(part, 1, (4 + i,)), (reduce_last[i], 3, (4 + i,))]
    group = jnp.concatenate(
        [
            (w ^ jnp.asarray(ORDER, jnp.int32)).astype(jnp.int32),
            jnp.stack([side, 1 - side]).astype(jnp.int32) * middle_rows,
        ]
    )
    layer_out, grad_hidden, branch_in, pair, lows = middle(
        group,
        tokens,
        keep,
        from_mate,
        from_other,
        cotangent,
        vector_pieces,
        expand_parts,
        reduce_parts,
    )
    branch_pieces = group_pieces(branch_in)
    branch_all = jnp.concatenate(branch_pieces, axis=0)
    outgrad = attend_outgrad(branch_all, output_rows, attn)
    grad_output = lax.dot_general(
        attended[:, :share], branch_all, (((0,), (0,)), ((), ())), preferred_element_type=WIDE
    ).astype(LOW)

    def rows_dot(left, right):
        return lax.dot_general(
            left, right, (((0,), (0,)), ((), ())), preferred_element_type=WIDE
        ).astype(LOW)

    def redeal(chunk):
        lines = chunk.shape[0] // 4
        return lax.all_to_all(chunk.astype(LOW).reshape(4, lines, -1), "wsh", 0, 0)

    def by_place(matrix):
        cols = matrix.shape[1]
        return matrix.reshape(4, n, share // n, cols).transpose(1, 0, 2, 3).reshape(n, -1, cols)

    def joined(dealt, first):
        return jnp.concatenate([dealt[i, :, first : first + share] for i in range(4)], axis=1)

    shard = reduce_matrix.shape[0]
    lines = share // n
    pair, lows, outgrad = barrier((pair, lows, outgrad))
    pair = lax.all_to_all(pair, "wsh", 0, 0)
    lows = [lows, wsh_swap(lows, 2)]
    grad_ring = RingGather(outgrad, n, split=False)
    grad_ring.step()
    grad_ring.last, outgrad, grad_output = barrier((grad_ring.last, outgrad, grad_output))
    grad_ring.step()
    grad_query = query_back(tab, outgrad, packed_queries, packed_keys, packed_values, tokens_all)
    grad_ring.last, grad_query = barrier((grad_ring.last, grad_query))
    grad_ring.step()
    grad_ring.last, pair, lows = barrier((grad_ring.last, pair, lows))
    lows = to_absolute([lows[0], wsh_swap(lows[0], 1), lows[1], wsh_swap(lows[1], 1)], w)
    reduce_all = jnp.concatenate([low[:BLOCK] for low in lows], axis=0)
    normed_all = jnp.concatenate([low[BLOCK:] for low in lows], axis=0)
    grad_reduce = rows_dot(pair[:, :BLOCK].reshape(4 * BLOCK, -1), reduce_all)
    grad_expand = rows_dot(normed_all, pair[:, BLOCK : 2 * BLOCK].reshape(4 * BLOCK, -1))
    sums = pair[:, 2 * BLOCK :, :share]
    early = jnp.concatenate(
        [grad_reduce.reshape(n, shard // n, width), by_place(grad_expand)], axis=1
    )
    for step in range(3, half):
        grad_ring.step()
        grad_ring.last, early, sums = barrier((grad_ring.last, early, sums))

    early_ring = RingReduce(early, rank, n)
    early_ring.step()
    grad_kv, late, ahead, behind = key_back(
        tab,
        token_pieces[:2],
        grad_query,
        grad_output,
        sums,
        grad_ring.pieces(),
        (packed_queries, packed_keys, packed_values),
        tokens_all,
    )
    early_ring.last, grad_kv, late, ahead, behind = barrier(
        (early_ring.last, grad_kv, late, ahead, behind)
    )
    late_ring = RingReduce(late, rank, n, (ahead, behind))
    for step in range(1, half):
        late_ring.step()
        early_ring.step()
        late_ring.last, early_ring.last = barrier((late_ring.last, early_ring.last))
    late_ring.step()
    early = early_ring.total()
    early = jnp.concatenate(
        [early[: shard // n].astype(LOW), redeal(early[shard // n :]).reshape(4 * lines, width)],
        axis=0,
    )
    late_ring.last, early = barrier((late_ring.last, early))

    early_gather = RingGather(early, n, split="halves")
    early_gather.step()
    late = late_ring.total()
    extra = late[4 * lines :].astype(LOW)
    own_output = late[: 4 * lines, 3 * share :].astype(LOW).reshape(4, lines, share)
    dealt = redeal(late[: 4 * lines, : 3 * share])
    late = jnp.concatenate(
        [joined(dealt, i * share) for i in range(3)] + [joined(own_output, 0), extra], axis=0
    )
    chunks = (rank + steps) % n
    late_gather = RingGather(late, n, split=False)
    for step in range(1, half):
        late_gather.step()
        early_gather.step()
        late_gather.last, early_gather.last = barrier((late_gather.last, early_gather.last))
    late_gather.step()
    out_reduce, out_expand = assemble(
        chunks,
        early_gather.pieces(),
        ((0, shard // n, 1), (shard // n, lines, 4)),
        ((shard, width), (share, 4 * width)),
    )
    late_gather.last, out_reduce, out_expand = barrier((late_gather.last, out_reduce, out_expand))
    tokens_grad = (
        scatter_group(
            dot_nt(grad_query, qkv_matrix[:, :PAD]) + dot_nt(grad_kv, qkv_matrix[:, PAD:])
        )
        + grad_hidden
    ).astype(LOW)
    out_query, out_key, out_value, out_output, small = assemble(
        chunks,
        late_gather.pieces(),
        tuple((i * lines, lines, 1) for i in range(4)) + ((4 * lines, 8, 1),),
        ((share, width),) * 4 + ((8 * n, width),),
    )
    small = small.reshape(n, 8, width)[:, : vector_rows(n), :share].reshape(-1, share)
    out_expand_bias = small[6:10].reshape(-1)
    return (
        layer_out,
        tokens_grad,
        out_query,
        out_key,
        out_value,
        out_output,
        out_expand,
        out_reduce,
        small[10],
        small[11],
        small[4],
        out_expand_bias,
        small[5],
        small[0],
        small[1],
        small[2],
        small[3],
    )


def solution(mesh):
    n = mesh.shape["ctx"]
    rows = P(("ctx", "wsh"), None)
    in_specs = (rows, P(), P(), rows) + (P("wsh", None),) * 6 + (P("wsh"),) * 9
    out_specs = (rows, rows) + (P("wsh", None),) * 6 + (P("wsh"),) * 9

    def run(*args):
        return on_device(n, *args)

    return jax.shard_map(run, mesh=mesh, in_specs=in_specs, out_specs=out_specs, check_vma=False)
```

```python
import math

import jax
import jax.numpy as jnp
from jax import lax
from jax.experimental import pallas as pl
from jax.experimental.pallas import tpu as pltpu
from jax.sharding import PartitionSpec as P

HDIM = 64
BLOCK = 128
EPSILON = 1e-12
LOW = jnp.bfloat16
WIDE = jnp.float32

ORDER = (0, 2, 1, 3)

PAD = 256
DELTA_LANE = 192
LSE_LANE = 201
SEQ_LANE = 216
BIG = 1e30
CHUNK = 1024
REST = 256


def ring_of(n):
    return list(range(0, n, 2)) + list(range(n - 1, 0, -2))


def exchange(value, axis, size, flip):
    return lax.ppermute(value, axis, [(i, i ^ flip) for i in range(size)])


def wsh_swap(value, flip):
    return exchange(value, "wsh", 4, flip)


def to_absolute(pieces, w):
    one = (w & 1) == 1
    two = (w & 2) == 2
    a = [jnp.where(one, pieces[j ^ 1], pieces[j]) for j in range(4)]
    return [jnp.where(two, a[j ^ 2], a[j]) for j in range(4)]


def group_pieces(value):
    other = wsh_swap(value, 2)
    return [value, other, wsh_swap(value, 1), wsh_swap(other, 1)]


def scatter_group(parts):
    rows = parts.shape[0] // 4
    mine, other, mate, last = [parts[i * rows : (i + 1) * rows] for i in range(4)]
    got = wsh_swap(jnp.concatenate([mate, last], axis=0).astype(LOW), 1).astype(WIDE)
    mine = mine + got[:rows]
    other = other + got[rows:]
    return mine + wsh_swap(other.astype(LOW), 2).astype(WIDE)


def ring_shift(value, n, step):
    ring = ring_of(n)
    return lax.ppermute(value, "ctx", [(ring[i], ring[(i + step) % n]) for i in range(n)])


def ring_gather(value, n, split=True, tie=None):
    half = n // 2
    rows = value.shape[0]
    ahead, back = [], []
    f = b = value
    tied = None
    for step in range(1, half + 1):
        if tie is not None and step == tie[0]:
            f, b, tied = lax.optimization_barrier((f, b, tie[1]))
        if step < half:
            f = ring_shift(f, n, 1)
            b = ring_shift(b, n, -1)
            ahead.append(f)
            back.append(b)
        elif not split:
            ahead.append(ring_shift(f, n, 1))
        else:
            first = ring_shift(f[: rows // 2], n, 1)
            second = ring_shift(b[rows // 2 :], n, -1)
            ahead.append(jnp.concatenate([first, second], axis=0))
    pieces = [value] + ahead + back
    return pieces if tie is None else (pieces, tied)


def slot_steps(n):
    half = n // 2
    return [0] + [-s for s in range(1, half + 1)] + list(range(1, half))


def lanes_of(head, lane):
    keep = (lane >= head * HDIM) & (lane < (head + 1) * HDIM)
    return keep


def stack_heads(value):
    lane = lax.broadcasted_iota(jnp.int32, value.shape, 1)
    out = []
    for head in range(3):
        keep = (
            lanes_of(head, lane)
            | ((lane >= DELTA_LANE + 3 * head) & (lane < DELTA_LANE + 3 * head + 3))
            | ((lane >= LSE_LANE + 3 * head) & (lane < LSE_LANE + 3 * head + 3))
            | (lane >= SEQ_LANE)
        )
        out.append(jnp.where(keep, value, jnp.zeros_like(value)))
    return jnp.concatenate(out, axis=0)


def pick_heads(value):
    lane = lax.broadcasted_iota(jnp.int32, (BLOCK, PAD), 1)
    total = jnp.zeros((BLOCK, PAD), WIDE)
    for head in range(3):
        total = jnp.where(lanes_of(head, lane), value[head * BLOCK : (head + 1) * BLOCK], total)
    return total


def dot_nt(a, b):
    return lax.dot_general(a, b, (((1,), (1,)), ((), ())), preferred_element_type=WIDE)


def dot_nn(a, b):
    return jnp.dot(a, b, preferred_element_type=WIDE)


def over_chunks(low, count, visit, state):
    large, small = CHUNK // BLOCK, REST // BLOCK

    def at(first, size):
        return pl.ds(pl.multiple_of(first * BLOCK, BLOCK), size)

    whole = count // large
    state = lax.fori_loop(
        0, whole, lambda c, now: visit(at(low + c * large, CHUNK), now), state
    )
    first = low + whole * large
    rest = (count - whole * large + small - 1) // small
    return lax.fori_loop(0, rest, lambda c, now: visit(at(first + c * small, REST), now), state)


def seq_marks(seq_ref, place):
    spot = place * BLOCK + lax.broadcasted_iota(jnp.int32, (BLOCK, PAD), 0)
    return (spot >= seq_ref[0:1, :]) & (spot < seq_ref[1:2, :])


def key_lanes(seq_ref, place, value):
    lane = lax.broadcasted_iota(jnp.int32, (BLOCK, PAD), 1)
    marks = seq_marks(seq_ref, place)
    minus = (lane >= LSE_LANE) & (lane < LSE_LANE + 9)
    out = jnp.where(minus, -1.0, value.astype(WIDE))
    return jnp.where((lane >= SEQ_LANE) & ~marks, -BIG, out).astype(LOW)


def query_lanes(seq_ref, place, value):
    return jnp.where(seq_marks(seq_ref, place), 1.0, value.astype(WIDE)).astype(LOW)


def value_lanes(value):
    lane = lax.broadcasted_iota(jnp.int32, (BLOCK, PAD), 1)
    minus = (lane >= DELTA_LANE) & (lane < DELTA_LANE + 9)
    return jnp.where(minus, -1.0, value.astype(WIDE)).astype(LOW)


def parts_of(column):
    high = column.astype(LOW).astype(WIDE)
    rest = column - high
    mid = rest.astype(LOW).astype(WIDE)
    return high, mid, (rest - mid).astype(LOW).astype(WIDE)


def end_rows(seq_value):
    lane = lax.broadcasted_iota(jnp.int32, (CHUNK, PAD), 1)
    return jnp.where(lane >= SEQ_LANE, seq_value, 0.0).astype(LOW)


def attend_kernel(pieces, tokens_all, tab_ref, seq_ref, matrix_ref, add_ref, output_ref, *refs):
    tokens = refs[:pieces]
    (
        out_ref,
        low_ref,
        keep_ref,
        send_ref,
        query_out,
        key_out,
        value_out,
        token_ref,
        query_ref,
        key_ref,
        value_ref,
        token_sems,
        sems,
    ) = refs[pieces:]
    per = tokens[0].shape[0] // BLOCK
    many = tokens[0].shape[0]
    copies = [
        pltpu.make_async_copy(tokens[i], token_ref.at[pl.ds(i * many, many)], token_sems.at[i])
        for i in range(pieces)
    ]
    for copy in copies:
        copy.start()
    base = tokens_all // BLOCK
    rest = pl.ds(tokens_all, CHUNK)
    key_ref[rest, :] = end_rows(-BIG)
    query_ref[rest, :] = end_rows(1.0)
    value_ref[rest, :] = jnp.zeros((CHUNK, PAD), LOW)

    def project(i, unused):
        rows = pl.ds(pl.multiple_of(i * 2 * many, BLOCK), 2 * many)
        for j in range(2):
            spot = token_ref.at[pl.ds(pl.multiple_of((i * 2 + j) * many, BLOCK), many)]
            pltpu.make_async_copy(spot, spot, token_sems.at[i * 2 + j]).wait()
        wide = dot_nn(token_ref[rows, :], matrix_ref[...]) + add_ref[...]
        low = wide.astype(LOW)
        for j in range(2 * per):
            place = tab_ref[i * 2 * per + j]
            spot = pl.ds(pl.multiple_of(place * BLOCK, BLOCK), BLOCK)
            block = low[j * BLOCK : (j + 1) * BLOCK]
            query = block[:, :PAD].astype(WIDE) * HDIM ** (-0.5)
            query_ref[spot, :] = query_lanes(seq_ref, place, query)
            key_ref[spot, :] = key_lanes(seq_ref, place, block[:, PAD : 2 * PAD])
            value_ref[spot, :] = value_lanes(block[:, 2 * PAD :])
        return unused

    lax.fori_loop(0, pieces // 2, project, 0)
    stores = [
        pltpu.make_async_copy(source, target, sems.at[i])
        for i, (source, target) in enumerate(
            ((query_ref, query_out), (key_ref, key_out), (value_ref, value_out))
        )
    ]
    for store in stores:
        store.start()
    lane = lax.broadcasted_iota(jnp.int32, (BLOCK, PAD), 1)

    def block(i, unused):
        rows = pl.ds(pl.multiple_of(i * BLOCK, BLOCK), BLOCK)
        own = pl.ds(pl.multiple_of(tab_ref[i] * BLOCK, BLOCK), BLOCK)
        low = tab_ref[base + i]
        count = tab_ref[base + 4 + i]
        queries = stack_heads(query_ref[own, :])

        def visit(spot, state):
            top, total, accum = state
            scores = dot_nt(queries, key_ref[spot, :])
            top_new = jnp.maximum(top, jnp.max(scores, axis=1, keepdims=True))
            weights = jnp.exp(scores - top_new)
            factor = jnp.exp(top - top_new)
            total = total * factor + jnp.sum(weights, axis=1, keepdims=True)
            accum = accum * factor + dot_nn(weights.astype(LOW), value_ref[spot, :])
            return top_new, total, accum

        top, total, accum = over_chunks(
            low,
            count,
            visit,
            (
                jnp.full((3 * BLOCK, 1), -2 * BIG, WIDE),
                jnp.zeros((3 * BLOCK, 1), WIDE),
                jnp.zeros((3 * BLOCK, PAD), WIDE),
            ),
        )
        result = pick_heads(accum / total)
        logsum = top + jnp.log(total)
        for head in range(3):
            result = jnp.where(
                lane == DELTA_LANE + head, logsum[head * BLOCK : (head + 1) * BLOCK], result
            )
        out_ref[rows, :] = result
        return unused

    lax.fori_loop(0, 4, block, 0)
    low = out_ref[...].astype(LOW)
    low_ref[...] = low
    half = 2 * BLOCK
    keep_ref[...] = dot_nn(low[:half], output_ref[...])
    send_ref[...] = dot_nn(low[half:], output_ref[...]).astype(LOW)
    for store in stores:
        store.wait()


def row_mean(values):
    return jnp.sum(values, axis=1, keepdims=True) * (1.0 / values.shape[1])


def norm_parts(values):
    centred = values - row_mean(values)
    scale = lax.rsqrt(row_mean(centred * centred) + EPSILON)
    return centred * scale, scale


def norm_back(upstream, normal, scale):
    return scale * (upstream - row_mean(upstream) - normal * row_mean(upstream * normal))


def middle_kernel(
    expand_spots,
    reduce_spots,
    share,
    place_ref,
    tokens_ref,
    mine_ref,
    mate_ref,
    other_ref,
    cotangent_ref,
    *refs,
):
    parts = len(expand_spots)
    vectors, refs = refs[:4], refs[4:]
    matrices = refs[: parts + len(reduce_spots)]
    (
        layer_ref,
        hidden_grad_ref,
        branch_ref,
        pair_ref,
        low_ref,
        expand_ref,
        reduce_ref,
        slope_ref,
        sums_ref,
        vector_ref,
        sems,
    ) = refs[len(matrices) :]
    copies = []
    for i, (part, (index, first)) in enumerate(zip(matrices, expand_spots + reduce_spots)):
        target, rows = (expand_ref, share) if i < parts else (reduce_ref, reduce_ref.shape[0] // 4)
        if isinstance(first, tuple):
            first = place_ref[first[0]]
        spot = pl.ds(pl.multiple_of(place_ref[index] * rows + first, 8), part.shape[0])
        copies.append(pltpu.make_async_copy(part, target.at[spot], sems.at[i]))
    for copy in copies:
        copy.start()
    for i, piece in enumerate(vectors):
        vector_ref[place_ref[i]] = piece[...].astype(WIDE)
    by_device = [vector_ref[j] for j in range(4)]
    output_add, reduce_add, first_scale, first_move, second_scale, second_move = [
        jnp.concatenate([rows[i : i + 1] for rows in by_device], axis=1) for i in range(6)
    ]
    expand_add = [
        jnp.concatenate([rows[i : i + 1] for i in range(6, 10)], axis=1) for rows in by_device
    ]
    own = pl.ds(0, BLOCK)
    branch = mine_ref[own, :] + mate_ref[own, :].astype(WIDE) + other_ref[...].astype(WIDE)
    hidden = tokens_ref[...].astype(WIDE) + (branch + output_add)
    first_normal, first_rate = norm_parts(hidden)
    normed = first_normal * first_scale + first_move
    normed_low = normed.astype(LOW)
    low_ref[pl.ds(BLOCK, BLOCK), :] = normed_low
    for copy in copies[:parts]:
        copy.wait()
    width = normed.shape[1]
    reduced = jnp.zeros(normed.shape, WIDE)
    for j in range(4):
        cols = pl.ds(j * width, width)
        expanded = dot_nn(normed_low, expand_ref[:, cols]) + expand_add[j]
        phi_cdf = 0.5 * (1.0 + lax.erf(expanded * (2.0**-0.5)))
        slope_ref[:, cols] = phi_cdf + expanded * (
            jnp.exp(-0.5 * expanded * expanded) * (2.0 * math.pi) ** -0.5
        )
        activated = (expanded * phi_cdf).astype(LOW)
        pair_ref[j, pl.ds(0, BLOCK), :] = activated
        if j == 0:
            for copy in copies[parts:]:
                copy.wait()
        reduced = reduced + dot_nn(activated, reduce_ref[cols, :])
    summed = normed + (reduced + reduce_add)
    second_normal, second_rate = norm_parts(summed)
    layer_ref[...] = (second_normal * second_scale + second_move).astype(LOW)
    upstream = cotangent_ref[...].astype(WIDE)

    def column_sum(row, values):
        sums_ref[row : row + 1, :] = jnp.sum(values, axis=0, keepdims=True)

    column_sum(2, upstream * second_normal)
    column_sum(3, upstream)
    grad_summed = norm_back(upstream * second_scale, second_normal, second_rate)
    reduce_in = grad_summed.astype(LOW)
    low_ref[pl.ds(0, BLOCK), :] = reduce_in
    column_sum(5, reduce_in.astype(WIDE))
    grad_normed = grad_summed
    for j in range(4):
        cols = pl.ds(j * width, width)
        expand_in = (dot_nt(reduce_in, reduce_ref[cols, :]) * slope_ref[:, cols]).astype(LOW)
        pair_ref[j, pl.ds(BLOCK, BLOCK), :] = expand_in
        column_sum(6 + j, expand_in.astype(WIDE))
        grad_normed = grad_normed + dot_nt(expand_in, expand_ref[:, cols])
    column_sum(0, grad_normed * first_normal)
    column_sum(1, grad_normed)
    grad_hidden = norm_back(grad_normed * first_scale, first_normal, first_rate)
    hidden_grad_ref[...] = grad_hidden
    branch_in = grad_hidden.astype(LOW)
    branch_ref[...] = branch_in
    column_sum(4, branch_in.astype(WIDE))
    for j in range(4):
        rows = [sums_ref[0:6, j * share : (j + 1) * share]]
        rows += [sums_ref[6 + j : 7 + j, k * share : (k + 1) * share] for k in range(4)]
        rows = jnp.concatenate(rows + [jnp.zeros((6, share), WIDE)], axis=0)
        pair_ref[j, pl.ds(2 * BLOCK, 16), :] = jnp.zeros((16, width), LOW)
        pair_ref[j, pl.ds(2 * BLOCK, 16), pl.ds(0, share)] = rows.astype(LOW)


def outgrad_kernel(branch_ref, matrix_ref, attn_ref, out_ref):
    grad = dot_nt(branch_ref[...], matrix_ref[...]).astype(LOW).astype(WIDE)
    attn = attn_ref[...]
    lane = lax.broadcasted_iota(jnp.int32, grad.shape, 1)
    product = grad * attn
    out = jnp.where(lane < DELTA_LANE, grad, 0.0)
    for head in range(3):
        delta = jnp.sum(jnp.where(lanes_of(head, lane), product, 0.0), axis=1, keepdims=True)
        logsum = jnp.sum(jnp.where(lane == DELTA_LANE + head, attn, 0.0), axis=1, keepdims=True)
        for first, column in ((DELTA_LANE, delta), (LSE_LANE, logsum)):
            for i, part in enumerate(parts_of(column)):
                out = jnp.where(lane == first + 3 * head + i, part, out)
    out_ref[...] = out.astype(LOW)


def lse_lanes(query, outgrad):
    lane = lax.broadcasted_iota(jnp.int32, query.shape, 1)
    return jnp.where((lane >= LSE_LANE) & (lane < LSE_LANE + 9), outgrad, query)


def own_blocks(tab_ref, packed, target, sem):
    for i in range(4):
        own = pl.ds(pl.multiple_of(tab_ref[i] * BLOCK, BLOCK), BLOCK)
        pltpu.make_async_copy(packed.at[own], target.at[pl.ds(i * BLOCK, BLOCK)], sem).start()


def own_wait(target, sem):
    pltpu.make_async_copy(target, target, sem).wait()


def query_back_kernel(
    tokens_all, tab_ref, grad_ref, query_all, key_ref, value_ref, out_ref, own_ref, sems
):
    own_blocks(tab_ref, query_all, own_ref, sems.at[0])
    base = tokens_all // BLOCK
    own_wait(own_ref, sems.at[0])

    def block(i, unused):
        rows = pl.ds(pl.multiple_of(i * BLOCK, BLOCK), BLOCK)
        low = tab_ref[base + i]
        outgrad = grad_ref[rows, :]
        left = stack_heads(lse_lanes(own_ref[rows, :], outgrad))
        right = stack_heads(outgrad)

        def visit(spot, accum):
            keys = key_ref[spot, :]
            probs = jnp.exp(dot_nt(left, keys))
            slopes = (probs * dot_nt(right, value_ref[spot, :])).astype(LOW)
            return accum + dot_nn(slopes, keys)

        accum = over_chunks(
            low, tab_ref[base + 4 + i], visit, jnp.zeros((3 * BLOCK, PAD), WIDE)
        )
        out_ref[rows, :] = (pick_heads(accum) * HDIM ** (-0.5)).astype(LOW)
        return unused

    lax.fori_loop(0, 4, block, 0)


def vector_rows(n):
    return max(1, 16 // n)


def key_back_kernel(pieces, n, tokens_all, tab_ref, first_ref, last_ref, dq_ref, side_ref, sums_ref, *refs):
    grads = refs[:pieces]
    (
        query_all,
        key_all,
        value_all,
        out_ref,
        late_ref,
        ahead_ref,
        behind_ref,
        query_ref,
        grad_ref,
        key_ref,
        value_ref,
        sems,
    ) = refs[pieces:]
    query_copy = pltpu.make_async_copy(query_all, query_ref, sems.at[0])
    query_copy.start()
    spots = [(array, j) for array in grads for j in range(array.shape[0] // BLOCK)]
    for i, (array, j) in enumerate(spots):
        place = pl.multiple_of(tab_ref[i] * BLOCK, BLOCK)
        pltpu.make_async_copy(
            array.at[pl.ds(j * BLOCK, BLOCK)], grad_ref.at[pl.ds(place, BLOCK)], sems.at[1]
        ).start()
    own_blocks(tab_ref, key_all, key_ref, sems.at[2])
    own_blocks(tab_ref, value_all, value_ref, sems.at[3])
    base = tokens_all // BLOCK
    grad_ref[pl.ds(tokens_all, CHUNK), :] = jnp.zeros((CHUNK, PAD), LOW)
    query_copy.wait()
    whole = grad_ref.at[pl.ds(0, tokens_all)]
    pltpu.make_async_copy(whole, whole, sems.at[1]).wait()
    own_wait(key_ref, sems.at[2])
    own_wait(value_ref, sems.at[3])

    def fix(place, unused):
        rows = pl.ds(pl.multiple_of(place * BLOCK, BLOCK), BLOCK)
        query_ref[rows, :] = lse_lanes(query_ref[rows, :], grad_ref[rows, :])
        return unused

    lax.fori_loop(0, base, fix, 0)

    def block(i, unused):
        rows = pl.ds(pl.multiple_of(i * BLOCK, BLOCK), BLOCK)
        low = tab_ref[base + i]
        zeros = jnp.zeros((3 * BLOCK, PAD), WIDE)
        key_left = stack_heads(key_ref[rows, :])
        value_right = stack_heads(value_ref[rows, :])

        def visit(spot, state):
            key_accum, value_accum = state
            queries = query_ref[spot, :]
            outgrads = grad_ref[spot, :]
            probs = jnp.exp(dot_nt(key_left, queries))
            slopes = (probs * dot_nt(value_right, outgrads)).astype(LOW)
            value_accum = value_accum + dot_nn(probs.astype(LOW), outgrads)
            key_accum = key_accum + dot_nn(slopes, queries)
            return key_accum, value_accum

        key_accum, value_accum = over_chunks(
            low, tab_ref[base + 4 + i], visit, (zeros, zeros)
        )
        out_ref[rows, pl.ds(0, PAD)] = pick_heads(key_accum).astype(LOW)
        out_ref[rows, pl.ds(PAD, PAD)] = pick_heads(value_accum).astype(LOW)
        return unused

    lax.fori_loop(0, 4, block, 0)
    share = DELTA_LANE
    lines = share // n
    many = first_ref.shape[0]
    dkv = out_ref[...]
    columns = [dq_ref[:, :share], dkv[:, :share], dkv[:, PAD : PAD + share]]
    grad_all = jnp.concatenate([dq_ref[...], dkv], axis=1)

    def turned(left, right):
        return lax.dot_general(
            left, right, (((0,), (0,)), ((), ())), preferred_element_type=WIDE
        )

    grad = turned(first_ref[...], grad_all[:many]) + turned(last_ref[...], grad_all[many:])
    for i in range(3):
        column = grad[:, i * PAD : i * PAD + share].astype(LOW)
        for place in range(n):
            for group in range(4):
                row = group * share + place * lines
                late_ref[
                    place, pl.ds(group * lines, lines), pl.ds(i * share, share)
                ] = column[row : row + lines]
    side = side_ref[...]
    for place in range(n):
        for group in range(4):
            late_ref[place, pl.ds(group * lines, lines), pl.ds(3 * share, share)] = side[
                place * lines : (place + 1) * lines, group * share : (group + 1) * share
            ]
    few = vector_rows(n)
    rows = jnp.concatenate(
        [
            jnp.sum(sums_ref[...].astype(WIDE), axis=0)[0:10],
            jnp.sum(columns[0].astype(WIDE), axis=0, keepdims=True),
            jnp.sum(columns[2].astype(WIDE), axis=0, keepdims=True),
            jnp.zeros((few * n - 12, share), WIDE),
        ],
        axis=0,
    ).astype(LOW)
    for place in range(n):
        late_ref[place, pl.ds(4 * lines, 16), :] = jnp.zeros((16, late_ref.shape[2]), LOW)
        late_ref[place, pl.ds(4 * lines, few), pl.ds(0, share)] = rows[
            place * few : (place + 1) * few
        ]
    ahead_ref[...] = late_ref[tab_ref[base + 8]]
    behind_ref[...] = late_ref[tab_ref[base + 9]]


def assemble_kernel(slots, layout, tab_ref, *refs):
    outs = refs[len(slots) :]
    for (i, start), piece in zip(slots, refs):
        chunk = tab_ref[i]
        for out_ref, (first, rows, blocks) in zip(outs, layout):
            wide = out_ref.shape[2] // blocks
            for j in range(blocks):
                at = first + j * rows - start
                if 0 <= at and at + rows <= piece.shape[0]:
                    out_ref[chunk, :, pl.ds(j * wide, wide)] = piece[pl.ds(at, rows), :].astype(WIDE)


def lasting(micros):
    return pl.CostEstimate(flops=0, transcendentals=0, bytes_accessed=int(micros * 3_000_000))


def whole_spec():
    return pl.BlockSpec(memory_space=pltpu.VMEM)


def any_spec():
    return pl.BlockSpec(memory_space=pl.ANY)


def smem_spec():
    return pl.BlockSpec(memory_space=pltpu.SMEM)


PARAMS = pltpu.CompilerParams(vmem_limit_bytes=60 << 20)


def attend(tab, seq_rows, matrix, add, output_rows, token_pieces, tokens_all):
    pieces = len(token_pieces)

    def kernel(*refs):
        attend_kernel(pieces, tokens_all, *refs)

    packed = jax.ShapeDtypeStruct((tokens_all + CHUNK, PAD), LOW)
    width = output_rows.shape[1]
    return pl.pallas_call(
        kernel,
        name="attend",
        cost_estimate=lasting(18),
        out_shape=(
            jax.ShapeDtypeStruct((4 * BLOCK, PAD), WIDE),
            jax.ShapeDtypeStruct((4 * BLOCK, PAD), LOW),
            jax.ShapeDtypeStruct((2 * BLOCK, width), WIDE),
            jax.ShapeDtypeStruct((2 * BLOCK, width), LOW),
            packed,
            packed,
            packed,
        ),
        in_specs=[smem_spec()] + [whole_spec()] * 4 + [any_spec()] * pieces,
        out_specs=(whole_spec(),) * 4 + (any_spec(),) * 3,
        scratch_shapes=[pltpu.VMEM((tokens_all, matrix.shape[0]), LOW)]
        + [pltpu.VMEM((tokens_all + CHUNK, PAD), LOW)] * 3
        + [pltpu.SemaphoreType.DMA((pieces,)), pltpu.SemaphoreType.DMA((3,))],
        compiler_params=PARAMS,
    )(tab, seq_rows, matrix, add, output_rows, *token_pieces)


def query_back(tab, outgrad, queries, keys, values, tokens_all):
    def kernel(*refs):
        query_back_kernel(tokens_all, *refs)

    return pl.pallas_call(
        kernel,
        name="query_back",
        cost_estimate=lasting(11),
        out_shape=jax.ShapeDtypeStruct((4 * BLOCK, PAD), LOW),
        in_specs=[smem_spec(), whole_spec(), any_spec(), whole_spec(), whole_spec()],
        out_specs=whole_spec(),
        scratch_shapes=[pltpu.VMEM((4 * BLOCK, PAD), LOW), pltpu.SemaphoreType.DMA((1,))],
        compiler_params=PARAMS,
    )(tab, outgrad, queries, keys, values)


def key_back(tab, token_pieces, grad_query, side, sums, grad_pieces, packed, tokens_all):
    flat = []
    for piece in grad_pieces:
        flat += piece if isinstance(piece, tuple) else [piece]
    grad_pieces = flat
    pieces = len(grad_pieces)
    n = tokens_all // (4 * BLOCK)
    width = token_pieces[0].shape[1]

    def kernel(*refs):
        key_back_kernel(pieces, n, tokens_all, *refs)

    return pl.pallas_call(
        kernel,
        name="key_back",
        cost_estimate=lasting(16),
        out_shape=(
            jax.ShapeDtypeStruct((4 * BLOCK, 2 * PAD), LOW),
            jax.ShapeDtypeStruct((n, width // n + 16, width), LOW),
            jax.ShapeDtypeStruct((width // n + 16, width), LOW),
            jax.ShapeDtypeStruct((width // n + 16, width), LOW),
        ),
        in_specs=[smem_spec()] + [whole_spec()] * 5 + [any_spec()] * (pieces + 3),
        out_specs=(whole_spec(),) * 4,
        scratch_shapes=[pltpu.VMEM((tokens_all + CHUNK, PAD), LOW)] * 2
        + [pltpu.VMEM((4 * BLOCK, PAD), LOW)] * 2
        + [pltpu.SemaphoreType.DMA((4,))],
        compiler_params=PARAMS,
    )(tab, *token_pieces, grad_query, side, sums, *grad_pieces, *packed)


def middle(places, tokens, mine, mate, other, cotangent, vectors, expands, reduces):
    rows, width = tokens.shape
    hidden = expands[0][0].shape[1]
    matrices = [part[0] for part in expands + reduces]
    expand_spots = [part[1:] for part in expands]
    reduce_spots = [part[1:] for part in reduces]

    def kernel(*refs):
        middle_kernel(expand_spots, reduce_spots, width // 4, *refs)

    return pl.pallas_call(
        kernel,
        name="middle",
        cost_estimate=lasting(11),
        out_shape=(
            jax.ShapeDtypeStruct((rows, width), LOW),
            jax.ShapeDtypeStruct((rows, width), WIDE),
            jax.ShapeDtypeStruct((rows, width), LOW),
            jax.ShapeDtypeStruct((4, 2 * rows + 16, hidden // 4), LOW),
            jax.ShapeDtypeStruct((2 * rows, width), LOW),
        ),
        in_specs=[smem_spec()] + [whole_spec()] * 9 + [any_spec()] * len(matrices),
        out_specs=(whole_spec(),) * 5,
        scratch_shapes=[
            pltpu.VMEM((width, hidden), LOW),
            pltpu.VMEM((hidden, width), LOW),
            pltpu.VMEM((rows, hidden), WIDE),
            pltpu.VMEM((16, width), WIDE),
            pltpu.VMEM((4,) + vectors[0].shape, WIDE),
            pltpu.SemaphoreType.DMA((len(matrices),)),
        ],
        compiler_params=PARAMS,
    )(places, tokens, mine, mate, other, cotangent, *vectors, *matrices)


def attend_outgrad(branch, matrix, attn):
    return pl.pallas_call(
        outgrad_kernel,
        name="outgrad",
        cost_estimate=lasting(3),
        out_shape=jax.ShapeDtypeStruct((4 * BLOCK, PAD), LOW),
        in_specs=[whole_spec()] * 3,
        out_specs=whole_spec(),
    )(branch, matrix, attn)


def assemble(chunks, pieces, layout, shapes):
    n = len(pieces)
    slots, arrays = [], []
    for i, piece in enumerate(pieces):
        start = 0
        for part in piece if isinstance(piece, tuple) else (piece,):
            slots.append((i, start))
            arrays.append(part)
            start += part.shape[0]

    def kernel(*refs):
        assemble_kernel(slots, layout, *refs)

    outs = pl.pallas_call(
        kernel,
        name="assemble",
        cost_estimate=lasting(4),
        out_shape=tuple(
            jax.ShapeDtypeStruct((n, shape[0] // n, shape[1]), WIDE) for shape in shapes
        ),
        in_specs=[smem_spec()] + [whole_spec()] * len(arrays),
        out_specs=tuple(whole_spec() for _ in shapes),
        compiler_params=PARAMS,
    )(chunks, *arrays)
    return [out.reshape(shape) for out, shape in zip(outs, shapes)]


class RingGather:
    def __init__(self, value, n, split=True):
        self.n, self.split, self.done = n, split, 0
        self.value = value
        self.last = (value, value)
        self.ahead, self.back = [], []

    def keep(self):
        if self.done:
            self.ahead.append(self.last[0])
            if self.done < self.n // 2:
                self.back.append(self.last[1])

    def step(self):
        self.keep()
        self.done += 1
        f, b = self.last
        rows = self.value.shape[0] // 2
        if self.done < self.n // 2:
            self.last = (ring_shift(f, self.n, 1), ring_shift(b, self.n, -1))
        elif self.split:
            parts = ring_shift(f[:rows], self.n, 1), ring_shift(b[rows:], self.n, -1)
            self.last = (parts if self.split == "halves" else jnp.concatenate(parts, axis=0),)
        else:
            self.last = (ring_shift(f, self.n, 1),)

    def pieces(self):
        self.keep()
        return [self.value] + self.ahead + self.back


class RingReduce:
    def __init__(self, local, rank, n, first=None):
        self.local, self.rank, self.n, self.done = local, rank, n, 0
        self.first, self.last = first, None

    def part(self, step):
        return lax.dynamic_index_in_dim(
            self.local, (self.rank + step) % self.n, 0, keepdims=False
        )

    def step(self):
        half = self.n // 2
        if self.done == 0:
            f, b = self.first or (self.part(half), self.part(1 - half))
        else:
            f, b = self.last
            f = (f.astype(WIDE) + self.part(half - self.done).astype(WIDE)).astype(LOW)
            if self.done < half - 1:
                b = (b.astype(WIDE) + self.part(1 - half + self.done).astype(WIDE)).astype(LOW)
        f = ring_shift(f, self.n, 1)
        if self.done < half - 1:
            b = ring_shift(b, self.n, -1)
        self.last = (f, b)
        self.done += 1

    def total(self):
        f, b = self.last
        return f.astype(WIDE) + b.astype(WIDE) + self.part(0).astype(WIDE)


def pad_group(block):
    return jnp.pad(block, ((0, 0), (0, PAD - block.shape[1])))


def on_device(
    n,
    tokens,
    block_order,
    seq_lengths,
    cotangent,
    query_matrix,
    key_matrix,
    value_matrix,
    output_matrix,
    expand_matrix,
    reduce_matrix,
    query_bias,
    value_bias,
    output_bias,
    expand_bias,
    reduce_bias,
    first_gain,
    first_shift,
    second_gain,
    second_shift,
):
    w = lax.axis_index("wsh")
    c = lax.axis_index("ctx")
    barrier = lax.optimization_barrier
    order = ring_of(n)
    rank = jnp.asarray([order.index(i) for i in range(n)], jnp.int32)[c]
    width = tokens.shape[1]
    share = width // 4
    tokens_all = n * 4 * BLOCK

    other = wsh_swap(tokens, 2)
    both = jnp.concatenate([tokens, other], axis=0)
    (
        query_matrix,
        key_matrix,
        value_matrix,
        output_matrix,
        expand_matrix,
        reduce_matrix,
        output_bias,
        reduce_bias,
        expand_bias,
        first_gain,
        first_shift,
        second_gain,
        second_shift,
        other,
    ) = lax.optimization_barrier(
        (
            query_matrix,
            key_matrix,
            value_matrix,
            output_matrix,
            expand_matrix,
            reduce_matrix,
            output_bias,
            reduce_bias,
            expand_bias,
            first_gain,
            first_shift,
            second_gain,
            second_shift,
            other,
        )
    )

    def columns(matrix, group):
        low = matrix.astype(LOW)
        return [group(low[:, i * share : (i + 1) * share]) for i in range(4)]

    qkv_blocks = jnp.stack(
        [
            jnp.concatenate(parts, axis=1)
            for parts in zip(
                columns(query_matrix, pad_group),
                columns(key_matrix, pad_group),
                columns(value_matrix, pad_group),
            )
        ]
    )
    def deal(blocks):
        return lax.all_to_all(blocks, "wsh", 0, 0).reshape(-1, blocks.shape[2])

    qkv_matrix = deal(qkv_blocks)
    vectors = jnp.stack(
        [output_bias, reduce_bias, first_gain, first_shift, second_gain, second_shift]
    )
    vectors = jnp.concatenate([vectors, expand_bias.reshape(4, share)], axis=0).astype(LOW)
    nothing = jnp.zeros((PAD,), LOW)
    fill = jnp.zeros((PAD - share,), LOW)
    qkv_add = jnp.concatenate(
        [query_bias.astype(LOW), fill, nothing, value_bias.astype(LOW), fill]
    ).astype(WIDE)[None, :]
    output_low = output_matrix.astype(LOW)
    output_rows = jnp.pad(output_low, ((0, PAD - share), (0, 0)))

    ends = jnp.cumsum(seq_lengths)
    steps = jnp.asarray(slot_steps(n), jnp.int32)
    from_ctx = jnp.asarray(order, jnp.int32)[(rank + steps) % n]
    blocks = (from_ctx[:, None] * 4 + (w ^ jnp.asarray(ORDER, jnp.int32))[None, :]).reshape(-1)
    places = block_order[blocks]
    first = places[:4] * BLOCK
    low = jnp.max(jnp.where(ends[None, :] <= first[:, None], ends[None, :], 0), axis=1)
    last = first + BLOCK - 1
    high = jnp.min(jnp.where(ends[None, :] > last[:, None], ends[None, :], tokens_all), axis=1)
    low_block = low // BLOCK
    count = (high - low_block * BLOCK + BLOCK - 1) // BLOCK
    sends = (rank + jnp.asarray([n // 2, 1 - n // 2], jnp.int32)) % n
    tab = jnp.concatenate([places, low_block, count, sends]).astype(jnp.int32)
    seqs = seq_lengths.shape[0]
    seq_rows = jnp.pad(
        jnp.stack([ends - seq_lengths, ends]), ((0, 6), (SEQ_LANE, PAD - SEQ_LANE - seqs))
    ).astype(jnp.int32)

    expand_low, reduce_low = expand_matrix.astype(LOW), reduce_matrix.astype(LOW)
    middle_rows = reduce_matrix.shape[0] // 2
    side = c & 1
    reduce_half = lax.dynamic_slice_in_dim(reduce_low, side * middle_rows, middle_rows)
    ring = RingGather(both, n)
    half = n // 2
    for step in range(1, half + 1):
        ring.step()
        if step == 1:
            ring.last, vectors = barrier((ring.last, vectors))
            vector_pieces = [vectors] + [wsh_swap(vectors, j) for j in ORDER[1:]]
        elif step == 2:
            ready = (tab, seq_rows, qkv_add, output_rows, expand_low, reduce_low, reduce_half)
            ring.last, qkv_matrix, ready, vector_pieces = barrier(
                (ring.last, qkv_matrix, ready, vector_pieces)
            )
            tab, seq_rows, qkv_add, output_rows, expand_low, reduce_low, reduce_half = ready
            reduce_near = wsh_swap(reduce_half, 2)
        elif step == 3:
            ring.last, reduce_near = barrier((ring.last, reduce_near))
    reduce_far = exchange(reduce_near, "ctx", n, 1)
    expand_other = wsh_swap(expand_low, 2)
    token_pieces = []
    for piece in ring.pieces():
        token_pieces += [piece, wsh_swap(piece, 1)]
    expand_mate, reduce_mate = wsh_swap(expand_low, 1), wsh_swap(reduce_low, 1)
    reduce_last = [wsh_swap(reduce_near, 1)]
    attn, attended, keep, send, packed_queries, packed_keys, packed_values = attend(
        tab, seq_rows, qkv_matrix, qkv_add, output_rows, token_pieces, tokens_all
    )
    from_mate = wsh_swap(send, 1)
    branch_sum = (keep[BLOCK:] + from_mate[BLOCK:].astype(WIDE)).astype(LOW)
    from_other = wsh_swap(branch_sum, 2)
    expand_other, reduce_far, unused = barrier((expand_other, reduce_far, from_mate))
    reduce_last += [wsh_swap(reduce_far, 1)]
    expand_parts = [
        (expand_low, 0, 0),
        (expand_mate, 2, 0),
        (expand_other, 1, 0),
        (wsh_swap(expand_other, 1), 3, 0),
    ]
    reduce_parts = [(reduce_low, 0, 0), (reduce_mate, 2, 0)]
    for i, part in enumerate((reduce_near, reduce_far)):
        reduce_parts += [(part, 1, (4 + i,)), (reduce_last[i], 3, (4 + i,))]
    group = jnp.concatenate(
        [
            (w ^ jnp.asarray(ORDER, jnp.int32)).astype(jnp.int32),
            jnp.stack([side, 1 - side]).astype(jnp.int32) * middle_rows,
        ]
    )
    layer_out, grad_hidden, branch_in, pair, lows = middle(
        group,
        tokens,
        keep,
        from_mate,
        from_other,
        cotangent,
        vector_pieces,
        expand_parts,
        reduce_parts,
    )
    branch_pieces = group_pieces(branch_in)
    branch_all = jnp.concatenate(branch_pieces, axis=0)
    outgrad = attend_outgrad(branch_all, output_rows, attn)
    grad_output = lax.dot_general(
        attended[:, :share], branch_all, (((0,), (0,)), ((), ())), preferred_element_type=WIDE
    ).astype(LOW)

    def rows_dot(left, right):
        return lax.dot_general(
            left, right, (((0,), (0,)), ((), ())), preferred_element_type=WIDE
        ).astype(LOW)

    def redeal(chunk):
        lines = chunk.shape[0] // 4
        return lax.all_to_all(chunk.astype(LOW).reshape(4, lines, -1), "wsh", 0, 0)

    def by_place(matrix):
        cols = matrix.shape[1]
        return matrix.reshape(4, n, share // n, cols).transpose(1, 0, 2, 3).reshape(n, -1, cols)

    def joined(dealt, first):
        return jnp.concatenate([dealt[i, :, first : first + share] for i in range(4)], axis=1)

    shard = reduce_matrix.shape[0]
    lines = share // n
    pair, lows, outgrad = barrier((pair, lows, outgrad))
    pair = lax.all_to_all(pair, "wsh", 0, 0)
    lows = [lows, wsh_swap(lows, 2)]
    grad_ring = RingGather(outgrad, n, split="halves")
    grad_ring.step()
    grad_ring.last, outgrad, grad_output = barrier((grad_ring.last, outgrad, grad_output))
    grad_ring.step()
    grad_query = query_back(tab, outgrad, packed_queries, packed_keys, packed_values, tokens_all)
    grad_ring.last, grad_query = barrier((grad_ring.last, grad_query))
    grad_ring.step()
    grad_ring.last, pair, lows = barrier((grad_ring.last, pair, lows))
    lows = to_absolute([lows[0], wsh_swap(lows[0], 1), lows[1], wsh_swap(lows[1], 1)], w)
    reduce_all = jnp.concatenate([low[:BLOCK] for low in lows], axis=0)
    normed_all = jnp.concatenate([low[BLOCK:] for low in lows], axis=0)
    grad_reduce = rows_dot(pair[:, :BLOCK].reshape(4 * BLOCK, -1), reduce_all)
    grad_expand = rows_dot(normed_all, pair[:, BLOCK : 2 * BLOCK].reshape(4 * BLOCK, -1))
    sums = pair[:, 2 * BLOCK :, :share]
    early = jnp.concatenate(
        [grad_reduce.reshape(n, shard // n, width), by_place(grad_expand)], axis=1
    )
    for step in range(3, half):
        grad_ring.step()
        grad_ring.last, early, sums = barrier((grad_ring.last, early, sums))

    early_ring = RingReduce(early, rank, n)
    early_ring.step()
    grad_kv, late, ahead, behind = key_back(
        tab,
        token_pieces[:2],
        grad_query,
        grad_output,
        sums,
        grad_ring.pieces(),
        (packed_queries, packed_keys, packed_values),
        tokens_all,
    )
    early_ring.last, grad_kv, late, ahead, behind = barrier(
        (early_ring.last, grad_kv, late, ahead, behind)
    )
    late_ring = RingReduce(late, rank, n, (ahead, behind))
    for step in range(1, half):
        late_ring.step()
        early_ring.step()
        late_ring.last, early_ring.last = barrier((late_ring.last, early_ring.last))
    late_ring.step()
    early = early_ring.total()
    early = jnp.concatenate(
        [early[: shard // n].astype(LOW), redeal(early[shard // n :]).reshape(4 * lines, width)],
        axis=0,
    )
    late_ring.last, early = barrier((late_ring.last, early))

    early_gather = RingGather(early, n, split="halves")
    early_gather.step()
    late = late_ring.total()
    extra = late[4 * lines :].astype(LOW)
    own_output = late[: 4 * lines, 3 * share :].astype(LOW).reshape(4, lines, share)
    dealt = redeal(late[: 4 * lines, : 3 * share])
    late = jnp.concatenate(
        [joined(dealt, i * share) for i in range(3)] + [joined(own_output, 0), extra], axis=0
    )
    chunks = (rank + steps) % n
    late_gather = RingGather(late, n, split=False)
    for step in range(1, half):
        late_gather.step()
        early_gather.step()
        late_gather.last, early_gather.last = barrier((late_gather.last, early_gather.last))
    late_gather.step()
    out_reduce, out_expand = assemble(
        chunks,
        early_gather.pieces(),
        ((0, shard // n, 1), (shard // n, lines, 4)),
        ((shard, width), (share, 4 * width)),
    )
    late_gather.last, out_reduce, out_expand = barrier((late_gather.last, out_reduce, out_expand))
    tokens_grad = (
        scatter_group(
            dot_nt(grad_query, qkv_matrix[:, :PAD]) + dot_nt(grad_kv, qkv_matrix[:, PAD:])
        )
        + grad_hidden
    ).astype(LOW)
    out_query, out_key, out_value, out_output, small = assemble(
        chunks,
        late_gather.pieces(),
        tuple((i * lines, lines, 1) for i in range(4)) + ((4 * lines, 8, 1),),
        ((share, width),) * 4 + ((8 * n, width),),
    )
    small = small.reshape(n, 8, width)[:, : vector_rows(n), :share].reshape(-1, share)
    out_expand_bias = small[6:10].reshape(-1)
    return (
        layer_out,
        tokens_grad,
        out_query,
        out_key,
        out_value,
        out_output,
        out_expand,
        out_reduce,
        small[10],
        small[11],
        small[4],
        out_expand_bias,
        small[5],
        small[0],
        small[1],
        small[2],
        small[3],
    )


def solution(mesh):
    n = mesh.shape["ctx"]
    rows = P(("ctx", "wsh"), None)
    in_specs = (rows, P(), P(), rows) + (P("wsh", None),) * 6 + (P("wsh"),) * 9
    out_specs = (rows, rows) + (P("wsh", None),) * 6 + (P("wsh"),) * 9

    def run(*args):
        return on_device(n, *args)

    return jax.shard_map(run, mesh=mesh, in_specs=in_specs, out_specs=out_specs, check_vma=False)
```
